32 devices in a mesh: groups: 2 (over y), seq: 4 (over z), dp: 4 (over x, core), head: 1.
Axes of the slice: x: 2, y: 2, z: 4, core: 2. Of those that a mesh axis runs over, the one named last changes fastest.
Arguments:
- x_in: bfloat16 [8, 2048, 768], P(('groups', 'dp'), 'seq'), parts along dimension 0, may hold values from -6 to 6
- kernel_weight: bfloat16 [3, 768, 1536], P(None, None, 'head'), may hold values from -0.125 to 0.125
- conv_bias: float32 [1536], P('head'), may hold values from -3 to 3
- norm_gain: float32 [1536], replicated, may hold values from 0.25 to 1.75
- w_query: bfloat16 [1536, 1024], P(None, 'head'), may hold values from -8 to 8
- w_key: bfloat16 [1536, 128], replicated, may hold values from -1 to 1
- w_value: bfloat16 [1536, 192], replicated, may hold values from -0.15625 to 0.15625
- w_out: bfloat16 [1536, 1536], P('head'), may hold values from -0.15625 to 0.15625
- cotangent: bfloat16 [8, 1024, 1536], P(('groups', 'dp'), 'seq'), parts along dimension 0, may hold values from -0.75 to 0.75
Outputs:
- mixed: bfloat16 [8, 1024, 1536], P(('groups', 'dp'), 'seq', 'head'), parts along dimension 0
- grad_out_t: float32 [3072, 1536], P(('groups', 'dp'), 'head'), parts along dimension 0
The draws below stay inside these ranges and needn't reach their ends.
There are 2 independent parts, one for each index of `groups`. The reference program is written for one: setup_inputs(seed, part) draws one part's arguments, and reference() takes and returns one part's arrays. A program takes and returns all parts, laid end to end along the dimension named above; an argument that names none is the same for every part. Nothing has to cross between parts.
All inputs are finite; a program needn't handle non-finite values.
Results may differ from the reference program's by a relative error of at most 0.02.
Values may be sent and summed in bfloat16 or wider, within the bound.
A program may use at most 128 MiB of HBM per device.

```python
import math
import jax
import jax.numpy as jnp
from jax import lax

C_IN = 768
D = 1536
HEADS = 8
KEY = 128
VAL = 192
KERNEL_TAPS = 3
DILATION_STEP = 2
TOKENS = 1024
ROWS = 2048
SAMPLES = 4


def shared_keys(key):
    return jax.random.normal(jax.random.fold_in(key, 11), (D, KEY), jnp.float32) / math.sqrt(D)


def draw_w_key(key, part):
    return shared_keys(key).astype(jnp.bfloat16)


def draw_w_query(key, part):
    perturb = jax.random.normal(jax.random.fold_in(key, 12), (D, HEADS, KEY), jnp.float32) / math.sqrt(D)
    blended = 2.5 * perturb
    blended = jnp.clip(blended, -8.0, 8.0)
    return blended.reshape(D, HEADS * KEY).astype(jnp.bfloat16)


def level_of(own_key, dims, shards, least, top_value):
    def one(axis_at, blocks):
        draws = jax.random.uniform(jax.random.fold_in(jax.random.fold_in(own_key, 6), axis_at), (blocks,), jnp.float32, least / len(shards), top_value / len(shards))
        return jnp.repeat(jnp.exp(draws), dims[axis_at] // blocks).reshape((-1,) + (1,) * (len(dims) - axis_at - 1))

    gain = one(*shards[0])
    for cut in shards[1:]:
        gain = gain * one(*cut)
    return gain


def centred(rng, dims, spread, limit, cuts=(), kind=jnp.bfloat16):
    array = spread * jax.random.normal(rng, dims, jnp.float32)
    if cuts:
        array = array * level_of(rng, dims, cuts, -0.22, 0.18)
    return jnp.clip(array, -limit, limit).astype(kind)


def setup_inputs(seed: int = 0, part: int = 0) -> dict:
    streams_of = jax.random.split(jax.random.key(seed), 10)
    part_keys = jax.random.split(jax.random.fold_in(streams_of[9], part), 10)
    return {
        "x_in": centred(part_keys[0], (SAMPLES, ROWS, C_IN), 1.0, 6.0, ((0, 4), (1, 4))),
        "kernel_weight": centred(streams_of[1], (KERNEL_TAPS, C_IN, D), (KERNEL_TAPS * C_IN) ** -0.5, 0.125),
        "conv_bias": centred(streams_of[2], (D,), 0.5, 3.0, (), jnp.float32),
        "norm_gain": jnp.clip(1.0 + 0.15 * jax.random.normal(streams_of[3], (D,), jnp.float32), 0.25, 1.75),
        "w_query": draw_w_query(jax.random.fold_in(streams_of[9], 71), part),
        "w_key": draw_w_key(jax.random.fold_in(streams_of[9], 71), part),
        "w_value": centred(streams_of[6], (D, VAL), D ** -0.5, 0.15625),
        "w_out": centred(streams_of[7], (HEADS * VAL, D), (HEADS * VAL) ** -0.5, 0.15625),
        "cotangent": centred(part_keys[8], (SAMPLES, TOKENS, D), (3.0 / (SAMPLES * TOKENS) ** 0.5), 0.75, ((0, 4), (1, 4))),
    }


rope_base = 10000.0
norm_eps = 1e-06

def rotate(vectors, positions):
    halfway = vectors.shape[-1] // 2
    frequency = jnp.exp(-math.log(rope_base) * 2.0 * jnp.arange(halfway, dtype=jnp.float32) / vectors.shape[-1])
    angles = positions.astype(jnp.float32)[:, None] * frequency[None, :]
    layout = (positions.shape[0],) + (1,) * (vectors.ndim - 2) + (halfway,)
    cosine = jnp.cos(angles).reshape(layout)
    sines = jnp.sin(angles).reshape(layout)
    leading = vectors[..., :halfway]
    trailing = vectors[..., halfway:]
    return jnp.concatenate([leading * cosine - trailing * sines, leading * sines + trailing * cosine], axis=-1)

def encode_slab(inputs, kernel_weight, conv_bias):
    edge_padding = DILATION_STEP * (KERNEL_TAPS - 1) // 2
    padded_rows = jnp.pad(inputs, ((edge_padding, edge_padding), (0, 0)))
    padded_row_count = inputs.shape[0]
    before_activation = conv_bias[None, :] + jnp.zeros((padded_row_count, kernel_weight.shape[2]), jnp.float32)
    for kernel_tap_index in range(KERNEL_TAPS):
        before_activation = before_activation + jnp.dot(padded_rows[kernel_tap_index * DILATION_STEP:kernel_tap_index * DILATION_STEP + padded_row_count], kernel_weight[kernel_tap_index], preferred_element_type=jnp.float32)
    activated = jax.nn.gelu(before_activation)
    return lax.optimization_barrier(jnp.max(activated.reshape(padded_row_count // 2, 2, -1), axis=1)).astype(jnp.bfloat16)

def reference(x_in, kernel_weight, conv_bias, norm_gain, w_query, w_key, w_value, w_out, cotangent):
    pooled = lax.map(lambda inputs: encode_slab(inputs, kernel_weight, conv_bias), x_in)
    widened = pooled.astype(jnp.float32)
    squares = lax.optimization_barrier(jnp.mean(widened * widened, axis=-1, keepdims=True))
    normed = (widened * lax.rsqrt(squares + norm_eps) * norm_gain).astype(jnp.bfloat16)
    positions = jnp.arange(TOKENS, dtype=jnp.int32)
    block_size = math.gcd(TOKENS, 512)

    def one_sample(normed_rows):
        queries = rotate(jnp.dot(normed_rows, w_query, preferred_element_type=jnp.float32).reshape(TOKENS, HEADS, KEY), positions).astype(jnp.bfloat16)
        key_rows = rotate(jnp.dot(normed_rows, w_key, preferred_element_type=jnp.float32), positions).astype(jnp.bfloat16)
        value_rows = jnp.dot(normed_rows, w_value, preferred_element_type=jnp.float32).astype(jnp.bfloat16)
        key_wide = key_rows.astype(jnp.float32)
        value_wide = value_rows.astype(jnp.float32)

        def one_block(query_block):
            scores = jnp.einsum('thd,ud->htu', query_block.astype(jnp.float32), key_wide) * KEY ** (-0.5)
            peak = lax.optimization_barrier(jnp.max(scores, axis=-1, keepdims=True))
            weights = jnp.exp(scores - peak)
            totals = lax.optimization_barrier(jnp.sum(weights, axis=-1))
            rounded = lax.optimization_barrier(weights.astype(jnp.bfloat16))
            weighted = jnp.einsum('htu,uv->thv', rounded.astype(jnp.float32), value_wide)
            return (weighted / jnp.transpose(totals)[:, :, None]).astype(jnp.bfloat16)
        blocks = queries.reshape(TOKENS // block_size, block_size, HEADS, KEY)
        return lax.map(one_block, blocks).reshape(TOKENS, HEADS * VAL)
    attended = lax.map(one_sample, normed)
    projected = jnp.einsum('btj,jo->bto', attended.astype(jnp.float32), w_out.astype(jnp.float32))
    mixed = (pooled.astype(jnp.float32) + projected).astype(jnp.bfloat16)
    grad_out_t = jnp.einsum('bto,btj->oj', cotangent.astype(jnp.float32), attended.astype(jnp.float32))
    return (mixed, grad_out_t)
```

```python
import functools
import math

import jax
import jax.numpy as jnp
from jax import lax
from jax.experimental import pallas as pl
from jax.experimental.pallas import tpu as pltpu
import numpy as np
from jax.sharding import PartitionSpec as P

KEY = 128
VAL = 192
KERNEL_TAPS = 3
DILATION_STEP = 2


rope_base = 10000.0
norm_eps = 1e-06


def padded(cells, sides, width):
    for axis, dim in sides:
        count = lax.axis_size(axis)
        ends = count - 1
        head = lax.slice_in_dim(cells, 0, width, axis=dim)
        tail = lax.slice_in_dim(cells, cells.shape[dim] - width, cells.shape[dim], axis=dim)
        cells = jnp.concatenate(
            [
                lax.ppermute(tail, axis, [(i, (i + 1) % count) for i in range(ends)]),
                cells,
                lax.ppermute(head, axis, [((i + 1) % count, i) for i in range(ends)]),
            ],
            axis=dim,
        )
    return cells


def rotate(vectors, positions):
    halfway = vectors.shape[-1] // 2
    frequency = jnp.exp(
        -math.log(rope_base) * 2.0 * jnp.arange(halfway, dtype=jnp.float32) / vectors.shape[-1]
    )
    angles = positions.astype(jnp.float32)[:, None] * frequency[None, :]
    layout = (positions.shape[0],) + (1,) * (vectors.ndim - 2) + (halfway,)
    cosine = jnp.cos(angles).reshape(layout)
    sines = jnp.sin(angles).reshape(layout)
    leading = vectors[..., :halfway]
    trailing = vectors[..., halfway:]
    return jnp.concatenate(
        [leading * cosine - trailing * sines, leading * sines + trailing * cosine], axis=-1
    )


def attend_pieces(queries, key_rows, value_rows, state_in):
    total_keys = key_rows.shape[0]
    block_size = math.gcd(total_keys, 512)

    def one_block(block_index, state):
        running_max, running_sum, weighted = state
        key_block = lax.dynamic_slice_in_dim(key_rows, block_index * block_size, block_size, 0)
        value_block = lax.dynamic_slice_in_dim(value_rows, block_index * block_size, block_size, 0)
        scores = jnp.einsum(
            "thd,ud->htu", queries, key_block, preferred_element_type=jnp.float32
        ) * KEY ** (-0.5)
        new_max = jnp.maximum(running_max, jnp.max(scores, axis=-1))
        rescale = jnp.exp(running_max - new_max)
        weights = jnp.exp(scores - new_max[:, :, None])
        running_sum = running_sum * rescale + jnp.sum(weights, axis=-1)
        weighted = weighted * jnp.transpose(rescale)[:, :, None] + jnp.einsum(
            "htu,uv->thv",
            weights.astype(jnp.bfloat16),
            value_block,
            preferred_element_type=jnp.float32,
        )
        return (new_max, running_sum, weighted)

    return lax.fori_loop(0, total_keys // block_size, one_block, state_in)


def signal_to(sem, where):
    pl.semaphore_signal(sem, inc=1, device_id=where, device_id_type=pl.DeviceIdType.MESH)


def remote(src, dst, send_sem, recv_sem, where):
    return pltpu.make_async_remote_copy(
        src_ref=src,
        dst_ref=dst,
        send_sem=send_sem,
        recv_sem=recv_sem,
        device_id=where,
        device_id_type=pl.DeviceIdType.MESH,
    )


class Plan:
    def __init__(self, tokens, width, columns, dp, seq):
        self.tokens, self.width, self.columns = tokens, width, columns
        self.dp, self.seq = dp, seq
        self.levels = dp.bit_length() - 1
        self.block = width // dp
        self.rows = 64 if self.block % 64 == 0 else self.block
        self.pieces = self.block // self.rows
        self.chunk = 2 * VAL
        self.chunks = columns // self.chunk
        self.units = self.chunks * self.pieces
        self.gap = 4

    def scratch(self):
        tile = (self.rows, self.chunk)
        self.slots = self.gap * self.levels + 1
        shapes = [
            pltpu.VMEM((self.pieces, self.dp * self.rows, self.tokens), jnp.bfloat16),
            pltpu.VMEM((self.chunks, self.tokens, self.chunk), jnp.bfloat16),
            pltpu.VMEM((self.units,) + tile, jnp.float32),
            pltpu.VMEM((self.slots, self.dp * self.rows, self.chunk), jnp.float32),
        ]
        sends = self.levels + 2
        for level in range(self.levels):
            held = self.dp >> (level + 1)
            shapes += [pltpu.VMEM((self.units, held) + tile, jnp.bfloat16)] * 2
        shapes += [pltpu.VMEM((self.units,) + tile, jnp.bfloat16)] * 4
        shapes += [pltpu.SemaphoreType.DMA((self.units,))] * (2 * sends)
        return shapes


def turn_over(plan, cot_ref, cot_t):
    for piece in range(plan.pieces):
        for p in range(plan.dp):
            start = p * plan.block + piece * plan.rows
            cot_t[piece, p * plan.rows : (p + 1) * plan.rows, :] = jnp.transpose(
                cot_ref[:, start : start + plan.rows]
            )


def gradient_loop(plan, refs, out_ref, produce=None, least=0):
    cot_t, att, own, products = refs[:4]
    refs = refs[1:]
    levels, units = plan.levels, plan.units
    pairs = refs[3 : 3 + 2 * levels]
    ahead_out, ahead_in, back_out, back_in = refs[3 + 2 * levels : 7 + 2 * levels]
    sems = refs[7 + 2 * levels :]
    d = lax.axis_index("dp")
    s = lax.axis_index("seq")
    gap = plan.gap
    last = plan.seq - 1

    def summed(unit, p, level):
        start = pl.multiple_of(p * plan.rows, plan.rows)
        value = products[unit % plan.slots, pl.ds(start, plan.rows), :]
        for done in range(level):
            value = value + pairs[2 * done + 1][unit, p // (2 << done)].astype(jnp.float32)
        return value

    def level_copy(unit, level):
        step = 1 << level
        peer = d + (1 - 2 * ((d // step) % 2)) * step
        return remote(
            pairs[2 * level].at[unit],
            pairs[2 * level + 1].at[unit],
            sems[2 * level].at[unit],
            sems[2 * level + 1].at[unit],
            {"dp": peer},
        )

    def ahead_copy(unit):
        at = 2 * levels
        return remote(
            ahead_out.at[unit], ahead_in.at[unit], sems[at].at[unit], sems[at + 1].at[unit],
            {"seq": s + 1},
        )

    def back_copy(unit):
        at = 2 * levels + 2
        return remote(
            back_out.at[unit], back_in.at[unit], sems[at].at[unit], sems[at + 1].at[unit],
            {"seq": s - 1},
        )

    def within(unit):
        return jnp.logical_and(unit >= 0, unit < units)

    def step_at(t, carry):
        if produce is not None:
            produce(t)
        for level in range(levels):
            unit = t - gap * level

            @pl.when(within(unit))
            def _(unit=unit, level=level):
                if level == 0:
                    products[unit % plan.slots] = jnp.dot(
                        cot_t[unit % plan.pieces],
                        att[unit // plan.pieces],
                        preferred_element_type=jnp.float32,
                    )
                else:
                    level_copy(unit, level - 1).wait_recv()
                step = 1 << level
                base = d % step + (1 - (d // step) % 2) * step
                for i in range(plan.dp >> (level + 1)):
                    pairs[2 * level][unit, i] = summed(unit, base + i * 2 * step, level).astype(
                        jnp.bfloat16
                    )
                level_copy(unit, level).start()

        unit = t - gap * levels

        @pl.when(within(unit))
        def _():
            if levels > 0:
                level_copy(unit, levels - 1).wait_recv()
            else:
                products[unit % plan.slots] = jnp.dot(
                    cot_t[unit % plan.pieces],
                    att[unit // plan.pieces],
                    preferred_element_type=jnp.float32,
                )
            own[unit] = summed(unit, d, levels)

        if last > 0:
            fore = t - gap * (levels + s)

            @pl.when(jnp.logical_and(within(fore), s == 0))
            def _():
                ahead_out[fore] = own[fore].astype(jnp.bfloat16)
                ahead_copy(fore).start()

            @pl.when(jnp.logical_and(within(fore), s > 0))
            def _():
                ahead_copy(fore).wait_recv()

                @pl.when(s < last)
                def _():
                    ahead_out[fore] = (own[fore] + ahead_in[fore].astype(jnp.float32)).astype(
                        jnp.bfloat16
                    )
                    ahead_copy(fore).start()

            rear = t - gap * (levels + last - s)

            @pl.when(jnp.logical_and(within(rear), s == last))
            def _():
                back_out[rear] = own[rear].astype(jnp.bfloat16)
                back_copy(rear).start()

            @pl.when(jnp.logical_and(within(rear), s < last))
            def _():
                back_copy(rear).wait_recv()

                @pl.when(s > 0)
                def _():
                    back_out[rear] = (own[rear] + back_in[rear].astype(jnp.float32)).astype(
                        jnp.bfloat16
                    )
                    back_copy(rear).start()

        ready = t - gap * (levels + last)

        def store(value):
            row = pl.multiple_of((ready % plan.pieces) * plan.rows, plan.rows)
            column = pl.multiple_of((ready // plan.pieces) * plan.chunk, plan.chunk)
            out_ref[pl.ds(row, plan.rows), pl.ds(column, plan.chunk)] = value.astype(out_ref.dtype)

        if last == 0:

            @pl.when(within(ready))
            def _():
                store(own[ready])

        else:

            @pl.when(jnp.logical_and(within(ready), s == 0))
            def _():
                store(own[ready] + back_in[ready].astype(jnp.float32))

            @pl.when(jnp.logical_and(within(ready), s == last))
            def _():
                store(own[ready] + ahead_in[ready].astype(jnp.float32))

            if last > 1:

                @pl.when(
                    jnp.logical_and(within(ready), jnp.logical_and(s > 0, s < last))
                )
                def _():
                    store(
                        own[ready]
                        + ahead_in[ready].astype(jnp.float32)
                        + back_in[ready].astype(jnp.float32)
                    )

        return carry

    lax.fori_loop(0, max(least, units + gap * (levels + last)), step_at, 0)

    def drain(unit, carry):
        for level in range(levels):
            level_copy(unit, level).wait_send()
        if last > 0:

            @pl.when(s < last)
            def _():
                ahead_copy(unit).wait_send()

            @pl.when(s > 0)
            def _():
                back_copy(unit).wait_send()

        return carry

    lax.fori_loop(0, units, drain, 0)


def greet(plan):
    barrier = pltpu.get_barrier_semaphore()
    d = lax.axis_index("dp")
    s = lax.axis_index("seq")
    for level in range(plan.levels):
        step = 1 << level
        signal_to(barrier, {"dp": d + (1 - 2 * ((d // step) % 2)) * step})
    if plan.seq > 1:

        @pl.when(s > 0)
        def _():
            signal_to(barrier, {"seq": s - 1})

        @pl.when(s < plan.seq - 1)
        def _():
            signal_to(barrier, {"seq": s + 1})

    if plan.seq == 1:
        pl.semaphore_wait(barrier, plan.levels)
        return
    edge = jnp.logical_or(s == 0, s == plan.seq - 1)

    @pl.when(edge)
    def _():
        pl.semaphore_wait(barrier, plan.levels + 1)

    @pl.when(jnp.logical_not(edge))
    def _():
        pl.semaphore_wait(barrier, plan.levels + 2)


def gradient_kernel(plan, cot_ref, att_ref, out_ref, *refs):
    greet(plan)
    turn_over(plan, cot_ref, refs[0])
    for c in range(plan.chunks):
        refs[1][c] = att_ref[:, c * plan.chunk : (c + 1) * plan.chunk]
    gradient_loop(plan, refs, out_ref)


def reduced_gradient(upstream, attended):
    plan = Plan(
        upstream.shape[0], upstream.shape[1], attended.shape[1],
        lax.axis_size("dp"), lax.axis_size("seq"),
    )
    whole = pl.BlockSpec(memory_space=pltpu.VMEM)
    return pl.pallas_call(
        functools.partial(gradient_kernel, plan),
        out_shape=jax.ShapeDtypeStruct((plan.block, plan.columns), jnp.float32),
        in_specs=[whole, whole],
        out_specs=whole,
        scratch_shapes=plan.scratch(),
        compiler_params=pltpu.CompilerParams(
            collective_id=0, has_side_effects=True, vmem_limit_bytes=56 * 2**20
        ),
        name="reduced_gradient",
    )(upstream, attended)


EDGE = 16
TILE = 512
LANES = 128
DP = 4
SEQ = 4
HOLD = 256
SPLIT = 3
GAP = 5


def section_kernel(*refs):
    (x_hbm, conv_hbm, bias_in, gain_in, query_hbm, key_hbm, value_hbm, out_hbm, cot_hbm, turn_hbm) = refs[:10]
    mixed, grad_out = refs[10:12]
    (
        x_rows, conv_w, query_w, key_w, value_w, out_w, turn, fetched,
        edges, edge_sems, spread, stacked, pooled, normed, queries,
        kv, kv_send, kv_recv, values, peaks, sums, bias, gain,
        cot_in, cot_t, cot_sems, att_rows, att, att_sems, own,
        ahead_out, ahead_in, back_out, back_in, line_sems,
    ) = refs[12:]
    rows, channels = x_rows.shape
    tokens, width = pooled.shape
    tiles, blocks = width // TILE, channels // LANES
    half, quarter = tokens // 2, tokens // 4
    heads = queries.shape[0]
    part_rows = width // DP
    strips = att.shape[0]
    taps = KERNEL_TAPS
    d = lax.axis_index("dp")
    s = lax.axis_index("seq")
    mate = d + 1 - 2 * (d % 2)
    across = d + 2 - 4 * (d // 2)
    opposite = 3 - d
    far = 3 - s
    upper = s // 2
    end = jnp.logical_or(s == 0, s == SEQ - 1)
    inner = jnp.logical_not(end)

    pieces = ((0, quarter, half), (half, 0, quarter), (half + quarter, half + quarter, quarter))

    def conv_fetch(n):
        return pltpu.make_async_copy(
            conv_hbm.at[:, pl.ds(pl.multiple_of(n * TILE, TILE), TILE)],
            conv_w.at[n],
            fetched.at[8 + n],
        )

    def turn_fetch(i):
        to, at, count = pieces[i]
        return pltpu.make_async_copy(
            turn_hbm.at[pl.ds(pl.multiple_of(s * tokens + at, quarter), count)],
            turn.at[pl.ds(to, count)],
            fetched.at[5 + i],
        )

    x_fetch = pltpu.make_async_copy(x_hbm, x_rows, fetched.at[0])
    key_fetch = pltpu.make_async_copy(key_hbm, key_w, fetched.at[1])
    value_fetch = pltpu.make_async_copy(value_hbm, value_w, fetched.at[2])
    query_fetch = pltpu.make_async_copy(query_hbm, query_w, fetched.at[3])
    out_fetch = pltpu.make_async_copy(out_hbm, out_w, fetched.at[4])

    def cot_columns(owner):
        start = pl.multiple_of(owner * part_rows, part_rows)
        return cot_hbm.at[:, pl.ds(start, part_rows)]

    cot_own = pltpu.make_async_copy(cot_columns(d), cot_in.at[0], cot_sems.at[0])

    def cot_copy(slot):
        peer = (d, mate, across, opposite)[slot]
        return remote(
            cot_columns(peer), cot_in.at[slot], cot_sems.at[2 * slot], cot_sems.at[2 * slot + 1],
            {"dp": peer},
        )

    x_fetch.start()
    for n in range(tiles):
        conv_fetch(n).start()
    key_fetch.start()
    value_fetch.start()
    for i in range(3):
        turn_fetch(i).start()

    barrier = pltpu.get_barrier_semaphore()
    for peer in (mate, across, opposite):
        signal_to(barrier, {"dp": peer})

    @pl.when(s > 0)
    def _():
        signal_to(barrier, {"seq": s - 1})

    @pl.when(s < SEQ - 1)
    def _():
        signal_to(barrier, {"seq": s + 1})

    @pl.when(end)
    def _():
        signal_to(barrier, {"seq": far})

    bias[...] = bias_in[...].reshape(bias.shape)
    gain[...] = gain_in[...].reshape(gain.shape)

    def edge_ahead():
        return remote(
            x_hbm.at[pl.ds(rows - EDGE, EDGE)], edges.at[0], edge_sems.at[0], edge_sems.at[1],
            {"seq": s + 1},
        )

    def edge_back():
        return remote(
            x_hbm.at[pl.ds(0, EDGE)], edges.at[1], edge_sems.at[2], edge_sems.at[3],
            {"seq": s - 1},
        )

    x_fetch.wait()
    query_fetch.start()
    for j in range(blocks):
        spread[j, EDGE : EDGE + rows, :] = x_rows[:, j * LANES : (j + 1) * LANES].astype(
            jnp.float32
        )
    blank = jnp.zeros((EDGE, LANES), jnp.float32)
    for j in range(blocks):
        spread[j, :EDGE, :] = blank
        spread[j, EDGE + rows :, :] = blank

    def stack(tap, to, first, count):
        for parity in range(2):
            for j in range(blocks):
                start = EDGE + parity + DILATION_STEP * (tap - 1) + 2 * first
                lane = tap * channels + j * LANES
                row = 2 * half * (to // half) + parity * half + to % half
                stacked[row : row + count, lane : lane + LANES] = spread[
                    j, pl.ds(start, count, stride=2), :
                ].astype(jnp.bfloat16)

    for tap in range(taps):
        for piece in pieces:
            stack(tap, *piece)

    pl.semaphore_wait(barrier, 5)

    @pl.when(s < SEQ - 1)
    def _():
        edge_ahead().start()

    @pl.when(s > 0)
    def _():
        edge_back().start()

    cot_own.start()
    for slot in range(1, DP):
        cot_copy(slot).start()
    out_fetch.start()

    def put_edge(which, start, tap, to, first):
        (edge_ahead if which == 0 else edge_back)().wait_recv()
        for j in range(blocks):
            spread[j, start : start + EDGE, :] = edges[
                which, :, j * LANES : (j + 1) * LANES
            ].astype(jnp.float32)
        stack(tap, to, first, EDGE)

    def turned(vectors, first, count):
        return (
            vectors * turn[pl.ds(first, count), :KEY]
            + pltpu.roll(vectors, KEY // 2, 1) * turn[pl.ds(first, count), KEY:]
        ).astype(jnp.bfloat16)

    def kv_copy(owner, part, sem, where):
        block = kv.at[owner, part]
        return remote(block, block, kv_send.at[sem], kv_recv.at[owner * 2 + part], {"seq": where})

    def kv_own(part, action):
        @pl.when(s > 0)
        def _():
            action(kv_copy(s, part, part, s - 1))

        @pl.when(s < SEQ - 1)
        def _():
            action(kv_copy(s, part, 2 + part, s + 1))

        @pl.when(end)
        def _():
            action(kv_copy(s, part, 4 + part, far))

    def kv_relay(part, action):
        action(kv_copy(s + 1, part, 6 + part, s - 1))
        action(kv_copy(s - 1, part, 8 + part, s + 1))

    def kv_wait(owner, part):
        kv_copy(owner, part, 0, s).wait_recv()

    def conv_pass(part, carry):
        first = part == 0
        base = pl.multiple_of(part * half, half)
        here = pl.ds(base, half)

        @pl.when(jnp.logical_and(part == 1, s > 0))
        def _():
            put_edge(0, 0, 0, half, 0)

        @pl.when(jnp.logical_and(part == 1, s < SEQ - 1))
        def _():
            put_edge(1, EDGE + rows, taps - 1, tokens - EDGE, tokens - EDGE)

        def conv_tile(n, carry):
            @pl.when(first)
            def _():
                conv_fetch(n).wait()

            columns = pl.ds(pl.multiple_of(n * TILE, TILE), TILE)
            pre = (
                jnp.dot(
                    stacked[pl.ds(pl.multiple_of(part * tokens, tokens), tokens), :],
                    conv_w[n],
                    preferred_element_type=jnp.float32,
                )
                + bias[:, columns]
            )
            inside = math.sqrt(2.0 / math.pi) * (pre + 0.044715 * (pre * pre * pre))
            activated = pre * (0.5 * (1.0 + jnp.tanh(inside)))
            pooled[here, columns] = jnp.maximum(activated[:half], activated[half:]).astype(
                jnp.bfloat16
            )
            return carry

        lax.fori_loop(0, tiles, conv_tile, 0)

        count = 32

        def norm_part(i, carry):
            few = pl.ds(pl.multiple_of(base + i * count, count), count)
            wide = pooled[few, :].astype(jnp.float32)
            squares = jnp.mean(wide * wide, axis=-1, keepdims=True)
            normed[few, :] = (wide * lax.rsqrt(squares + norm_eps) * gain[...]).astype(
                jnp.bfloat16
            )
            return carry

        lax.fori_loop(0, half // count, norm_part, 0)

        @pl.when(first)
        def _():
            key_fetch.wait()
            value_fetch.wait()
            for i in range(3):
                turn_fetch(i).wait()

        ready = normed[here, :]
        kv[s, part, :half, :] = turned(
            jnp.dot(ready, key_w[...], preferred_element_type=jnp.float32), base, half
        )
        own_values = lax.dot_general(
            ready, value_w[...], (((1,), (1,)), ((), ())), preferred_element_type=jnp.float32
        )
        kv[s, part, half : 2 * half, :] = own_values[:, :LANES].astype(jnp.bfloat16)
        kv[s, part, 2 * half :, :] = jnp.concatenate(
            [own_values[:quarter, LANES:], own_values[quarter:, LANES:]], axis=1
        ).astype(jnp.bfloat16)
        kv_own(part, lambda copy: copy.start())
        return carry

    lax.fori_loop(0, 2, conv_pass, 0)

    @pl.when(inner)
    def _():
        kv_wait(s - 1, 0)
        kv_wait(s + 1, 0)
        kv_relay(0, lambda copy: copy.start())

    query_fetch.wait()

    def query_pair(c, carry):
        pair = jnp.dot(
            normed[...],
            query_w[:, pl.ds(pl.multiple_of(c * 2 * KEY, 2 * KEY), 2 * KEY)],
            preferred_element_type=jnp.float32,
        )
        queries[2 * c] = turned(pair[:, :KEY], 0, tokens)
        queries[2 * c + 1] = turned(pair[:, KEY:], 0, tokens)
        return carry

    lax.fori_loop(0, heads // 2, query_pair, 0)

    def turn_over(slot):
        (cot_own.wait if slot == 0 else cot_copy(slot).wait_recv)()
        middle = cot_in[slot, quarter : quarter + half, :]
        outer = jnp.concatenate(
            [cot_in[slot, :quarter, :], cot_in[slot, quarter + half :, :]], axis=0
        )
        at = slot * tokens
        cot_t[:, at : at + half] = jnp.transpose(middle)
        cot_t[:, at + half : at + tokens] = jnp.transpose(outer)

    def owner_of(k):
        low = s + upper * (3 - 2 * s)
        at = (k + low) % 2 if k < 2 else (k - 2 + 1 - low) % 2 + 2
        return at + upper * (3 - 2 * at)

    side = lax.broadcasted_iota(jnp.int32, (half, LANES), 1)

    def unpack(owner):
        for part in range(2):
            at = part * half
            values[at : at + half, :LANES] = kv[owner, part, half : 2 * half, :]
            rest = kv[owner, part, 2 * half :, :]
            rest = jnp.concatenate(
                [rest, pltpu.roll(rest.astype(jnp.float32), LANES // 2, 1).astype(jnp.bfloat16)],
                axis=0,
            ).astype(jnp.float32)
            rest = jnp.where(
                side < VAL - LANES, rest, jnp.where(side == VAL - LANES, 1.0, 0.0)
            )
            values[at : at + half, LANES:] = rest.astype(jnp.bfloat16)

    factor = KEY ** (-0.5) * math.log2(math.e)

    def twice(column):
        return jnp.concatenate([column, column], axis=1)

    def attend(h, keys, first):
        scores = lax.dot_general(
            queries[h], keys, (((1,), (1,)), ((), ())), preferred_element_type=jnp.float32
        )
        peak = jnp.max(scores, axis=-1, keepdims=True)
        if first:
            peak = jnp.broadcast_to(peak, (tokens, LANES))
        else:
            before = peaks[h]
            peak = jnp.maximum(before, peak)
        weights = jnp.exp2((scores - twice(peak)) * factor).astype(jnp.bfloat16)
        total = jnp.dot(weights, values[...], preferred_element_type=jnp.float32)
        if not first:
            total = total + sums[h] * twice(jnp.exp2((before - peak) * factor))
        return peak, total

    def keys_of(owner):
        return kv[owner, :, :half, :].reshape(tokens, KEY)

    def attend_block(k):
        owner = owner_of(k)
        unpack(owner)

        def pair(c, carry):
            for h in (2 * c, 2 * c + 1):
                peak, total = attend(h, keys_of(owner), k == 0)
                peaks[h] = peak
                sums[h] = total
            return carry

        lax.fori_loop(0, heads // 2, pair, 0)

    def wait_block(k):
        owner = owner_of(k)
        kv_wait(owner, 0)
        kv_wait(owner, 1)

    def att_copy(kind, b):
        slot = (0, 0, 2)[kind]
        to = (1, 2, 3)[kind]
        return remote(
            att.at[b, slot], att.at[b, to],
            att_sems.at[(2 * kind) * strips + b], att_sems.at[(2 * kind + 1) * strips + b],
            {"dp": across if kind == 1 else mate},
        )

    attend_block(0)

    @pl.when(inner)
    def _():
        kv_wait(s - 1, 1)
        kv_wait(s + 1, 1)
        kv_relay(1, lambda copy: copy.start())

    for slot in range(DP):
        turn_over(slot)

    @pl.when(end)
    def _():
        wait_block(1)

    attend_block(1)

    @pl.when(end)
    def _():
        wait_block(2)

    attend_block(2)
    wait_block(3)
    last_owner = owner_of(3)
    unpack(last_owner)
    chunk = 2 * VAL
    each = chunk // LANES

    def last_pair(c, carry):
        done = []
        for h in (2 * c, 2 * c + 1):
            _, total = attend(h, keys_of(last_owner), False)
            done.append(total[:, :VAL] / total[:, VAL : VAL + 1])
        both = jnp.concatenate(done, axis=1).astype(jnp.bfloat16)
        att_rows[:, pl.ds(pl.multiple_of(c * chunk, LANES), chunk)] = both
        for i in range(each):
            b = c * each + i
            att[b, 0] = both[:, i * LANES : (i + 1) * LANES]
            att_copy(1, b).start()
            att_copy(0, b).start()
        return carry

    lax.fori_loop(0, heads // 2, last_pair, 0)
    out_fetch.wait()

    def mixed_tile(n, carry):
        columns = pl.ds(pl.multiple_of(n * TILE, TILE), TILE)
        total = pooled[:, columns].astype(jnp.float32) + jnp.dot(
            att_rows[...], out_w[:, columns], preferred_element_type=jnp.float32
        )
        total = total.astype(jnp.bfloat16)
        for at, to, count in pieces:
            mixed[to : to + count, columns] = total[at : at + count]
        return carry

    lax.fori_loop(0, tiles, mixed_tile, 0)

    units = strips * SPLIT
    last = SEQ - 1
    lead = SPLIT

    def place(unit):
        return unit // SPLIT, unit % SPLIT

    def ahead_copy(unit):
        at = place(unit)
        return remote(
            ahead_out.at[at], ahead_in.at[at], line_sems.at[unit], line_sems.at[units + unit],
            {"seq": s + 1},
        )

    def back_copy(unit):
        at = place(unit)
        return remote(
            back_out.at[at], back_in.at[at], line_sems.at[2 * units + unit],
            line_sems.at[3 * units + unit], {"seq": s - 1},
        )

    def within(unit):
        return jnp.logical_and(unit >= 0, unit < units)

    def step_at(t, carry):
        @pl.when(jnp.logical_and(within(t), t % SPLIT == 0))
        def _():
            b = t // SPLIT
            att_copy(1, b).wait_recv()
            att_copy(2, b).start()

        @pl.when(jnp.logical_and(within(t - lead), t % SPLIT == 0))
        def _():
            b = (t - lead) // SPLIT
            att_copy(0, b).wait_recv()
            att_copy(2, b).wait_recv()
            own[b] = jnp.dot(
                cot_t[...],
                att[b].reshape(DP * tokens, LANES),
                preferred_element_type=jnp.float32,
            ).reshape(own.shape[1:])

        fore = t - lead - GAP * s

        @pl.when(jnp.logical_and(within(fore), s == 0))
        def _():
            ahead_out[place(fore)] = own[place(fore)].astype(jnp.bfloat16)
            ahead_copy(fore).start()

        @pl.when(jnp.logical_and(within(fore), s > 0))
        def _():
            ahead_copy(fore).wait_recv()

            @pl.when(s < last)
            def _():
                ahead_out[place(fore)] = (
                    own[place(fore)] + ahead_in[place(fore)].astype(jnp.float32)
                ).astype(jnp.bfloat16)
                ahead_copy(fore).start()

        rear = t - lead - GAP * (last - s)

        @pl.when(jnp.logical_and(within(rear), s == last))
        def _():
            back_out[place(rear)] = own[place(rear)].astype(jnp.bfloat16)
            back_copy(rear).start()

        @pl.when(jnp.logical_and(within(rear), s < last))
        def _():
            back_copy(rear).wait_recv()

            @pl.when(s > 0)
            def _():
                back_out[place(rear)] = (
                    own[place(rear)] + back_in[place(rear)].astype(jnp.float32)
                ).astype(jnp.bfloat16)
                back_copy(rear).start()

        ready = t - lead - GAP * last

        def store(value):
            b, i = place(ready)
            size = part_rows // SPLIT
            row = pl.multiple_of(i * size, size)
            column = pl.multiple_of(b * LANES, LANES)
            grad_out[pl.ds(row, size), pl.ds(column, LANES)] = value.astype(grad_out.dtype)

        @pl.when(jnp.logical_and(within(ready), s == 0))
        def _():
            store(own[place(ready)] + back_in[place(ready)].astype(jnp.float32))

        @pl.when(jnp.logical_and(within(ready), s == last))
        def _():
            store(own[place(ready)] + ahead_in[place(ready)].astype(jnp.float32))

        @pl.when(jnp.logical_and(within(ready), inner))
        def _():
            store(
                own[place(ready)]
                + ahead_in[place(ready)].astype(jnp.float32)
                + back_in[place(ready)].astype(jnp.float32)
            )

        return carry

    lax.fori_loop(0, units + lead + GAP * last, step_at, 0)

    def drain_line(unit, carry):
        @pl.when(s < last)
        def _():
            ahead_copy(unit).wait_send()

        @pl.when(s > 0)
        def _():
            back_copy(unit).wait_send()

        return carry

    lax.fori_loop(0, units, drain_line, 0)

    def drain_strip(b, carry):
        for kind in range(3):
            att_copy(kind, b).wait_send()
        return carry

    lax.fori_loop(0, strips, drain_strip, 0)
    for part in range(2):
        kv_own(part, lambda copy: copy.wait_send())

        @pl.when(inner)
        def _(part=part):
            kv_relay(part, lambda copy: copy.wait_send())

    for slot in range(1, DP):
        cot_copy(slot).wait_send()

    @pl.when(s < SEQ - 1)
    def _():
        edge_ahead().wait_send()

    @pl.when(s > 0)
    def _():
        edge_back().wait_send()


def turn_table(count):
    frequency = np.exp(
        np.float32(-math.log(rope_base) * 2.0) * np.arange(KEY // 2, dtype=np.float32) / KEY
    ).astype(np.float32)
    angles = np.arange(count, dtype=np.float32)[:, None] * frequency[None, :]
    cosine, sines = np.cos(angles), np.sin(angles)
    return np.concatenate([cosine, cosine, -sines, sines], axis=1).astype(np.float32)


def finish_kernel(mixed_in, grad_in, mixed, grad):
    mixed[...] = mixed_in[...]
    grad[...] = grad_in[...].astype(jnp.float32)


def finish(mixed, gradient):
    steps = 4

    def cut(array):
        return pl.BlockSpec((array.shape[0] // steps, array.shape[1]), lambda i: (i, 0))

    return pl.pallas_call(
        finish_kernel,
        grid=(steps,),
        out_shape=(
            jax.ShapeDtypeStruct(mixed.shape, mixed.dtype),
            jax.ShapeDtypeStruct(gradient.shape, jnp.float32),
        ),
        in_specs=[cut(mixed), cut(gradient)],
        out_specs=(cut(mixed), cut(gradient)),
        name="finish",
    )(mixed, gradient)


def section(x_in, kernel_weight, conv_bias, norm_gain, w_query, w_key, w_value, w_out, cotangent):
    inputs, upstream = x_in[0], cotangent[0]
    rows, channels = inputs.shape
    width, columns = kernel_weight.shape[2], w_out.shape[0]
    tokens, tiles, strips = rows // 2, width // TILE, columns // LANES
    heads, part_rows = w_query.shape[1] // KEY, width // DP
    depth = KERNEL_TAPS * channels
    units = strips * SPLIT
    bf, f32 = jnp.bfloat16, jnp.float32
    line = pltpu.VMEM((strips, SPLIT, part_rows // SPLIT, LANES), bf)
    held = pl.BlockSpec(memory_space=pltpu.VMEM)
    away = pl.BlockSpec(memory_space=pl.ANY)
    mixed, gradient = pl.pallas_call(
        section_kernel,
        out_shape=(
            jax.ShapeDtypeStruct((tokens, width), bf),
            jax.ShapeDtypeStruct((part_rows, columns), bf),
        ),
        in_specs=[away, away, held, held, away, away, away, away, away, away],
        out_specs=(held, held),
        scratch_shapes=[
            pltpu.VMEM((rows, channels), bf),
            pltpu.VMEM((tiles, depth, TILE), bf),
            pltpu.VMEM(w_query.shape, bf),
            pltpu.VMEM(w_key.shape, bf),
            pltpu.VMEM(w_value.shape[::-1], bf),
            pltpu.VMEM(w_out.shape, bf),
            pltpu.VMEM((tokens, 2 * KEY), f32),
            pltpu.SemaphoreType.DMA((8 + tiles,)),
            pltpu.VMEM((2, EDGE, channels), bf),
            pltpu.SemaphoreType.DMA((4,)),
            pltpu.VMEM((channels // LANES, rows + 2 * EDGE, LANES), f32),
            pltpu.VMEM((rows, depth), bf),
            pltpu.VMEM((tokens, width), bf),
            pltpu.VMEM((tokens, width), bf),
            pltpu.VMEM((heads, tokens, KEY), bf),
            pltpu.VMEM((SEQ, 2, 5 * tokens // 4, KEY), bf),
            pltpu.SemaphoreType.DMA((10,)),
            pltpu.SemaphoreType.DMA((2 * SEQ,)),
            pltpu.VMEM((tokens, HOLD), bf),
            pltpu.VMEM((heads, tokens, LANES), f32),
            pltpu.VMEM((heads, tokens, HOLD), f32),
            pltpu.VMEM((1, width), f32),
            pltpu.VMEM((1, width), f32),
            pltpu.VMEM((DP, tokens, part_rows), bf),
            pltpu.VMEM((part_rows, DP * tokens), bf),
            pltpu.SemaphoreType.DMA((2 * DP,)),
            pltpu.VMEM((tokens, columns), bf),
            pltpu.VMEM((strips, DP, tokens, LANES), bf),
            pltpu.SemaphoreType.DMA((6 * strips,)),
            pltpu.VMEM((strips, SPLIT, part_rows // SPLIT, LANES), f32),
            line, line, line, line,
            pltpu.SemaphoreType.DMA((4 * units,)),
        ],
        compiler_params=pltpu.CompilerParams(
            collective_id=1, has_side_effects=True, vmem_limit_bytes=60 * 2**20
        ),
        name="section",
    )(
        inputs,
        kernel_weight.reshape(depth, width),
        conv_bias,
        norm_gain,
        w_query,
        w_key,
        jnp.transpose(w_value),
        w_out,
        upstream,
        turn_table(tokens * SEQ),
    )
    mixed, gradient = finish(mixed, gradient)
    return mixed[None], gradient


def local(x_in, kernel_weight, conv_bias, norm_gain, w_query, w_key, w_value, w_out, cotangent):
    inputs = x_in[0]
    edge_padding = DILATION_STEP * (KERNEL_TAPS - 1) // 2
    padded_rows = padded(inputs, (("seq", 0),), edge_padding)
    padded_row_count = inputs.shape[0]
    before_activation = jnp.broadcast_to(
        conv_bias[None, :], (padded_row_count, kernel_weight.shape[2])
    )
    for kernel_tap_index in range(KERNEL_TAPS):
        before_activation = before_activation + jnp.dot(
            padded_rows[
                kernel_tap_index * DILATION_STEP : kernel_tap_index * DILATION_STEP
                + padded_row_count
            ],
            kernel_weight[kernel_tap_index],
            preferred_element_type=jnp.float32,
        )
    activated = jax.nn.gelu(before_activation)
    pooled = jnp.max(activated.reshape(padded_row_count // 2, 2, -1), axis=1).astype(jnp.bfloat16)
    token_count = pooled.shape[0]
    features = lax.all_gather(pooled, "head", axis=1, tiled=True)
    widened = features.astype(jnp.float32)
    squares = jnp.mean(widened * widened, axis=-1, keepdims=True)
    normed = (widened * lax.rsqrt(squares + norm_eps) * norm_gain).astype(jnp.bfloat16)
    seq_offset = lax.axis_index("seq") * token_count
    positions = seq_offset + jnp.arange(token_count, dtype=jnp.int32)
    local_heads = w_query.shape[1] // KEY
    queries = rotate(
        jnp.dot(normed, w_query, preferred_element_type=jnp.float32).reshape(
            token_count, local_heads, KEY
        ),
        positions,
    ).astype(jnp.bfloat16)
    own_rows = token_count // lax.axis_size("head")
    row_offset = lax.axis_index("head") * own_rows
    own_normed = lax.dynamic_slice_in_dim(normed, row_offset, own_rows, 0)
    own_positions = seq_offset + row_offset + jnp.arange(own_rows, dtype=jnp.int32)
    key_rows = rotate(
        jnp.dot(own_normed, w_key, preferred_element_type=jnp.float32), own_positions
    ).astype(jnp.bfloat16)
    value_rows = jnp.dot(own_normed, w_value, preferred_element_type=jnp.float32).astype(
        jnp.bfloat16
    )
    start_state = (
        jnp.full((local_heads, token_count), -1e30, jnp.float32),
        jnp.zeros((local_heads, token_count), jnp.float32),
        jnp.zeros((token_count, local_heads, VAL), jnp.float32),
    )
    both = lax.all_gather(
        jnp.concatenate([key_rows, value_rows], axis=1), ("seq", "head"), axis=0, tiled=True
    )
    final_state = attend_pieces(
        queries,
        both[:, :KEY],
        both[:, KEY:],
        start_state,
    )
    running_max, running_sum, weighted = final_state
    attended = (
        (weighted / jnp.transpose(running_sum)[:, :, None])
        .astype(jnp.bfloat16)
        .reshape(token_count, local_heads * VAL)
    )
    projected = lax.psum_scatter(
        lax.dot_general(
            w_out, attended, (((0,), (1,)), ((), ())), preferred_element_type=jnp.float32
        ).astype(jnp.bfloat16),
        "head",
        scatter_dimension=0,
        tiled=True,
    ).astype(jnp.float32)
    mixed = (pooled.astype(jnp.float32) + jnp.transpose(projected)).astype(jnp.bfloat16)[None]
    upstream = cotangent[0]
    gradient = reduced_gradient(upstream, attended)
    return (mixed, gradient)


def solution(mesh):
    sizes = tuple(mesh.shape[axis] for axis in ("head", "seq", "dp"))
    return jax.shard_map(
        section if sizes == (1, SEQ, DP) else local,
        mesh=mesh,
        in_specs=(
            P(("groups", "dp"), "seq", None),
            P(None, None, "head"),
            P("head"),
            P(),
            P(None, "head"),
            P(),
            P(),
            P("head", None),
            P(("groups", "dp"), "seq", None),
        ),
        out_specs=(P(("groups", "dp"), "seq", "head"), P(("groups", "dp"), "head")),
        check_vma=False,
    )
```

```python
import functools
import math

import jax
import jax.numpy as jnp
from jax import lax
from jax.experimental import pallas as pl
from jax.experimental.pallas import tpu as pltpu
import numpy as np
from jax.sharding import PartitionSpec as P

KEY = 128
VAL = 192
KERNEL_TAPS = 3
DILATION_STEP = 2


rope_base = 10000.0
norm_eps = 1e-06


def padded(cells, sides, width):
    for axis, dim in sides:
        count = lax.axis_size(axis)
        ends = count - 1
        head = lax.slice_in_dim(cells, 0, width, axis=dim)
        tail = lax.slice_in_dim(cells, cells.shape[dim] - width, cells.shape[dim], axis=dim)
        cells = jnp.concatenate(
            [
                lax.ppermute(tail, axis, [(i, (i + 1) % count) for i in range(ends)]),
                cells,
                lax.ppermute(head, axis, [((i + 1) % count, i) for i in range(ends)]),
            ],
            axis=dim,
        )
    return cells


def rotate(vectors, positions):
    halfway = vectors.shape[-1] // 2
    frequency = jnp.exp(
        -math.log(rope_base) * 2.0 * jnp.arange(halfway, dtype=jnp.float32) / vectors.shape[-1]
    )
    angles = positions.astype(jnp.float32)[:, None] * frequency[None, :]
    layout = (positions.shape[0],) + (1,) * (vectors.ndim - 2) + (halfway,)
    cosine = jnp.cos(angles).reshape(layout)
    sines = jnp.sin(angles).reshape(layout)
    leading = vectors[..., :halfway]
    trailing = vectors[..., halfway:]
    return jnp.concatenate(
        [leading * cosine - trailing * sines, leading * sines + trailing * cosine], axis=-1
    )


def attend_pieces(queries, key_rows, value_rows, state_in):
    total_keys = key_rows.shape[0]
    block_size = math.gcd(total_keys, 512)

    def one_block(block_index, state):
        running_max, running_sum, weighted = state
        key_block = lax.dynamic_slice_in_dim(key_rows, block_index * block_size, block_size, 0)
        value_block = lax.dynamic_slice_in_dim(value_rows, block_index * block_size, block_size, 0)
        scores = jnp.einsum(
            "thd,ud->htu", queries, key_block, preferred_element_type=jnp.float32
        ) * KEY ** (-0.5)
        new_max = jnp.maximum(running_max, jnp.max(scores, axis=-1))
        rescale = jnp.exp(running_max - new_max)
        weights = jnp.exp(scores - new_max[:, :, None])
        running_sum = running_sum * rescale + jnp.sum(weights, axis=-1)
        weighted = weighted * jnp.transpose(rescale)[:, :, None] + jnp.einsum(
            "htu,uv->thv",
            weights.astype(jnp.bfloat16),
            value_block,
            preferred_element_type=jnp.float32,
        )
        return (new_max, running_sum, weighted)

    return lax.fori_loop(0, total_keys // block_size, one_block, state_in)


def signal_to(sem, where):
    pl.semaphore_signal(sem, inc=1, device_id=where, device_id_type=pl.DeviceIdType.MESH)


def remote(src, dst, send_sem, recv_sem, where):
    return pltpu.make_async_remote_copy(
        src_ref=src,
        dst_ref=dst,
        send_sem=send_sem,
        recv_sem=recv_sem,
        device_id=where,
        device_id_type=pl.DeviceIdType.MESH,
    )


class Plan:
    def __init__(self, tokens, width, columns, dp, seq):
        self.tokens, self.width, self.columns = tokens, width, columns
        self.dp, self.seq = dp, seq
        self.levels = dp.bit_length() - 1
        self.block = width // dp
        self.rows = 64 if self.block % 64 == 0 else self.block
        self.pieces = self.block // self.rows
        self.chunk = 2 * VAL
        self.chunks = columns // self.chunk
        self.units = self.chunks * self.pieces
        self.gap = 4

    def scratch(self):
        tile = (self.rows, self.chunk)
        self.slots = self.gap * self.levels + 1
        shapes = [
            pltpu.VMEM((self.pieces, self.dp * self.rows, self.tokens), jnp.bfloat16),
            pltpu.VMEM((self.chunks, self.tokens, self.chunk), jnp.bfloat16),
            pltpu.VMEM((self.units,) + tile, jnp.float32),
            pltpu.VMEM((self.slots, self.dp * self.rows, self.chunk), jnp.float32),
        ]
        sends = self.levels + 2
        for level in range(self.levels):
            held = self.dp >> (level + 1)
            shapes += [pltpu.VMEM((self.units, held) + tile, jnp.bfloat16)] * 2
        shapes += [pltpu.VMEM((self.units,) + tile, jnp.bfloat16)] * 4
        shapes += [pltpu.SemaphoreType.DMA((self.units,))] * (2 * sends)
        return shapes


def turn_over(plan, cot_ref, cot_t):
    for piece in range(plan.pieces):
        for p in range(plan.dp):
            start = p * plan.block + piece * plan.rows
            cot_t[piece, p * plan.rows : (p + 1) * plan.rows, :] = jnp.transpose(
                cot_ref[:, start : start + plan.rows]
            )


def gradient_loop(plan, refs, out_ref, produce=None, least=0):
    cot_t, att, own, products = refs[:4]
    refs = refs[1:]
    levels, units = plan.levels, plan.units
    pairs = refs[3 : 3 + 2 * levels]
    ahead_out, ahead_in, back_out, back_in = refs[3 + 2 * levels : 7 + 2 * levels]
    sems = refs[7 + 2 * levels :]
    d = lax.axis_index("dp")
    s = lax.axis_index("seq")
    gap = plan.gap
    last = plan.seq - 1

    def summed(unit, p, level):
        start = pl.multiple_of(p * plan.rows, plan.rows)
        value = products[unit % plan.slots, pl.ds(start, plan.rows), :]
        for done in range(level):
            value = value + pairs[2 * done + 1][unit, p // (2 << done)].astype(jnp.float32)
        return value

    def level_copy(unit, level):
        step = 1 << level
        peer = d + (1 - 2 * ((d // step) % 2)) * step
        return remote(
            pairs[2 * level].at[unit],
            pairs[2 * level + 1].at[unit],
            sems[2 * level].at[unit],
            sems[2 * level + 1].at[unit],
            {"dp": peer},
        )

    def ahead_copy(unit):
        at = 2 * levels
        return remote(
            ahead_out.at[unit], ahead_in.at[unit], sems[at].at[unit], sems[at + 1].at[unit],
            {"seq": s + 1},
        )

    def back_copy(unit):
        at = 2 * levels + 2
        return remote(
            back_out.at[unit], back_in.at[unit], sems[at].at[unit], sems[at + 1].at[unit],
            {"seq": s - 1},
        )

    def within(unit):
        return jnp.logical_and(unit >= 0, unit < units)

    def step_at(t, carry):
        if produce is not None:
            produce(t)
        for level in range(levels):
            unit = t - gap * level

            @pl.when(within(unit))
            def _(unit=unit, level=level):
                if level == 0:
                    products[unit % plan.slots] = jnp.dot(
                        cot_t[unit % plan.pieces],
                        att[unit // plan.pieces],
                        preferred_element_type=jnp.float32,
                    )
                else:
                    level_copy(unit, level - 1).wait_recv()
                step = 1 << level
                base = d % step + (1 - (d // step) % 2) * step
                for i in range(plan.dp >> (level + 1)):
                    pairs[2 * level][unit, i] = summed(unit, base + i * 2 * step, level).astype(
                        jnp.bfloat16
                    )
                level_copy(unit, level).start()

        unit = t - gap * levels

        @pl.when(within(unit))
        def _():
            if levels > 0:
                level_copy(unit, levels - 1).wait_recv()
            else:
                products[unit % plan.slots] = jnp.dot(
                    cot_t[unit % plan.pieces],
                    att[unit // plan.pieces],
                    preferred_element_type=jnp.float32,
                )
            own[unit] = summed(unit, d, levels)

        if last > 0:
            fore = t - gap * (levels + s)

            @pl.when(jnp.logical_and(within(fore), s == 0))
            def _():
                ahead_out[fore] = own[fore].astype(jnp.bfloat16)
                ahead_copy(fore).start()

            @pl.when(jnp.logical_and(within(fore), s > 0))
            def _():
                ahead_copy(fore).wait_recv()

                @pl.when(s < last)
                def _():
                    ahead_out[fore] = (own[fore] + ahead_in[fore].astype(jnp.float32)).astype(
                        jnp.bfloat16
                    )
                    ahead_copy(fore).start()

            rear = t - gap * (levels + last - s)

            @pl.when(jnp.logical_and(within(rear), s == last))
            def _():
                back_out[rear] = own[rear].astype(jnp.bfloat16)
                back_copy(rear).start()

            @pl.when(jnp.logical_and(within(rear), s < last))
            def _():
                back_copy(rear).wait_recv()

                @pl.when(s > 0)
                def _():
                    back_out[rear] = (own[rear] + back_in[rear].astype(jnp.float32)).astype(
                        jnp.bfloat16
                    )
                    back_copy(rear).start()

        ready = t - gap * (levels + last)

        def store(value):
            row = pl.multiple_of((ready % plan.pieces) * plan.rows, plan.rows)
            column = pl.multiple_of((ready // plan.pieces) * plan.chunk, plan.chunk)
            out_ref[pl.ds(row, plan.rows), pl.ds(column, plan.chunk)] = value.astype(out_ref.dtype)

        if last == 0:

            @pl.when(within(ready))
            def _():
                store(own[ready])

        else:

            @pl.when(jnp.logical_and(within(ready), s == 0))
            def _():
                store(own[ready] + back_in[ready].astype(jnp.float32))

            @pl.when(jnp.logical_and(within(ready), s == last))
            def _():
                store(own[ready] + ahead_in[ready].astype(jnp.float32))

            if last > 1:

                @pl.when(
                    jnp.logical_and(within(ready), jnp.logical_and(s > 0, s < last))
                )
                def _():
                    store(
                        own[ready]
                        + ahead_in[ready].astype(jnp.float32)
                        + back_in[ready].astype(jnp.float32)
                    )

        return carry

    lax.fori_loop(0, max(least, units + gap * (levels + last)), step_at, 0)

    def drain(unit, carry):
        for level in range(levels):
            level_copy(unit, level).wait_send()
        if last > 0:

            @pl.when(s < last)
            def _():
                ahead_copy(unit).wait_send()

            @pl.when(s > 0)
            def _():
                back_copy(unit).wait_send()

        return carry

    lax.fori_loop(0, units, drain, 0)


def greet(plan):
    barrier = pltpu.get_barrier_semaphore()
    d = lax.axis_index("dp")
    s = lax.axis_index("seq")
    for level in range(plan.levels):
        step = 1 << level
        signal_to(barrier, {"dp": d + (1 - 2 * ((d // step) % 2)) * step})
    if plan.seq > 1:

        @pl.when(s > 0)
        def _():
            signal_to(barrier, {"seq": s - 1})

        @pl.when(s < plan.seq - 1)
        def _():
            signal_to(barrier, {"seq": s + 1})

    if plan.seq == 1:
        pl.semaphore_wait(barrier, plan.levels)
        return
    edge = jnp.logical_or(s == 0, s == plan.seq - 1)

    @pl.when(edge)
    def _():
        pl.semaphore_wait(barrier, plan.levels + 1)

    @pl.when(jnp.logical_not(edge))
    def _():
        pl.semaphore_wait(barrier, plan.levels + 2)


def gradient_kernel(plan, cot_ref, att_ref, out_ref, *refs):
    greet(plan)
    turn_over(plan, cot_ref, refs[0])
    for c in range(plan.chunks):
        refs[1][c] = att_ref[:, c * plan.chunk : (c + 1) * plan.chunk]
    gradient_loop(plan, refs, out_ref)


def reduced_gradient(upstream, attended):
    plan = Plan(
        upstream.shape[0], upstream.shape[1], attended.shape[1],
        lax.axis_size("dp"), lax.axis_size("seq"),
    )
    whole = pl.BlockSpec(memory_space=pltpu.VMEM)
    return pl.pallas_call(
        functools.partial(gradient_kernel, plan),
        out_shape=jax.ShapeDtypeStruct((plan.block, plan.columns), jnp.float32),
        in_specs=[whole, whole],
        out_specs=whole,
        scratch_shapes=plan.scratch(),
        compiler_params=pltpu.CompilerParams(
            collective_id=0, has_side_effects=True, vmem_limit_bytes=56 * 2**20
        ),
        name="reduced_gradient",
    )(upstream, attended)


EDGE = 16
TILE = 512
LANES = 128
DP = 4
SEQ = 4
HOLD = 256
SPLIT = 3
GAP = 5


def section_kernel(*refs):
    (x_hbm, conv_hbm, bias_in, gain_in, query_hbm, key_hbm, value_hbm, out_hbm, cot_hbm, turn_hbm) = refs[:10]
    mixed, grad_out = refs[10:12]
    (
        x_rows, conv_w, query_w, key_w, value_w, out_w, turn, fetched,
        edges, edge_sems, spread, stacked, pooled, normed, queries,
        kv, kv_send, kv_recv, values, peaks, sums, bias, gain,
        cot_in, cot_t, cot_sems, att_rows, att, att_sems, own,
        ahead_out, ahead_in, back_out, back_in, line_sems,
    ) = refs[12:]
    rows, channels = x_rows.shape
    tokens, width = pooled.shape
    tiles, blocks = width // TILE, channels // LANES
    half, quarter = tokens // 2, tokens // 4
    heads = queries.shape[0]
    part_rows = width // DP
    strips = att.shape[0]
    taps = KERNEL_TAPS
    d = lax.axis_index("dp")
    s = lax.axis_index("seq")
    mate = d + 1 - 2 * (d % 2)
    across = d + 2 - 4 * (d // 2)
    opposite = 3 - d
    far = 3 - s
    upper = s // 2
    end = jnp.logical_or(s == 0, s == SEQ - 1)
    inner = jnp.logical_not(end)

    pieces = ((0, quarter, half), (half, 0, quarter), (half + quarter, half + quarter, quarter))

    def conv_fetch(n):
        return pltpu.make_async_copy(
            conv_hbm.at[:, pl.ds(pl.multiple_of(n * TILE, TILE), TILE)],
            conv_w.at[n],
            fetched.at[6 + n],
        )

    def turn_fetch(i):
        to, at, count = pieces[i]
        return pltpu.make_async_copy(
            turn_hbm.at[pl.ds(pl.multiple_of(s * tokens + at, quarter), count)],
            turn.at[pl.ds(to, count)],
            fetched.at[5],
        )

    turn_whole = pltpu.make_async_copy(turn_hbm.at[pl.ds(0, tokens)], turn, fetched.at[5])

    x_fetch = pltpu.make_async_copy(x_hbm, x_rows, fetched.at[0])
    key_fetch = pltpu.make_async_copy(key_hbm, key_w, fetched.at[1])
    value_fetch = pltpu.make_async_copy(value_hbm, value_w, fetched.at[2])
    query_fetch = pltpu.make_async_copy(query_hbm, query_w, fetched.at[3])
    out_fetch = pltpu.make_async_copy(out_hbm, out_w, fetched.at[4])

    def cot_columns(owner):
        start = pl.multiple_of(owner * part_rows, part_rows)
        return cot_hbm.at[:, pl.ds(start, part_rows)]

    cot_own = pltpu.make_async_copy(cot_columns(d), cot_in.at[0], cot_sems.at[0])

    def cot_copy(slot):
        peer = (d, across, mate, opposite)[slot]
        return remote(
            cot_columns(peer), cot_in.at[slot], cot_sems.at[DP], cot_sems.at[slot], {"dp": peer}
        )

    x_fetch.start()
    for n in range(tiles):
        conv_fetch(n).start()
    key_fetch.start()
    value_fetch.start()
    for i in range(3):
        turn_fetch(i).start()

    barrier = pltpu.get_barrier_semaphore()
    for peer in (mate, across, opposite):
        signal_to(barrier, {"dp": peer})

    @pl.when(s > 0)
    def _():
        signal_to(barrier, {"seq": s - 1})

    @pl.when(s < SEQ - 1)
    def _():
        signal_to(barrier, {"seq": s + 1})

    @pl.when(end)
    def _():
        signal_to(barrier, {"seq": far})

    bias[...] = bias_in[...].reshape(bias.shape)
    gain[...] = gain_in[...].reshape(gain.shape)

    def edge_ahead():
        return remote(
            x_hbm.at[pl.ds(rows - EDGE, EDGE)], edges.at[0], edge_sems.at[0], edge_sems.at[1],
            {"seq": s + 1},
        )

    def edge_back():
        return remote(
            x_hbm.at[pl.ds(0, EDGE)], edges.at[1], edge_sems.at[2], edge_sems.at[3],
            {"seq": s - 1},
        )

    x_fetch.wait()
    query_fetch.start()
    for j in range(blocks):
        spread[j, EDGE : EDGE + rows, :] = x_rows[:, j * LANES : (j + 1) * LANES].astype(
            jnp.float32
        )
    blank = jnp.zeros((EDGE, LANES), jnp.float32)
    for j in range(blocks):
        spread[j, :EDGE, :] = blank
        spread[j, EDGE + rows :, :] = blank

    def stack(tap, to, first, count):
        for parity in range(2):
            for j in range(blocks):
                start = EDGE + parity + DILATION_STEP * (tap - 1) + 2 * first
                lane = tap * channels + j * LANES
                row = 2 * half * (to // half) + parity * half + to % half
                stacked[row : row + count, lane : lane + LANES] = spread[
                    j, pl.ds(start, count, stride=2), :
                ].astype(jnp.bfloat16)

    for tap in range(taps):
        for piece in pieces:
            stack(tap, *piece)

    pl.semaphore_wait(barrier, 5)

    @pl.when(s < SEQ - 1)
    def _():
        edge_ahead().start()

    @pl.when(s > 0)
    def _():
        edge_back().start()

    cot_own.start()
    for slot in range(1, DP):
        cot_copy(slot).start()
    out_fetch.start()

    def put_edge(which, start, tap, to, first):
        (edge_ahead if which == 0 else edge_back)().wait_recv()
        for j in range(blocks):
            spread[j, start : start + EDGE, :] = edges[
                which, :, j * LANES : (j + 1) * LANES
            ].astype(jnp.float32)
        stack(tap, to, first, EDGE)

    def turned(vectors, first, count):
        return (
            vectors * turn[pl.ds(first, count), :KEY]
            + pltpu.roll(vectors, KEY // 2, 1) * turn[pl.ds(first, count), KEY:]
        ).astype(jnp.bfloat16)

    def kv_copy(owner, part, piece, sem, where):
        span = pl.ds(0, half) if piece == 0 else pl.ds(half, half + quarter)
        block = kv.at[owner, part, span]
        return remote(
            block, block, kv_send.at[sem], kv_recv.at[(owner * 2 + part) * 2 + piece],
            {"seq": where},
        )

    def kv_own(part):
        for piece in range(2):

            @pl.when(s > 0)
            def _():
                kv_copy(s, part, piece, 0, s - 1).start()

            @pl.when(s < SEQ - 1)
            def _():
                kv_copy(s, part, piece, 0, s + 1).start()

            @pl.when(end)
            def _():
                kv_copy(s, part, piece, 0, far).start()

    def kv_relay(part):
        for piece in range(2):
            kv_copy(s - 1, part, piece, 1, s + 1).wait_recv()
            kv_copy(s - 1, part, piece, 1, s + 1).start()
            kv_copy(s + 1, part, piece, 1, s - 1).wait_recv()
            kv_copy(s + 1, part, piece, 1, s - 1).start()

    def conv_pass(part, carry):
        first = part == 0
        base = pl.multiple_of(part * half, half)
        here = pl.ds(base, half)

        @pl.when(jnp.logical_and(part == 1, s > 0))
        def _():
            put_edge(0, 0, 0, half, 0)

        @pl.when(jnp.logical_and(part == 1, s < SEQ - 1))
        def _():
            put_edge(1, EDGE + rows, taps - 1, tokens - EDGE, tokens - EDGE)

        def conv_tile(n, carry):
            @pl.when(first)
            def _():
                conv_fetch(n).wait()

            columns = pl.ds(pl.multiple_of(n * TILE, TILE), TILE)
            pre = (
                jnp.dot(
                    stacked[pl.ds(pl.multiple_of(part * tokens, tokens), tokens), :],
                    conv_w[n],
                    preferred_element_type=jnp.float32,
                )
                + bias[:, columns]
            )
            inside = math.sqrt(2.0 / math.pi) * (pre + 0.044715 * (pre * pre * pre))
            activated = pre * (0.5 * (1.0 + jnp.tanh(inside)))
            pooled[here, columns] = jnp.maximum(activated[:half], activated[half:]).astype(
                jnp.bfloat16
            )
            return carry

        lax.fori_loop(0, tiles, conv_tile, 0)

        count = 32

        def norm_part(i, carry):
            few = pl.ds(pl.multiple_of(base + i * count, count), count)
            wide = pooled[few, :].astype(jnp.float32)
            squares = jnp.mean(wide * wide, axis=-1, keepdims=True)
            normed[few, :] = (wide * lax.rsqrt(squares + norm_eps) * gain[...]).astype(
                jnp.bfloat16
            )
            return carry

        lax.fori_loop(0, half // count, norm_part, 0)

        @pl.when(first)
        def _():
            key_fetch.wait()
            value_fetch.wait()
            turn_whole.wait()

        ready = normed[here, :]
        kv[s, part, :half, :] = turned(
            jnp.dot(ready, key_w[...], preferred_element_type=jnp.float32), base, half
        )
        own_values = lax.dot_general(
            ready, value_w[...], (((1,), (1,)), ((), ())), preferred_element_type=jnp.float32
        )
        kv[s, part, half : 2 * half, :] = own_values[:, :LANES].astype(jnp.bfloat16)
        kv[s, part, 2 * half :, :] = jnp.concatenate(
            [own_values[:quarter, LANES:], own_values[quarter:, LANES:]], axis=1
        ).astype(jnp.bfloat16)
        kv_own(part)
        return carry

    lax.fori_loop(0, 2, conv_pass, 0)

    @pl.when(inner)
    def _():
        kv_relay(0)

    query_fetch.wait()

    def query_pair(c, carry):
        pair = jnp.dot(
            normed[...],
            query_w[:, pl.ds(pl.multiple_of(c * 2 * KEY, 2 * KEY), 2 * KEY)],
            preferred_element_type=jnp.float32,
        )
        queries[2 * c] = turned(pair[:, :KEY], 0, tokens)
        queries[2 * c + 1] = turned(pair[:, KEY:], 0, tokens)
        return carry

    lax.fori_loop(0, heads // 2, query_pair, 0)

    def turn_over(slot):
        (cot_own.wait if slot == 0 else cot_copy(slot).wait_recv)()
        middle = cot_in[slot, quarter : quarter + half, :]
        outer = jnp.concatenate(
            [cot_in[slot, :quarter, :], cot_in[slot, quarter + half :, :]], axis=0
        )
        at = slot * tokens
        cot_t[:, at : at + half] = jnp.transpose(middle)
        cot_t[:, at + half : at + tokens] = jnp.transpose(outer)

    def owner_of(k):
        low = s + upper * (3 - 2 * s)
        at = (k + low) % 2 if k < 2 else (k - 2 + 1 - low) % 2 + 2
        return at + upper * (3 - 2 * at)

    side = lax.broadcasted_iota(jnp.int32, (half, LANES), 1)

    def unpack(owner):
        for part in range(2):
            at = part * half
            values[at : at + half, :LANES] = kv[owner, part, half : 2 * half, :]
            rest = kv[owner, part, 2 * half :, :]
            rest = jnp.concatenate(
                [rest, pltpu.roll(rest.astype(jnp.float32), LANES // 2, 1).astype(jnp.bfloat16)],
                axis=0,
            ).astype(jnp.float32)
            rest = jnp.where(
                side < VAL - LANES, rest, jnp.where(side == VAL - LANES, 1.0, 0.0)
            )
            values[at : at + half, LANES:] = rest.astype(jnp.bfloat16)

    factor = KEY ** (-0.5) * math.log2(math.e)

    def twice(column):
        return jnp.concatenate([column, column], axis=1)

    def attend(h, keys, first):
        scores = lax.dot_general(
            queries[h], keys, (((1,), (1,)), ((), ())), preferred_element_type=jnp.float32
        )
        peak = jnp.max(scores, axis=-1, keepdims=True)
        if first:
            peak = jnp.broadcast_to(peak, (tokens, LANES))
        else:
            before = peaks[h]
            peak = jnp.maximum(before, peak)
        weights = jnp.exp2((scores - twice(peak)) * factor).astype(jnp.bfloat16)
        total = jnp.dot(weights, values[...], preferred_element_type=jnp.float32)
        if not first:
            total = total + sums[h] * twice(jnp.exp2((before - peak) * factor))
        return peak, total

    def keys_of(owner):
        return kv[owner, :, :half, :].reshape(tokens, KEY)

    def attend_block(k):
        owner = owner_of(k)
        unpack(owner)

        def pair(c, carry):
            for h in (2 * c, 2 * c + 1):
                peak, total = attend(h, keys_of(owner), k == 0)
                peaks[h] = peak
                sums[h] = total
            return carry

        lax.fori_loop(0, heads // 2, pair, 0)

    def wait_block(k):
        owner = owner_of(k)
        for part in range(2):
            for piece in range(2):
                kv_copy(owner, part, piece, 0, far).wait_recv()

    def att_copy(kind, b):
        slot = (0, 0, 1)[kind]
        to = (2, 1, 3)[kind]
        arrived = strips + b if kind == 1 else b
        return remote(
            att.at[b, slot], att.at[b, to], att_sems.at[2 * strips + kind], att_sems.at[arrived],
            {"dp": across if kind == 1 else mate},
        )

    def mate_strips(b):
        both = att.at[b, pl.ds(2, 2)]
        return remote(both, both, att_sems.at[2 * strips], att_sems.at[b], {"dp": mate})

    attend_block(0)

    @pl.when(inner)
    def _():
        kv_relay(1)

    for slot in range(DP):
        turn_over(slot)

    @pl.when(end)
    def _():
        wait_block(1)

    attend_block(1)

    @pl.when(end)
    def _():
        wait_block(2)

    attend_block(2)
    wait_block(3)
    last_owner = owner_of(3)
    unpack(last_owner)
    chunk = 2 * VAL
    each = chunk // LANES

    def last_pair(c, carry):
        done = []
        for h in (2 * c, 2 * c + 1):
            _, total = attend(h, keys_of(last_owner), False)
            done.append(total[:, :VAL] / total[:, VAL : VAL + 1])
        both = jnp.concatenate(done, axis=1).astype(jnp.bfloat16)
        att_rows[:, pl.ds(pl.multiple_of(c * chunk, LANES), chunk)] = both
        for i in range(each):
            b = c * each + i
            att[b, 0] = both[:, i * LANES : (i + 1) * LANES]
            att_copy(1, b).start()
            att_copy(0, b).start()
        return carry

    lax.fori_loop(0, heads // 2, last_pair, 0)
    out_fetch.wait()

    def mixed_tile(n, carry):
        columns = pl.ds(pl.multiple_of(n * TILE, TILE), TILE)
        total = pooled[:, columns].astype(jnp.float32) + jnp.dot(
            att_rows[...], out_w[:, columns], preferred_element_type=jnp.float32
        )
        total = total.astype(jnp.bfloat16)
        for at, to, count in pieces:
            mixed[to : to + count, columns] = total[at : at + count]
        return carry

    lax.fori_loop(0, tiles, mixed_tile, 0)

    units = strips * SPLIT
    last = SEQ - 1
    lead = SPLIT

    def place(unit):
        return unit // SPLIT, unit % SPLIT

    def ahead_copy(unit):
        at = place(unit)
        return remote(
            ahead_out.at[at], ahead_in.at[at], line_sems.at[2 * units], line_sems.at[unit],
            {"seq": s + 1},
        )

    def back_copy(unit):
        at = place(unit)
        return remote(
            back_out.at[at], back_in.at[at], line_sems.at[2 * units + 1],
            line_sems.at[units + unit], {"seq": s - 1},
        )

    def within(unit):
        return jnp.logical_and(unit >= 0, unit < units)

    def step_at(t, carry):
        @pl.when(jnp.logical_and(within(t), t % SPLIT == 0))
        def _():
            b = t // SPLIT
            att_copy(1, b).wait_recv()
            att_copy(2, b).start()

        @pl.when(jnp.logical_and(within(t - lead), t % SPLIT == 0))
        def _():
            b = (t - lead) // SPLIT
            mate_strips(b).wait_recv()
            own[b] = jnp.dot(
                cot_t[...],
                att[b].reshape(DP * tokens, LANES),
                preferred_element_type=jnp.float32,
            ).reshape(own.shape[1:])

        fore = t - lead - GAP * s

        @pl.when(jnp.logical_and(within(fore), s == 0))
        def _():
            ahead_out[place(fore)] = own[place(fore)].astype(jnp.bfloat16)
            ahead_copy(fore).start()

        @pl.when(jnp.logical_and(within(fore), s > 0))
        def _():
            ahead_copy(fore).wait_recv()

            @pl.when(s < last)
            def _():
                ahead_out[place(fore)] = (
                    own[place(fore)] + ahead_in[place(fore)].astype(jnp.float32)
                ).astype(jnp.bfloat16)
                ahead_copy(fore).start()

        rear = t - lead - GAP * (last - s)

        @pl.when(jnp.logical_and(within(rear), s == last))
        def _():
            back_out[place(rear)] = own[place(rear)].astype(jnp.bfloat16)
            back_copy(rear).start()

        @pl.when(jnp.logical_and(within(rear), s < last))
        def _():
            back_copy(rear).wait_recv()

            @pl.when(s > 0)
            def _():
                back_out[place(rear)] = (
                    own[place(rear)] + back_in[place(rear)].astype(jnp.float32)
                ).astype(jnp.bfloat16)
                back_copy(rear).start()

        ready = t - lead - GAP * last

        def store(value):
            b, i = place(ready)
            size = part_rows // SPLIT
            row = pl.multiple_of(i * size, size)
            column = pl.multiple_of(b * LANES, LANES)
            grad_out[pl.ds(row, size), pl.ds(column, LANES)] = value.astype(grad_out.dtype)

        @pl.when(jnp.logical_and(within(ready), s == 0))
        def _():
            store(own[place(ready)] + back_in[place(ready)].astype(jnp.float32))

        @pl.when(jnp.logical_and(within(ready), s == last))
        def _():
            store(own[place(ready)] + ahead_in[place(ready)].astype(jnp.float32))

        @pl.when(jnp.logical_and(within(ready), inner))
        def _():
            store(
                own[place(ready)]
                + ahead_in[place(ready)].astype(jnp.float32)
                + back_in[place(ready)].astype(jnp.float32)
            )

        return carry

    lax.fori_loop(0, units + lead + GAP * last, step_at, 0)

    @pl.when(s < last)
    def _():
        remote(
            ahead_out, ahead_in, line_sems.at[2 * units], line_sems.at[0], {"seq": s + 1}
        ).wait_send()

    @pl.when(s > 0)
    def _():
        remote(
            back_out, back_in, line_sems.at[2 * units + 1], line_sems.at[0], {"seq": s - 1}
        ).wait_send()

    for kind in range(3):
        sent = att.at[:, 0]
        remote(
            sent, sent, att_sems.at[2 * strips + kind], att_sems.at[0], {"dp": mate}
        ).wait_send()
    pair_of = kv.at[pl.ds(0, 2)]
    remote(pair_of, pair_of, kv_send.at[0], kv_recv.at[0], {"seq": far}).wait_send()

    @pl.when(inner)
    def _():
        remote(pair_of, pair_of, kv_send.at[1], kv_recv.at[0], {"seq": far}).wait_send()

    others = cot_in.at[pl.ds(1, DP - 1)]
    remote(others, others, cot_sems.at[DP], cot_sems.at[1], {"dp": mate}).wait_send()

    @pl.when(s < SEQ - 1)
    def _():
        edge_ahead().wait_send()

    @pl.when(s > 0)
    def _():
        edge_back().wait_send()


def turn_table(count):
    frequency = np.exp(
        np.float32(-math.log(rope_base) * 2.0) * np.arange(KEY // 2, dtype=np.float32) / KEY
    ).astype(np.float32)
    angles = np.arange(count, dtype=np.float32)[:, None] * frequency[None, :]
    cosine, sines = np.cos(angles), np.sin(angles)
    return np.concatenate([cosine, cosine, -sines, sines], axis=1).astype(np.float32)


def finish_kernel(mixed_in, grad_in, mixed, grad, sems):
    copies = (
        pltpu.make_async_copy(grad_in, grad, sems.at[0]),
        pltpu.make_async_copy(mixed_in, mixed, sems.at[1]),
    )
    for copy in copies:
        copy.start()
    for copy in copies:
        copy.wait()


def finish(mixed, gradient):
    away = pl.BlockSpec(memory_space=pl.ANY)
    return pl.pallas_call(
        finish_kernel,
        out_shape=(
            jax.ShapeDtypeStruct(mixed.shape, mixed.dtype),
            jax.ShapeDtypeStruct(gradient.shape, gradient.dtype),
        ),
        in_specs=[pl.BlockSpec(memory_space=pltpu.VMEM)] * 2,
        out_specs=(away, away),
        scratch_shapes=[pltpu.SemaphoreType.DMA((2,))],
        name="finish",
    )(
        pltpu.with_memory_space_constraint(mixed, pltpu.VMEM),
        pltpu.with_memory_space_constraint(gradient, pltpu.VMEM),
    )


def section(x_in, kernel_weight, conv_bias, norm_gain, w_query, w_key, w_value, w_out, cotangent):
    inputs, upstream = x_in[0], cotangent[0]
    rows, channels = inputs.shape
    width, columns = kernel_weight.shape[2], w_out.shape[0]
    tokens, tiles, strips = rows // 2, width // TILE, columns // LANES
    heads, part_rows = w_query.shape[1] // KEY, width // DP
    depth = KERNEL_TAPS * channels
    units = strips * SPLIT
    bf, f32 = jnp.bfloat16, jnp.float32
    line = pltpu.VMEM((strips, SPLIT, part_rows // SPLIT, LANES), bf)
    held = pl.BlockSpec(memory_space=pltpu.VMEM)
    away = pl.BlockSpec(memory_space=pl.ANY)
    mixed, gradient = pl.pallas_call(
        section_kernel,
        out_shape=(
            pltpu.VMEM((tokens, width), bf),
            pltpu.VMEM((part_rows, columns), f32),
        ),
        in_specs=[away, away, held, held, away, away, away, away, away, away],
        out_specs=(held, held),
        scratch_shapes=[
            pltpu.VMEM((rows, channels), bf),
            pltpu.VMEM((tiles, depth, TILE), bf),
            pltpu.VMEM(w_query.shape, bf),
            pltpu.VMEM(w_key.shape, bf),
            pltpu.VMEM(w_value.shape[::-1], bf),
            pltpu.VMEM(w_out.shape, bf),
            pltpu.VMEM((tokens, 2 * KEY), f32),
            pltpu.SemaphoreType.DMA((6 + tiles,)),
            pltpu.VMEM((2, EDGE, channels), bf),
            pltpu.SemaphoreType.DMA((4,)),
            pltpu.VMEM((channels // LANES, rows + 2 * EDGE, LANES), f32),
            pltpu.VMEM((rows, depth), bf),
            pltpu.VMEM((tokens, width), bf),
            pltpu.VMEM((tokens, width), bf),
            pltpu.VMEM((heads, tokens, KEY), bf),
            pltpu.VMEM((SEQ, 2, 5 * tokens // 4, KEY), bf),
            pltpu.SemaphoreType.DMA((2,)),
            pltpu.SemaphoreType.DMA((4 * SEQ,)),
            pltpu.VMEM((tokens, HOLD), bf),
            pltpu.VMEM((heads, tokens, LANES), f32),
            pltpu.VMEM((heads, tokens, HOLD), f32),
            pltpu.VMEM((1, width), f32),
            pltpu.VMEM((1, width), f32),
            pltpu.VMEM((DP, tokens, part_rows), bf),
            pltpu.VMEM((part_rows, DP * tokens), bf),
            pltpu.SemaphoreType.DMA((DP + 1,)),
            pltpu.VMEM((tokens, columns), bf),
            pltpu.VMEM((strips, DP, tokens, LANES), bf),
            pltpu.SemaphoreType.DMA((2 * strips + 3,)),
            pltpu.VMEM((strips, SPLIT, part_rows // SPLIT, LANES), f32),
            line, line, line, line,
            pltpu.SemaphoreType.DMA((2 * units + 2,)),
        ],
        compiler_params=pltpu.CompilerParams(
            collective_id=1, has_side_effects=True, vmem_limit_bytes=54 * 2**20
        ),
        name="section",
    )(
        inputs,
        kernel_weight.reshape(depth, width),
        conv_bias,
        norm_gain,
        w_query,
        w_key,
        jnp.transpose(w_value),
        w_out,
        upstream,
        turn_table(tokens * SEQ),
    )
    mixed, gradient = finish(mixed, gradient)
    return mixed[None], gradient


def local(x_in, kernel_weight, conv_bias, norm_gain, w_query, w_key, w_value, w_out, cotangent):
    inputs = x_in[0]
    edge_padding = DILATION_STEP * (KERNEL_TAPS - 1) // 2
    padded_rows = padded(inputs, (("seq", 0),), edge_padding)
    padded_row_count = inputs.shape[0]
    before_activation = jnp.broadcast_to(
        conv_bias[None, :], (padded_row_count, kernel_weight.shape[2])
    )
    for kernel_tap_index in range(KERNEL_TAPS):
        before_activation = before_activation + jnp.dot(
            padded_rows[
                kernel_tap_index * DILATION_STEP : kernel_tap_index * DILATION_STEP
                + padded_row_count
            ],
            kernel_weight[kernel_tap_index],
            preferred_element_type=jnp.float32,
        )
    activated = jax.nn.gelu(before_activation)
    pooled = jnp.max(activated.reshape(padded_row_count // 2, 2, -1), axis=1).astype(jnp.bfloat16)
    token_count = pooled.shape[0]
    features = lax.all_gather(pooled, "head", axis=1, tiled=True)
    widened = features.astype(jnp.float32)
    squares = jnp.mean(widened * widened, axis=-1, keepdims=True)
    normed = (widened * lax.rsqrt(squares + norm_eps) * norm_gain).astype(jnp.bfloat16)
    seq_offset = lax.axis_index("seq") * token_count
    positions = seq_offset + jnp.arange(token_count, dtype=jnp.int32)
    local_heads = w_query.shape[1] // KEY
    queries = rotate(
        jnp.dot(normed, w_query, preferred_element_type=jnp.float32).reshape(
            token_count, local_heads, KEY
        ),
        positions,
    ).astype(jnp.bfloat16)
    own_rows = token_count // lax.axis_size("head")
    row_offset = lax.axis_index("head") * own_rows
    own_normed = lax.dynamic_slice_in_dim(normed, row_offset, own_rows, 0)
    own_positions = seq_offset + row_offset + jnp.arange(own_rows, dtype=jnp.int32)
    key_rows = rotate(
        jnp.dot(own_normed, w_key, preferred_element_type=jnp.float32), own_positions
    ).astype(jnp.bfloat16)
    value_rows = jnp.dot(own_normed, w_value, preferred_element_type=jnp.float32).astype(
        jnp.bfloat16
    )
    start_state = (
        jnp.full((local_heads, token_count), -1e30, jnp.float32),
        jnp.zeros((local_heads, token_count), jnp.float32),
        jnp.zeros((token_count, local_heads, VAL), jnp.float32),
    )
    both = lax.all_gather(
        jnp.concatenate([key_rows, value_rows], axis=1), ("seq", "head"), axis=0, tiled=True
    )
    final_state = attend_pieces(
        queries,
        both[:, :KEY],
        both[:, KEY:],
        start_state,
    )
    running_max, running_sum, weighted = final_state
    attended = (
        (weighted / jnp.transpose(running_sum)[:, :, None])
        .astype(jnp.bfloat16)
        .reshape(token_count, local_heads * VAL)
    )
    projected = lax.psum_scatter(
        lax.dot_general(
            w_out, attended, (((0,), (1,)), ((), ())), preferred_element_type=jnp.float32
        ).astype(jnp.bfloat16),
        "head",
        scatter_dimension=0,
        tiled=True,
    ).astype(jnp.float32)
    mixed = (pooled.astype(jnp.float32) + jnp.transpose(projected)).astype(jnp.bfloat16)[None]
    upstream = cotangent[0]
    gradient = reduced_gradient(upstream, attended)
    return (mixed, gradient)


def solution(mesh):
    sizes = tuple(mesh.shape[axis] for axis in ("head", "seq", "dp"))
    return jax.shard_map(
        section if sizes == (1, SEQ, DP) else local,
        mesh=mesh,
        in_specs=(
            P(("groups", "dp"), "seq", None),
            P(None, None, "head"),
            P("head"),
            P(),
            P(None, "head"),
            P(),
            P(),
            P("head", None),
            P(("groups", "dp"), "seq", None),
        ),
        out_specs=(P(("groups", "dp"), "seq", "head"), P(("groups", "dp"), "head")),
        check_vma=False,
    )
```

```python
import functools
import math

import jax
import jax.numpy as jnp
from jax import lax
from jax.experimental import pallas as pl
from jax.experimental.pallas import tpu as pltpu
import numpy as np
from jax.sharding import PartitionSpec as P

KEY = 128
VAL = 192
KERNEL_TAPS = 3
DILATION_STEP = 2


rope_base = 10000.0
norm_eps = 1e-06


def padded(cells, sides, width):
    for axis, dim in sides:
        count = lax.axis_size(axis)
        ends = count - 1
        head = lax.slice_in_dim(cells, 0, width, axis=dim)
        tail = lax.slice_in_dim(cells, cells.shape[dim] - width, cells.shape[dim], axis=dim)
        cells = jnp.concatenate(
            [
                lax.ppermute(tail, axis, [(i, (i + 1) % count) for i in range(ends)]),
                cells,
                lax.ppermute(head, axis, [((i + 1) % count, i) for i in range(ends)]),
            ],
            axis=dim,
        )
    return cells


def rotate(vectors, positions):
    halfway = vectors.shape[-1] // 2
    frequency = jnp.exp(
        -math.log(rope_base) * 2.0 * jnp.arange(halfway, dtype=jnp.float32) / vectors.shape[-1]
    )
    angles = positions.astype(jnp.float32)[:, None] * frequency[None, :]
    layout = (positions.shape[0],) + (1,) * (vectors.ndim - 2) + (halfway,)
    cosine = jnp.cos(angles).reshape(layout)
    sines = jnp.sin(angles).reshape(layout)
    leading = vectors[..., :halfway]
    trailing = vectors[..., halfway:]
    return jnp.concatenate(
        [leading * cosine - trailing * sines, leading * sines + trailing * cosine], axis=-1
    )


def attend_pieces(queries, key_rows, value_rows, state_in):
    total_keys = key_rows.shape[0]
    block_size = math.gcd(total_keys, 512)

    def one_block(block_index, state):
        running_max, running_sum, weighted = state
        key_block = lax.dynamic_slice_in_dim(key_rows, block_index * block_size, block_size, 0)
        value_block = lax.dynamic_slice_in_dim(value_rows, block_index * block_size, block_size, 0)
        scores = jnp.einsum(
            "thd,ud->htu", queries, key_block, preferred_element_type=jnp.float32
        ) * KEY ** (-0.5)
        new_max = jnp.maximum(running_max, jnp.max(scores, axis=-1))
        rescale = jnp.exp(running_max - new_max)
        weights = jnp.exp(scores - new_max[:, :, None])
        running_sum = running_sum * rescale + jnp.sum(weights, axis=-1)
        weighted = weighted * jnp.transpose(rescale)[:, :, None] + jnp.einsum(
            "htu,uv->thv",
            weights.astype(jnp.bfloat16),
            value_block,
            preferred_element_type=jnp.float32,
        )
        return (new_max, running_sum, weighted)

    return lax.fori_loop(0, total_keys // block_size, one_block, state_in)


def signal_to(sem, where):
    pl.semaphore_signal(sem, inc=1, device_id=where, device_id_type=pl.DeviceIdType.MESH)


def remote(src, dst, send_sem, recv_sem, where):
    return pltpu.make_async_remote_copy(
        src_ref=src,
        dst_ref=dst,
        send_sem=send_sem,
        recv_sem=recv_sem,
        device_id=where,
        device_id_type=pl.DeviceIdType.MESH,
    )


class Plan:
    def __init__(self, tokens, width, columns, dp, seq):
        self.tokens, self.width, self.columns = tokens, width, columns
        self.dp, self.seq = dp, seq
        self.levels = dp.bit_length() - 1
        self.block = width // dp
        self.rows = 64 if self.block % 64 == 0 else self.block
        self.pieces = self.block // self.rows
        self.chunk = 2 * VAL
        self.chunks = columns // self.chunk
        self.units = self.chunks * self.pieces
        self.gap = 4

    def scratch(self):
        tile = (self.rows, self.chunk)
        self.slots = self.gap * self.levels + 1
        shapes = [
            pltpu.VMEM((self.pieces, self.dp * self.rows, self.tokens), jnp.bfloat16),
            pltpu.VMEM((self.chunks, self.tokens, self.chunk), jnp.bfloat16),
            pltpu.VMEM((self.units,) + tile, jnp.float32),
            pltpu.VMEM((self.slots, self.dp * self.rows, self.chunk), jnp.float32),
        ]
        sends = self.levels + 2
        for level in range(self.levels):
            held = self.dp >> (level + 1)
            shapes += [pltpu.VMEM((self.units, held) + tile, jnp.bfloat16)] * 2
        shapes += [pltpu.VMEM((self.units,) + tile, jnp.bfloat16)] * 4
        shapes += [pltpu.SemaphoreType.DMA((self.units,))] * (2 * sends)
        return shapes


def turn_over(plan, cot_ref, cot_t):
    for piece in range(plan.pieces):
        for p in range(plan.dp):
            start = p * plan.block + piece * plan.rows
            cot_t[piece, p * plan.rows : (p + 1) * plan.rows, :] = jnp.transpose(
                cot_ref[:, start : start + plan.rows]
            )


def gradient_loop(plan, refs, out_ref, produce=None, least=0):
    cot_t, att, own, products = refs[:4]
    refs = refs[1:]
    levels, units = plan.levels, plan.units
    pairs = refs[3 : 3 + 2 * levels]
    ahead_out, ahead_in, back_out, back_in = refs[3 + 2 * levels : 7 + 2 * levels]
    sems = refs[7 + 2 * levels :]
    d = lax.axis_index("dp")
    s = lax.axis_index("seq")
    gap = plan.gap
    last = plan.seq - 1

    def summed(unit, p, level):
        start = pl.multiple_of(p * plan.rows, plan.rows)
        value = products[unit % plan.slots, pl.ds(start, plan.rows), :]
        for done in range(level):
            value = value + pairs[2 * done + 1][unit, p // (2 << done)].astype(jnp.float32)
        return value

    def level_copy(unit, level):
        step = 1 << level
        peer = d + (1 - 2 * ((d // step) % 2)) * step
        return remote(
            pairs[2 * level].at[unit],
            pairs[2 * level + 1].at[unit],
            sems[2 * level].at[unit],
            sems[2 * level + 1].at[unit],
            {"dp": peer},
        )

    def ahead_copy(unit):
        at = 2 * levels
        return remote(
            ahead_out.at[unit], ahead_in.at[unit], sems[at].at[unit], sems[at + 1].at[unit],
            {"seq": s + 1},
        )

    def back_copy(unit):
        at = 2 * levels + 2
        return remote(
            back_out.at[unit], back_in.at[unit], sems[at].at[unit], sems[at + 1].at[unit],
            {"seq": s - 1},
        )

    def within(unit):
        return jnp.logical_and(unit >= 0, unit < units)

    def step_at(t, carry):
        if produce is not None:
            produce(t)
        for level in range(levels):
            unit = t - gap * level

            @pl.when(within(unit))
            def _(unit=unit, level=level):
                if level == 0:
                    products[unit % plan.slots] = jnp.dot(
                        cot_t[unit % plan.pieces],
                        att[unit // plan.pieces],
                        preferred_element_type=jnp.float32,
                    )
                else:
                    level_copy(unit, level - 1).wait_recv()
                step = 1 << level
                base = d % step + (1 - (d // step) % 2) * step
                for i in range(plan.dp >> (level + 1)):
                    pairs[2 * level][unit, i] = summed(unit, base + i * 2 * step, level).astype(
                        jnp.bfloat16
                    )
                level_copy(unit, level).start()

        unit = t - gap * levels

        @pl.when(within(unit))
        def _():
            if levels > 0:
                level_copy(unit, levels - 1).wait_recv()
            else:
                products[unit % plan.slots] = jnp.dot(
                    cot_t[unit % plan.pieces],
                    att[unit // plan.pieces],
                    preferred_element_type=jnp.float32,
                )
            own[unit] = summed(unit, d, levels)

        if last > 0:
            fore = t - gap * (levels + s)

            @pl.when(jnp.logical_and(within(fore), s == 0))
            def _():
                ahead_out[fore] = own[fore].astype(jnp.bfloat16)
                ahead_copy(fore).start()

            @pl.when(jnp.logical_and(within(fore), s > 0))
            def _():
                ahead_copy(fore).wait_recv()

                @pl.when(s < last)
                def _():
                    ahead_out[fore] = (own[fore] + ahead_in[fore].astype(jnp.float32)).astype(
                        jnp.bfloat16
                    )
                    ahead_copy(fore).start()

            rear = t - gap * (levels + last - s)

            @pl.when(jnp.logical_and(within(rear), s == last))
            def _():
                back_out[rear] = own[rear].astype(jnp.bfloat16)
                back_copy(rear).start()

            @pl.when(jnp.logical_and(within(rear), s < last))
            def _():
                back_copy(rear).wait_recv()

                @pl.when(s > 0)
                def _():
                    back_out[rear] = (own[rear] + back_in[rear].astype(jnp.float32)).astype(
                        jnp.bfloat16
                    )
                    back_copy(rear).start()

        ready = t - gap * (levels + last)

        def store(value):
            row = pl.multiple_of((ready % plan.pieces) * plan.rows, plan.rows)
            column = pl.multiple_of((ready // plan.pieces) * plan.chunk, plan.chunk)
            out_ref[pl.ds(row, plan.rows), pl.ds(column, plan.chunk)] = value.astype(out_ref.dtype)

        if last == 0:

            @pl.when(within(ready))
            def _():
                store(own[ready])

        else:

            @pl.when(jnp.logical_and(within(ready), s == 0))
            def _():
                store(own[ready] + back_in[ready].astype(jnp.float32))

            @pl.when(jnp.logical_and(within(ready), s == last))
            def _():
                store(own[ready] + ahead_in[ready].astype(jnp.float32))

            if last > 1:

                @pl.when(
                    jnp.logical_and(within(ready), jnp.logical_and(s > 0, s < last))
                )
                def _():
                    store(
                        own[ready]
                        + ahead_in[ready].astype(jnp.float32)
                        + back_in[ready].astype(jnp.float32)
                    )

        return carry

    lax.fori_loop(0, max(least, units + gap * (levels + last)), step_at, 0)

    def drain(unit, carry):
        for level in range(levels):
            level_copy(unit, level).wait_send()
        if last > 0:

            @pl.when(s < last)
            def _():
                ahead_copy(unit).wait_send()

            @pl.when(s > 0)
            def _():
                back_copy(unit).wait_send()

        return carry

    lax.fori_loop(0, units, drain, 0)


def greet(plan):
    barrier = pltpu.get_barrier_semaphore()
    d = lax.axis_index("dp")
    s = lax.axis_index("seq")
    for level in range(plan.levels):
        step = 1 << level
        signal_to(barrier, {"dp": d + (1 - 2 * ((d // step) % 2)) * step})
    if plan.seq > 1:

        @pl.when(s > 0)
        def _():
            signal_to(barrier, {"seq": s - 1})

        @pl.when(s < plan.seq - 1)
        def _():
            signal_to(barrier, {"seq": s + 1})

    if plan.seq == 1:
        pl.semaphore_wait(barrier, plan.levels)
        return
    edge = jnp.logical_or(s == 0, s == plan.seq - 1)

    @pl.when(edge)
    def _():
        pl.semaphore_wait(barrier, plan.levels + 1)

    @pl.when(jnp.logical_not(edge))
    def _():
        pl.semaphore_wait(barrier, plan.levels + 2)


def gradient_kernel(plan, cot_ref, att_ref, out_ref, *refs):
    greet(plan)
    turn_over(plan, cot_ref, refs[0])
    for c in range(plan.chunks):
        refs[1][c] = att_ref[:, c * plan.chunk : (c + 1) * plan.chunk]
    gradient_loop(plan, refs, out_ref)


def reduced_gradient(upstream, attended):
    plan = Plan(
        upstream.shape[0], upstream.shape[1], attended.shape[1],
        lax.axis_size("dp"), lax.axis_size("seq"),
    )
    whole = pl.BlockSpec(memory_space=pltpu.VMEM)
    return pl.pallas_call(
        functools.partial(gradient_kernel, plan),
        out_shape=jax.ShapeDtypeStruct((plan.block, plan.columns), jnp.float32),
        in_specs=[whole, whole],
        out_specs=whole,
        scratch_shapes=plan.scratch(),
        compiler_params=pltpu.CompilerParams(
            collective_id=0, has_side_effects=True, vmem_limit_bytes=56 * 2**20
        ),
        name="reduced_gradient",
    )(upstream, attended)


EDGE = 16
TILE = 512
LANES = 128
DP = 4
SEQ = 4
HOLD = 256
SPLIT = 3
GAP = 5


def section_kernel(*refs):
    (x_hbm, conv_hbm, bias_in, gain_in, query_hbm, key_hbm, value_hbm, out_hbm, cot_hbm, turn_hbm) = refs[:10]
    mixed, grad_out = refs[10:12]
    (
        x_rows, conv_w, query_w, key_w, value_w, out_w, turn, fetched,
        edges, edge_sems, spread, stacked, pooled, normed, queries,
        kv, kv_send, kv_recv, values, peaks, sums, bias, gain,
        cot_in, cot_t, cot_sems, att_rows, att, att_sems, own,
        ahead_out, ahead_in, back_out, back_in, line_sems, cross,
    ) = refs[12:]
    rows, channels = x_rows.shape
    tokens, width = pooled.shape
    tiles, blocks = width // TILE, channels // LANES
    half, quarter = tokens // 2, tokens // 4
    heads = queries.shape[0]
    part_rows = width // DP
    strips = att.shape[0]
    taps = KERNEL_TAPS
    d = lax.axis_index("dp")
    s = lax.axis_index("seq")
    mate = d + 1 - 2 * (d % 2)
    across = d + 2 - 4 * (d // 2)
    opposite = 3 - d
    far = 3 - s
    upper = s // 2
    end = jnp.logical_or(s == 0, s == SEQ - 1)
    inner = jnp.logical_not(end)

    pieces = ((0, quarter, half), (half, 0, quarter), (half + quarter, half + quarter, quarter))

    def conv_fetch(n):
        return pltpu.make_async_copy(
            conv_hbm.at[:, pl.ds(pl.multiple_of(n * TILE, TILE), TILE)],
            conv_w.at[n],
            fetched.at[6 + n],
        )

    def turn_fetch(i):
        to, at, count = pieces[i]
        return pltpu.make_async_copy(
            turn_hbm.at[pl.ds(pl.multiple_of(s * tokens + at, quarter), count)],
            turn.at[pl.ds(to, count)],
            fetched.at[5],
        )

    turn_whole = pltpu.make_async_copy(turn_hbm.at[pl.ds(0, tokens)], turn, fetched.at[5])

    x_fetch = pltpu.make_async_copy(x_hbm, x_rows, fetched.at[0])
    key_fetch = pltpu.make_async_copy(key_hbm, key_w, fetched.at[1])
    value_fetch = pltpu.make_async_copy(value_hbm, value_w, fetched.at[2])
    query_fetch = pltpu.make_async_copy(query_hbm, query_w, fetched.at[3])
    out_fetch = pltpu.make_async_copy(out_hbm, out_w, fetched.at[4])

    def cot_columns(owner):
        start = pl.multiple_of(owner * part_rows, part_rows)
        return cot_hbm.at[:, pl.ds(start, part_rows)]

    cot_local = tuple(
        pltpu.make_async_copy(cot_columns(block), cot_in.at[slot], cot_sems.at[slot])
        for slot, block in ((1, d), (4, across))
    )

    def cot_copy(slot):
        columns = {0: across, 2: mate, 3: opposite, 5: opposite}[slot]
        peer = mate if slot == 5 else columns
        return remote(
            cot_columns(columns), cot_in.at[slot], cot_sems.at[6], cot_sems.at[slot],
            {"dp": peer},
        )

    x_fetch.start()
    for n in range(tiles):
        conv_fetch(n).start()
    key_fetch.start()
    value_fetch.start()
    for i in range(3):
        turn_fetch(i).start()

    barrier = pltpu.get_barrier_semaphore()
    for peer in (mate, across, opposite):
        signal_to(barrier, {"dp": peer})

    @pl.when(s > 0)
    def _():
        signal_to(barrier, {"seq": s - 1})

    @pl.when(s < SEQ - 1)
    def _():
        signal_to(barrier, {"seq": s + 1})

    @pl.when(end)
    def _():
        signal_to(barrier, {"seq": far})

    bias[...] = bias_in[...].reshape(bias.shape)
    gain[...] = gain_in[...].reshape(gain.shape)

    def edge_ahead():
        return remote(
            x_hbm.at[pl.ds(rows - EDGE, EDGE)], edges.at[0], edge_sems.at[0], edge_sems.at[1],
            {"seq": s + 1},
        )

    def edge_back():
        return remote(
            x_hbm.at[pl.ds(0, EDGE)], edges.at[1], edge_sems.at[2], edge_sems.at[3],
            {"seq": s - 1},
        )

    x_fetch.wait()
    query_fetch.start()
    for j in range(blocks):
        spread[j, EDGE : EDGE + rows, :] = x_rows[:, j * LANES : (j + 1) * LANES].astype(
            jnp.float32
        )
    blank = jnp.zeros((EDGE, LANES), jnp.float32)
    for j in range(blocks):
        spread[j, :EDGE, :] = blank
        spread[j, EDGE + rows :, :] = blank

    def stack(tap, to, first, count):
        for parity in range(2):
            for j in range(blocks):
                start = EDGE + parity + DILATION_STEP * (tap - 1) + 2 * first
                lane = tap * channels + j * LANES
                row = 2 * half * (to // half) + parity * half + to % half
                stacked[row : row + count, lane : lane + LANES] = spread[
                    j, pl.ds(start, count, stride=2), :
                ].astype(jnp.bfloat16)

    for tap in range(taps):
        for piece in pieces:
            stack(tap, *piece)

    pl.semaphore_wait(barrier, 5)

    @pl.when(s < SEQ - 1)
    def _():
        edge_ahead().start()

    @pl.when(s > 0)
    def _():
        edge_back().start()

    for slot in (0, 2, 3, 5):
        cot_copy(slot).start()
    for copy in cot_local:
        copy.start()
    out_fetch.start()

    def put_edge(which, start, tap, to, first):
        (edge_ahead if which == 0 else edge_back)().wait_recv()
        for j in range(blocks):
            spread[j, start : start + EDGE, :] = edges[
                which, :, j * LANES : (j + 1) * LANES
            ].astype(jnp.float32)
        stack(tap, to, first, EDGE)

    def turned(vectors, first, count):
        return (
            vectors * turn[pl.ds(first, count), :KEY]
            + pltpu.roll(vectors, KEY // 2, 1) * turn[pl.ds(first, count), KEY:]
        ).astype(jnp.bfloat16)

    def kv_copy(owner, part, piece, sem, where):
        span = pl.ds(0, half) if piece == 0 else pl.ds(half, half + quarter)
        block = kv.at[owner, part, span]
        return remote(
            block, block, kv_send.at[sem], kv_recv.at[(owner * 2 + part) * 2 + piece],
            {"seq": where},
        )

    def kv_own(part):
        for piece in range(2):

            @pl.when(s > 0)
            def _():
                kv_copy(s, part, piece, 0, s - 1).start()

            @pl.when(s < SEQ - 1)
            def _():
                kv_copy(s, part, piece, 0, s + 1).start()

            @pl.when(end)
            def _():
                kv_copy(s, part, piece, 0, far).start()

    def kv_relay(part):
        for piece in range(2):
            kv_copy(s - 1, part, piece, 1, s + 1).wait_recv()
            kv_copy(s - 1, part, piece, 1, s + 1).start()
            kv_copy(s + 1, part, piece, 1, s - 1).wait_recv()
            kv_copy(s + 1, part, piece, 1, s - 1).start()

    def conv_pass(part, carry):
        first = part == 0
        base = pl.multiple_of(part * half, half)
        here = pl.ds(base, half)

        @pl.when(jnp.logical_and(part == 1, s > 0))
        def _():
            put_edge(0, 0, 0, half, 0)

        @pl.when(jnp.logical_and(part == 1, s < SEQ - 1))
        def _():
            put_edge(1, EDGE + rows, taps - 1, tokens - EDGE, tokens - EDGE)

        def conv_tile(n, carry):
            @pl.when(first)
            def _():
                conv_fetch(n).wait()

            columns = pl.ds(pl.multiple_of(n * TILE, TILE), TILE)
            pre = (
                jnp.dot(
                    stacked[pl.ds(pl.multiple_of(part * tokens, tokens), tokens), :],
                    conv_w[n],
                    preferred_element_type=jnp.float32,
                )
                + bias[:, columns]
            )
            inside = math.sqrt(2.0 / math.pi) * (pre + 0.044715 * (pre * pre * pre))
            activated = pre * (0.5 * (1.0 + jnp.tanh(inside)))
            pooled[here, columns] = jnp.maximum(activated[:half], activated[half:]).astype(
                jnp.bfloat16
            )
            return carry

        lax.fori_loop(0, tiles, conv_tile, 0)

        count = 32

        def norm_part(i, carry):
            few = pl.ds(pl.multiple_of(base + i * count, count), count)
            wide = pooled[few, :].astype(jnp.float32)
            squares = jnp.mean(wide * wide, axis=-1, keepdims=True)
            normed[few, :] = (wide * lax.rsqrt(squares + norm_eps) * gain[...]).astype(
                jnp.bfloat16
            )
            return carry

        lax.fori_loop(0, half // count, norm_part, 0)

        @pl.when(first)
        def _():
            key_fetch.wait()
            value_fetch.wait()
            turn_whole.wait()

        ready = normed[here, :]
        kv[s, part, :half, :] = turned(
            jnp.dot(ready, key_w[...], preferred_element_type=jnp.float32), base, half
        )
        own_values = lax.dot_general(
            ready, value_w[...], (((1,), (1,)), ((), ())), preferred_element_type=jnp.float32
        )
        kv[s, part, half : 2 * half, :] = own_values[:, :LANES].astype(jnp.bfloat16)
        kv[s, part, 2 * half :, :] = jnp.concatenate(
            [own_values[:quarter, LANES:], own_values[quarter:, LANES:]], axis=1
        ).astype(jnp.bfloat16)
        kv_own(part)
        return carry

    lax.fori_loop(0, 2, conv_pass, 0)

    @pl.when(inner)
    def _():
        kv_relay(0)

    query_fetch.wait()

    def query_pair(c, carry):
        pair = jnp.dot(
            normed[...],
            query_w[:, pl.ds(pl.multiple_of(c * 2 * KEY, 2 * KEY), 2 * KEY)],
            preferred_element_type=jnp.float32,
        )
        queries[2 * c] = turned(pair[:, :KEY], 0, tokens)
        queries[2 * c + 1] = turned(pair[:, KEY:], 0, tokens)
        return carry

    lax.fori_loop(0, heads // 2, query_pair, 0)

    def turn_over(slot):
        if slot in (1, 4):
            cot_local[slot // 4].wait()
        else:
            cot_copy(slot).wait_recv()
        middle = cot_in[slot, quarter : quarter + half, :]
        outer = jnp.concatenate(
            [cot_in[slot, :quarter, :], cot_in[slot, quarter + half :, :]], axis=0
        )
        at = slot * tokens
        cot_t[:, at : at + half] = jnp.transpose(middle)
        cot_t[:, at + half : at + tokens] = jnp.transpose(outer)

    def owner_of(k):
        low = s + upper * (3 - 2 * s)
        at = (k + low) % 2 if k < 2 else (k - 2 + 1 - low) % 2 + 2
        return at + upper * (3 - 2 * at)

    side = lax.broadcasted_iota(jnp.int32, (half, LANES), 1)

    def unpack(owner):
        for part in range(2):
            at = part * half
            values[at : at + half, :LANES] = kv[owner, part, half : 2 * half, :]
            rest = kv[owner, part, 2 * half :, :]
            rest = jnp.concatenate(
                [rest, pltpu.roll(rest.astype(jnp.float32), LANES // 2, 1).astype(jnp.bfloat16)],
                axis=0,
            ).astype(jnp.float32)
            rest = jnp.where(
                side < VAL - LANES, rest, jnp.where(side == VAL - LANES, 1.0, 0.0)
            )
            values[at : at + half, LANES:] = rest.astype(jnp.bfloat16)

    factor = KEY ** (-0.5) * math.log2(math.e)

    def twice(column):
        return jnp.concatenate([column, column], axis=1)

    def attend(h, keys, first):
        scores = lax.dot_general(
            queries[h], keys, (((1,), (1,)), ((), ())), preferred_element_type=jnp.float32
        )
        peak = jnp.max(scores, axis=-1, keepdims=True)
        if first:
            peak = jnp.broadcast_to(peak, (tokens, LANES))
        else:
            before = peaks[h]
            peak = jnp.maximum(before, peak)
        weights = jnp.exp2((scores - twice(peak)) * factor).astype(jnp.bfloat16)
        total = jnp.dot(weights, values[...], preferred_element_type=jnp.float32)
        if not first:
            total = total + sums[h] * twice(jnp.exp2((before - peak) * factor))
        return peak, total

    def keys_of(owner):
        return kv[owner, :, :half, :].reshape(tokens, KEY)

    def attend_block(k):
        owner = owner_of(k)
        unpack(owner)

        def pair(c, carry):
            for h in (2 * c, 2 * c + 1):
                peak, total = attend(h, keys_of(owner), k == 0)
                peaks[h] = peak
                sums[h] = total
            return carry

        lax.fori_loop(0, heads // 2, pair, 0)

    def wait_block(k):
        owner = owner_of(k)
        for part in range(2):
            for piece in range(2):
                kv_copy(owner, part, piece, 0, far).wait_recv()

    def att_copy(kind, b):
        slot = (1, 1, 0)[kind]
        to = (2, 0, 3)[kind]
        arrived = strips + b if kind == 1 else b
        return remote(
            att.at[b, slot], att.at[b, to], att_sems.at[2 * strips + kind], att_sems.at[arrived],
            {"dp": across if kind == 1 else mate},
        )

    def mate_strips(b):
        both = att.at[b, pl.ds(2, 2)]
        return remote(both, both, att_sems.at[2 * strips], att_sems.at[b], {"dp": mate})

    attend_block(0)

    @pl.when(inner)
    def _():
        kv_relay(1)

    for slot in range(6):
        turn_over(slot)

    @pl.when(end)
    def _():
        wait_block(1)

    attend_block(1)

    @pl.when(end)
    def _():
        wait_block(2)

    attend_block(2)
    wait_block(3)
    last_owner = owner_of(3)
    unpack(last_owner)
    chunk = 2 * VAL
    each = chunk // LANES

    def last_pair(c):
        done = []
        for h in (2 * c, 2 * c + 1):
            _, total = attend(h, keys_of(last_owner), False)
            done.append(total[:, :VAL] / total[:, VAL : VAL + 1])
        both = jnp.concatenate(done, axis=1).astype(jnp.bfloat16)
        for i in range(each):
            b = c * each + i
            att[b, 1] = both[:, i * LANES : (i + 1) * LANES]
            att_copy(0, b).start()

            @pl.when(b > 0)
            def _(b=b):
                att_copy(1, b).start()

        att_rows[:, pl.ds(pl.multiple_of(c * chunk, LANES), chunk)] = both

    def mixed_tile(n):
        columns = pl.ds(pl.multiple_of(n * TILE, TILE), TILE)
        total = pooled[:, columns].astype(jnp.float32) + jnp.dot(
            att_rows[...], out_w[:, columns], preferred_element_type=jnp.float32
        )
        total = total.astype(jnp.bfloat16)
        for at, to, count in pieces:
            mixed[to : to + count, columns] = total[at : at + count]

    out_fetch.wait()

    count = strips + 1
    size = part_rows // SPLIT
    units = count * SPLIT
    last = SEQ - 1

    def place(unit):
        return unit // SPLIT, unit % SPLIT

    def ahead_copy(unit):
        at = place(unit)
        return remote(
            ahead_out.at[at], ahead_in.at[at], line_sems.at[2 * units], line_sems.at[unit],
            {"seq": s + 1},
        )

    def back_copy(unit):
        at = place(unit)
        return remote(
            back_out.at[at], back_in.at[at], line_sems.at[2 * units + 1],
            line_sems.at[units + unit], {"seq": s - 1},
        )

    def within(unit):
        return jnp.logical_and(unit >= 0, unit < units)

    def cross_copy():
        return remote(
            cross.at[0], cross.at[1], line_sems.at[2 * units + 2], line_sems.at[2 * units + 3],
            {"dp": across},
        )

    def step_at(step, carry):
        t = step - 1

        @pl.when(t == 0)
        def _():
            att_copy(0, 0).wait_recv()
            near = att[0, 1:3].reshape(2 * tokens, LANES)
            for i, at in enumerate((1, 4)):
                own[i] = jnp.dot(
                    cot_t[:, at * tokens : (at + 2) * tokens],
                    near,
                    preferred_element_type=jnp.float32,
                ).reshape(own.shape[1:])

        @pl.when(jnp.logical_and(jnp.logical_and(t >= 2 * SPLIT, t < units), t % SPLIT == 0))
        def _():
            q = t // SPLIT
            mate_strips(q - 1).wait_recv()
            own[q] = jnp.dot(
                cot_t[:, : DP * tokens],
                att[q - 1].reshape(DP * tokens, LANES),
                preferred_element_type=jnp.float32,
            ).reshape(own.shape[1:])

        fore = t - GAP * s

        @pl.when(jnp.logical_and(within(fore), s == 0))
        def _():
            ahead_out[place(fore)] = own[place(fore)].astype(jnp.bfloat16)
            ahead_copy(fore).start()

        @pl.when(jnp.logical_and(within(fore), s > 0))
        def _():
            ahead_copy(fore).wait_recv()

            @pl.when(s < last)
            def _():
                ahead_out[place(fore)] = (
                    own[place(fore)] + ahead_in[place(fore)].astype(jnp.float32)
                ).astype(jnp.bfloat16)
                ahead_copy(fore).start()

        rear = t - GAP * (last - s)

        @pl.when(jnp.logical_and(within(rear), s == last))
        def _():
            back_out[place(rear)] = own[place(rear)].astype(jnp.bfloat16)
            back_copy(rear).start()

        @pl.when(jnp.logical_and(within(rear), s < last))
        def _():
            back_copy(rear).wait_recv()

            @pl.when(s > 0)
            def _():
                back_out[place(rear)] = (
                    own[place(rear)] + back_in[place(rear)].astype(jnp.float32)
                ).astype(jnp.bfloat16)
                back_copy(rear).start()

        ready = t - GAP * last

        def store(value):
            q, i = place(ready)
            row = pl.multiple_of(i * size, size)

            @pl.when(q == 1)
            def _():
                cross[0, pl.ds(row, size), :] = value.astype(cross.dtype)

            @pl.when(q == 0)
            def _():
                grad_out[pl.ds(row, size), :LANES] = value

            @pl.when(q > 1)
            def _():
                column = pl.multiple_of((q - 1) * LANES, LANES)
                grad_out[pl.ds(row, size), pl.ds(column, LANES)] = value

        @pl.when(jnp.logical_and(within(ready), s == 0))
        def _():
            store(own[place(ready)] + back_in[place(ready)].astype(jnp.float32))

        @pl.when(jnp.logical_and(within(ready), s == last))
        def _():
            store(own[place(ready)] + ahead_in[place(ready)].astype(jnp.float32))

        @pl.when(jnp.logical_and(within(ready), inner))
        def _():
            store(
                own[place(ready)]
                + ahead_in[place(ready)].astype(jnp.float32)
                + back_in[place(ready)].astype(jnp.float32)
            )

        @pl.when(ready == 2 * SPLIT - 1)
        def _():
            cross_copy().start()

        @pl.when(jnp.logical_and(step < heads, step % 2 == 0))
        def _():
            last_pair(step // 2)

        @pl.when(
            jnp.logical_and(
                jnp.logical_and(t >= SPLIT, t < strips * SPLIT), t % SPLIT == SPLIT // 2
            )
        )
        def _():
            b = t // SPLIT
            att_copy(1, b).wait_recv()
            att_copy(2, b).start()

        tile = t - 4 * SPLIT

        @pl.when(
            jnp.logical_and(jnp.logical_and(tile >= 0, tile < 2 * tiles), tile % 2 == 0)
        )
        def _():
            mixed_tile(tile // 2)

        return carry

    lax.fori_loop(0, units + GAP * last + 1, step_at, 0)
    cross_copy().wait_recv()
    grad_out[:, :LANES] = grad_out[:, :LANES] + cross[1].astype(jnp.float32)
    cross_copy().wait_send()

    @pl.when(s < last)
    def _():
        remote(
            ahead_out, ahead_in, line_sems.at[2 * units], line_sems.at[0], {"seq": s + 1}
        ).wait_send()

    @pl.when(s > 0)
    def _():
        remote(
            back_out, back_in, line_sems.at[2 * units + 1], line_sems.at[0], {"seq": s - 1}
        ).wait_send()

    for kind in range(3):
        sent = att.at[:, 0] if kind == 0 else att.at[pl.ds(1, strips - 1), 0]
        remote(
            sent, sent, att_sems.at[2 * strips + kind], att_sems.at[0], {"dp": mate}
        ).wait_send()
    pair_of = kv.at[pl.ds(0, 2)]
    remote(pair_of, pair_of, kv_send.at[0], kv_recv.at[0], {"seq": far}).wait_send()

    @pl.when(inner)
    def _():
        remote(pair_of, pair_of, kv_send.at[1], kv_recv.at[0], {"seq": far}).wait_send()

    others = cot_in.at[pl.ds(0, 4)]
    remote(others, others, cot_sems.at[6], cot_sems.at[0], {"dp": mate}).wait_send()

    @pl.when(s < SEQ - 1)
    def _():
        edge_ahead().wait_send()

    @pl.when(s > 0)
    def _():
        edge_back().wait_send()


def turn_table(count):
    frequency = np.exp(
        np.float32(-math.log(rope_base) * 2.0) * np.arange(KEY // 2, dtype=np.float32) / KEY
    ).astype(np.float32)
    angles = np.arange(count, dtype=np.float32)[:, None] * frequency[None, :]
    cosine, sines = np.cos(angles), np.sin(angles)
    return np.concatenate([cosine, cosine, -sines, sines], axis=1).astype(np.float32)


def finish_kernel(mixed_in, grad_in, mixed, grad, sems):
    copies = (
        pltpu.make_async_copy(grad_in, grad, sems.at[0]),
        pltpu.make_async_copy(mixed_in, mixed, sems.at[1]),
    )
    for copy in copies:
        copy.start()
    for copy in copies:
        copy.wait()


def finish(mixed, gradient):
    away = pl.BlockSpec(memory_space=pl.ANY)
    return pl.pallas_call(
        finish_kernel,
        out_shape=(
            jax.ShapeDtypeStruct(mixed.shape, mixed.dtype),
            jax.ShapeDtypeStruct(gradient.shape, gradient.dtype),
        ),
        in_specs=[pl.BlockSpec(memory_space=pltpu.VMEM)] * 2,
        out_specs=(away, away),
        scratch_shapes=[pltpu.SemaphoreType.DMA((2,))],
        name="finish",
    )(
        pltpu.with_memory_space_constraint(mixed, pltpu.VMEM),
        pltpu.with_memory_space_constraint(gradient, pltpu.VMEM),
    )


def section(x_in, kernel_weight, conv_bias, norm_gain, w_query, w_key, w_value, w_out, cotangent):
    inputs, upstream = x_in[0], cotangent[0]
    rows, channels = inputs.shape
    width, columns = kernel_weight.shape[2], w_out.shape[0]
    tokens, tiles, strips = rows // 2, width // TILE, columns // LANES
    heads, part_rows = w_query.shape[1] // KEY, width // DP
    depth = KERNEL_TAPS * channels
    units = (strips + 1) * SPLIT
    bf, f32 = jnp.bfloat16, jnp.float32
    line = pltpu.VMEM((strips + 1, SPLIT, part_rows // SPLIT, LANES), bf)
    held = pl.BlockSpec(memory_space=pltpu.VMEM)
    away = pl.BlockSpec(memory_space=pl.ANY)
    mixed, gradient = pl.pallas_call(
        section_kernel,
        out_shape=(
            pltpu.VMEM((tokens, width), bf),
            pltpu.VMEM((part_rows, columns), f32),
        ),
        in_specs=[away, away, held, held, away, away, away, away, away, away],
        out_specs=(held, held),
        scratch_shapes=[
            pltpu.VMEM((rows, channels), bf),
            pltpu.VMEM((tiles, depth, TILE), bf),
            pltpu.VMEM(w_query.shape, bf),
            pltpu.VMEM(w_key.shape, bf),
            pltpu.VMEM(w_value.shape[::-1], bf),
            pltpu.VMEM(w_out.shape, bf),
            pltpu.VMEM((tokens, 2 * KEY), f32),
            pltpu.SemaphoreType.DMA((6 + tiles,)),
            pltpu.VMEM((2, EDGE, channels), bf),
            pltpu.SemaphoreType.DMA((4,)),
            pltpu.VMEM((channels // LANES, rows + 2 * EDGE, LANES), f32),
            pltpu.VMEM((rows, depth), bf),
            pltpu.VMEM((tokens, width), bf),
            pltpu.VMEM((tokens, width), bf),
            pltpu.VMEM((heads, tokens, KEY), bf),
            pltpu.VMEM((SEQ, 2, 5 * tokens // 4, KEY), bf),
            pltpu.SemaphoreType.DMA((2,)),
            pltpu.SemaphoreType.DMA((4 * SEQ,)),
            pltpu.VMEM((tokens, HOLD), bf),
            pltpu.VMEM((heads, tokens, LANES), f32),
            pltpu.VMEM((heads, tokens, HOLD), f32),
            pltpu.VMEM((1, width), f32),
            pltpu.VMEM((1, width), f32),
            pltpu.VMEM((6, tokens, part_rows), bf),
            pltpu.VMEM((part_rows, 6 * tokens), bf),
            pltpu.SemaphoreType.DMA((7,)),
            pltpu.VMEM((tokens, columns), bf),
            pltpu.VMEM((strips, DP, tokens, LANES), bf),
            pltpu.SemaphoreType.DMA((2 * strips + 3,)),
            pltpu.VMEM((strips + 1, SPLIT, part_rows // SPLIT, LANES), f32),
            line, line, line, line,
            pltpu.SemaphoreType.DMA((2 * units + 4,)),
            pltpu.VMEM((2, part_rows, LANES), bf),
        ],
        compiler_params=pltpu.CompilerParams(
            collective_id=1, has_side_effects=True, vmem_limit_bytes=54 * 2**20
        ),
        name="section",
    )(
        inputs,
        kernel_weight.reshape(depth, width),
        conv_bias,
        norm_gain,
        w_query,
        w_key,
        jnp.transpose(w_value),
        w_out,
        upstream,
        turn_table(tokens * SEQ),
    )
    mixed, gradient = finish(mixed, gradient)
    return mixed[None], gradient


def local(x_in, kernel_weight, conv_bias, norm_gain, w_query, w_key, w_value, w_out, cotangent):
    inputs = x_in[0]
    edge_padding = DILATION_STEP * (KERNEL_TAPS - 1) // 2
    padded_rows = padded(inputs, (("seq", 0),), edge_padding)
    padded_row_count = inputs.shape[0]
    before_activation = jnp.broadcast_to(
        conv_bias[None, :], (padded_row_count, kernel_weight.shape[2])
    )
    for kernel_tap_index in range(KERNEL_TAPS):
        before_activation = before_activation + jnp.dot(
            padded_rows[
                kernel_tap_index * DILATION_STEP : kernel_tap_index * DILATION_STEP
                + padded_row_count
            ],
            kernel_weight[kernel_tap_index],
            preferred_element_type=jnp.float32,
        )
    activated = jax.nn.gelu(before_activation)
    pooled = jnp.max(activated.reshape(padded_row_count // 2, 2, -1), axis=1).astype(jnp.bfloat16)
    token_count = pooled.shape[0]
    features = lax.all_gather(pooled, "head", axis=1, tiled=True)
    widened = features.astype(jnp.float32)
    squares = jnp.mean(widened * widened, axis=-1, keepdims=True)
    normed = (widened * lax.rsqrt(squares + norm_eps) * norm_gain).astype(jnp.bfloat16)
    seq_offset = lax.axis_index("seq") * token_count
    positions = seq_offset + jnp.arange(token_count, dtype=jnp.int32)
    local_heads = w_query.shape[1] // KEY
    queries = rotate(
        jnp.dot(normed, w_query, preferred_element_type=jnp.float32).reshape(
            token_count, local_heads, KEY
        ),
        positions,
    ).astype(jnp.bfloat16)
    own_rows = token_count // lax.axis_size("head")
    row_offset = lax.axis_index("head") * own_rows
    own_normed = lax.dynamic_slice_in_dim(normed, row_offset, own_rows, 0)
    own_positions = seq_offset + row_offset + jnp.arange(own_rows, dtype=jnp.int32)
    key_rows = rotate(
        jnp.dot(own_normed, w_key, preferred_element_type=jnp.float32), own_positions
    ).astype(jnp.bfloat16)
    value_rows = jnp.dot(own_normed, w_value, preferred_element_type=jnp.float32).astype(
        jnp.bfloat16
    )
    start_state = (
        jnp.full((local_heads, token_count), -1e30, jnp.float32),
        jnp.zeros((local_heads, token_count), jnp.float32),
        jnp.zeros((token_count, local_heads, VAL), jnp.float32),
    )
    both = lax.all_gather(
        jnp.concatenate([key_rows, value_rows], axis=1), ("seq", "head"), axis=0, tiled=True
    )
    final_state = attend_pieces(
        queries,
        both[:, :KEY],
        both[:, KEY:],
        start_state,
    )
    running_max, running_sum, weighted = final_state
    attended = (
        (weighted / jnp.transpose(running_sum)[:, :, None])
        .astype(jnp.bfloat16)
        .reshape(token_count, local_heads * VAL)
    )
    projected = lax.psum_scatter(
        lax.dot_general(
            w_out, attended, (((0,), (1,)), ((), ())), preferred_element_type=jnp.float32
        ).astype(jnp.bfloat16),
        "head",
        scatter_dimension=0,
        tiled=True,
    ).astype(jnp.float32)
    mixed = (pooled.astype(jnp.float32) + jnp.transpose(projected)).astype(jnp.bfloat16)[None]
    upstream = cotangent[0]
    gradient = reduced_gradient(upstream, attended)
    return (mixed, gradient)


def solution(mesh):
    sizes = tuple(mesh.shape[axis] for axis in ("head", "seq", "dp"))
    return jax.shard_map(
        section if sizes == (1, SEQ, DP) else local,
        mesh=mesh,
        in_specs=(
            P(("groups", "dp"), "seq", None),
            P(None, None, "head"),
            P("head"),
            P(),
            P(None, "head"),
            P(),
            P(),
            P("head", None),
            P(("groups", "dp"), "seq", None),
        ),
        out_specs=(P(("groups", "dp"), "seq", "head"), P(("groups", "dp"), "head")),
        check_vma=False,
    )
```

```python
import functools
import math

import jax
import jax.numpy as jnp
from jax import lax
from jax.experimental import pallas as pl
from jax.experimental.pallas import tpu as pltpu
import numpy as np
from jax.sharding import PartitionSpec as P

KEY = 128
VAL = 192
KERNEL_TAPS = 3
DILATION_STEP = 2


rope_base = 10000.0
norm_eps = 1e-06


def padded(cells, sides, width):
    for axis, dim in sides:
        count = lax.axis_size(axis)
        ends = count - 1
        head = lax.slice_in_dim(cells, 0, width, axis=dim)
        tail = lax.slice_in_dim(cells, cells.shape[dim] - width, cells.shape[dim], axis=dim)
        cells = jnp.concatenate(
            [
                lax.ppermute(tail, axis, [(i, (i + 1) % count) for i in range(ends)]),
                cells,
                lax.ppermute(head, axis, [((i + 1) % count, i) for i in range(ends)]),
            ],
            axis=dim,
        )
    return cells


def rotate(vectors, positions):
    halfway = vectors.shape[-1] // 2
    frequency = jnp.exp(
        -math.log(rope_base) * 2.0 * jnp.arange(halfway, dtype=jnp.float32) / vectors.shape[-1]
    )
    angles = positions.astype(jnp.float32)[:, None] * frequency[None, :]
    layout = (positions.shape[0],) + (1,) * (vectors.ndim - 2) + (halfway,)
    cosine = jnp.cos(angles).reshape(layout)
    sines = jnp.sin(angles).reshape(layout)
    leading = vectors[..., :halfway]
    trailing = vectors[..., halfway:]
    return jnp.concatenate(
        [leading * cosine - trailing * sines, leading * sines + trailing * cosine], axis=-1
    )


def attend_pieces(queries, key_rows, value_rows, state_in):
    total_keys = key_rows.shape[0]
    block_size = math.gcd(total_keys, 512)

    def one_block(block_index, state):
        running_max, running_sum, weighted = state
        key_block = lax.dynamic_slice_in_dim(key_rows, block_index * block_size, block_size, 0)
        value_block = lax.dynamic_slice_in_dim(value_rows, block_index * block_size, block_size, 0)
        scores = jnp.einsum(
            "thd,ud->htu", queries, key_block, preferred_element_type=jnp.float32
        ) * KEY ** (-0.5)
        new_max = jnp.maximum(running_max, jnp.max(scores, axis=-1))
        rescale = jnp.exp(running_max - new_max)
        weights = jnp.exp(scores - new_max[:, :, None])
        running_sum = running_sum * rescale + jnp.sum(weights, axis=-1)
        weighted = weighted * jnp.transpose(rescale)[:, :, None] + jnp.einsum(
            "htu,uv->thv",
            weights.astype(jnp.bfloat16),
            value_block,
            preferred_element_type=jnp.float32,
        )
        return (new_max, running_sum, weighted)

    return lax.fori_loop(0, total_keys // block_size, one_block, state_in)


def signal_to(sem, where):
    pl.semaphore_signal(sem, inc=1, device_id=where, device_id_type=pl.DeviceIdType.MESH)


def remote(src, dst, send_sem, recv_sem, where):
    return pltpu.make_async_remote_copy(
        src_ref=src,
        dst_ref=dst,
        send_sem=send_sem,
        recv_sem=recv_sem,
        device_id=where,
        device_id_type=pl.DeviceIdType.MESH,
    )


class Plan:
    def __init__(self, tokens, width, columns, dp, seq):
        self.tokens, self.width, self.columns = tokens, width, columns
        self.dp, self.seq = dp, seq
        self.levels = dp.bit_length() - 1
        self.block = width // dp
        self.rows = 64 if self.block % 64 == 0 else self.block
        self.pieces = self.block // self.rows
        self.chunk = 2 * VAL
        self.chunks = columns // self.chunk
        self.units = self.chunks * self.pieces
        self.gap = 4

    def scratch(self):
        tile = (self.rows, self.chunk)
        self.slots = self.gap * self.levels + 1
        shapes = [
            pltpu.VMEM((self.pieces, self.dp * self.rows, self.tokens), jnp.bfloat16),
            pltpu.VMEM((self.chunks, self.tokens, self.chunk), jnp.bfloat16),
            pltpu.VMEM((self.units,) + tile, jnp.float32),
            pltpu.VMEM((self.slots, self.dp * self.rows, self.chunk), jnp.float32),
        ]
        sends = self.levels + 2
        for level in range(self.levels):
            held = self.dp >> (level + 1)
            shapes += [pltpu.VMEM((self.units, held) + tile, jnp.bfloat16)] * 2
        shapes += [pltpu.VMEM((self.units,) + tile, jnp.bfloat16)] * 4
        shapes += [pltpu.SemaphoreType.DMA((self.units,))] * (2 * sends)
        return shapes


def turn_over(plan, cot_ref, cot_t):
    for piece in range(plan.pieces):
        for p in range(plan.dp):
            start = p * plan.block + piece * plan.rows
            cot_t[piece, p * plan.rows : (p + 1) * plan.rows, :] = jnp.transpose(
                cot_ref[:, start : start + plan.rows]
            )


def gradient_loop(plan, refs, out_ref, produce=None, least=0):
    cot_t, att, own, products = refs[:4]
    refs = refs[1:]
    levels, units = plan.levels, plan.units
    pairs = refs[3 : 3 + 2 * levels]
    ahead_out, ahead_in, back_out, back_in = refs[3 + 2 * levels : 7 + 2 * levels]
    sems = refs[7 + 2 * levels :]
    d = lax.axis_index("dp")
    s = lax.axis_index("seq")
    gap = plan.gap
    last = plan.seq - 1

    def summed(unit, p, level):
        start = pl.multiple_of(p * plan.rows, plan.rows)
        value = products[unit % plan.slots, pl.ds(start, plan.rows), :]
        for done in range(level):
            value = value + pairs[2 * done + 1][unit, p // (2 << done)].astype(jnp.float32)
        return value

    def level_copy(unit, level):
        step = 1 << level
        peer = d + (1 - 2 * ((d // step) % 2)) * step
        return remote(
            pairs[2 * level].at[unit],
            pairs[2 * level + 1].at[unit],
            sems[2 * level].at[unit],
            sems[2 * level + 1].at[unit],
            {"dp": peer},
        )

    def ahead_copy(unit):
        at = 2 * levels
        return remote(
            ahead_out.at[unit], ahead_in.at[unit], sems[at].at[unit], sems[at + 1].at[unit],
            {"seq": s + 1},
        )

    def back_copy(unit):
        at = 2 * levels + 2
        return remote(
            back_out.at[unit], back_in.at[unit], sems[at].at[unit], sems[at + 1].at[unit],
            {"seq": s - 1},
        )

    def within(unit):
        return jnp.logical_and(unit >= 0, unit < units)

    def step_at(t, carry):
        if produce is not None:
            produce(t)
        for level in range(levels):
            unit = t - gap * level

            @pl.when(within(unit))
            def _(unit=unit, level=level):
                if level == 0:
                    products[unit % plan.slots] = jnp.dot(
                        cot_t[unit % plan.pieces],
                        att[unit // plan.pieces],
                        preferred_element_type=jnp.float32,
                    )
                else:
                    level_copy(unit, level - 1).wait_recv()
                step = 1 << level
                base = d % step + (1 - (d // step) % 2) * step
                for i in range(plan.dp >> (level + 1)):
                    pairs[2 * level][unit, i] = summed(unit, base + i * 2 * step, level).astype(
                        jnp.bfloat16
                    )
                level_copy(unit, level).start()

        unit = t - gap * levels

        @pl.when(within(unit))
        def _():
            if levels > 0:
                level_copy(unit, levels - 1).wait_recv()
            else:
                products[unit % plan.slots] = jnp.dot(
                    cot_t[unit % plan.pieces],
                    att[unit // plan.pieces],
                    preferred_element_type=jnp.float32,
                )
            own[unit] = summed(unit, d, levels)

        if last > 0:
            fore = t - gap * (levels + s)

            @pl.when(jnp.logical_and(within(fore), s == 0))
            def _():
                ahead_out[fore] = own[fore].astype(jnp.bfloat16)
                ahead_copy(fore).start()

            @pl.when(jnp.logical_and(within(fore), s > 0))
            def _():
                ahead_copy(fore).wait_recv()

                @pl.when(s < last)
                def _():
                    ahead_out[fore] = (own[fore] + ahead_in[fore].astype(jnp.float32)).astype(
                        jnp.bfloat16
                    )
                    ahead_copy(fore).start()

            rear = t - gap * (levels + last - s)

            @pl.when(jnp.logical_and(within(rear), s == last))
            def _():
                back_out[rear] = own[rear].astype(jnp.bfloat16)
                back_copy(rear).start()

            @pl.when(jnp.logical_and(within(rear), s < last))
            def _():
                back_copy(rear).wait_recv()

                @pl.when(s > 0)
                def _():
                    back_out[rear] = (own[rear] + back_in[rear].astype(jnp.float32)).astype(
                        jnp.bfloat16
                    )
                    back_copy(rear).start()

        ready = t - gap * (levels + last)

        def store(value):
            row = pl.multiple_of((ready % plan.pieces) * plan.rows, plan.rows)
            column = pl.multiple_of((ready // plan.pieces) * plan.chunk, plan.chunk)
            out_ref[pl.ds(row, plan.rows), pl.ds(column, plan.chunk)] = value.astype(out_ref.dtype)

        if last == 0:

            @pl.when(within(ready))
            def _():
                store(own[ready])

        else:

            @pl.when(jnp.logical_and(within(ready), s == 0))
            def _():
                store(own[ready] + back_in[ready].astype(jnp.float32))

            @pl.when(jnp.logical_and(within(ready), s == last))
            def _():
                store(own[ready] + ahead_in[ready].astype(jnp.float32))

            if last > 1:

                @pl.when(
                    jnp.logical_and(within(ready), jnp.logical_and(s > 0, s < last))
                )
                def _():
                    store(
                        own[ready]
                        + ahead_in[ready].astype(jnp.float32)
                        + back_in[ready].astype(jnp.float32)
                    )

        return carry

    lax.fori_loop(0, max(least, units + gap * (levels + last)), step_at, 0)

    def drain(unit, carry):
        for level in range(levels):
            level_copy(unit, level).wait_send()
        if last > 0:

            @pl.when(s < last)
            def _():
                ahead_copy(unit).wait_send()

            @pl.when(s > 0)
            def _():
                back_copy(unit).wait_send()

        return carry

    lax.fori_loop(0, units, drain, 0)


def greet(plan):
    barrier = pltpu.get_barrier_semaphore()
    d = lax.axis_index("dp")
    s = lax.axis_index("seq")
    for level in range(plan.levels):
        step = 1 << level
        signal_to(barrier, {"dp": d + (1 - 2 * ((d // step) % 2)) * step})
    if plan.seq > 1:

        @pl.when(s > 0)
        def _():
            signal_to(barrier, {"seq": s - 1})

        @pl.when(s < plan.seq - 1)
        def _():
            signal_to(barrier, {"seq": s + 1})

    if plan.seq == 1:
        pl.semaphore_wait(barrier, plan.levels)
        return
    edge = jnp.logical_or(s == 0, s == plan.seq - 1)

    @pl.when(edge)
    def _():
        pl.semaphore_wait(barrier, plan.levels + 1)

    @pl.when(jnp.logical_not(edge))
    def _():
        pl.semaphore_wait(barrier, plan.levels + 2)


def gradient_kernel(plan, cot_ref, att_ref, out_ref, *refs):
    greet(plan)
    turn_over(plan, cot_ref, refs[0])
    for c in range(plan.chunks):
        refs[1][c] = att_ref[:, c * plan.chunk : (c + 1) * plan.chunk]
    gradient_loop(plan, refs, out_ref)


def reduced_gradient(upstream, attended):
    plan = Plan(
        upstream.shape[0], upstream.shape[1], attended.shape[1],
        lax.axis_size("dp"), lax.axis_size("seq"),
    )
    whole = pl.BlockSpec(memory_space=pltpu.VMEM)
    return pl.pallas_call(
        functools.partial(gradient_kernel, plan),
        out_shape=jax.ShapeDtypeStruct((plan.block, plan.columns), jnp.float32),
        in_specs=[whole, whole],
        out_specs=whole,
        scratch_shapes=plan.scratch(),
        compiler_params=pltpu.CompilerParams(
            collective_id=0, has_side_effects=True, vmem_limit_bytes=56 * 2**20
        ),
        name="reduced_gradient",
    )(upstream, attended)


EDGE = 16
TILE = 512
LANES = 128
DP = 4
SEQ = 4
HOLD = 256
SPLIT = 3
GAP = 5
TURNS = 20


def section_kernel(*refs):
    (x_hbm, conv_hbm, bias_in, gain_in, query_hbm, key_hbm, value_hbm, out_hbm, cot_hbm, turn_hbm) = refs[:10]
    mixed, grad_out = refs[10:12]
    (
        x_rows, conv_w, query_w, key_w, value_w, out_w, turn, fetched,
        edges, edge_sems, spread, stacked, pooled, normed, queries,
        kv, kv_send, kv_recv, values, peaks, sums, bias, gain,
        cot_in, cot_t, cot_sems, att_rows, att, att_sems, own,
        ahead_out, ahead_in, back_out, back_in, line_sems, cross,
    ) = refs[12:]
    rows, channels = x_rows.shape
    tokens, width = pooled.shape
    tiles, blocks = width // TILE, channels // LANES
    half, quarter = tokens // 2, tokens // 4
    heads = queries.shape[0]
    part_rows = width // DP
    strips = att.shape[0]
    taps = KERNEL_TAPS
    d = lax.axis_index("dp")
    s = lax.axis_index("seq")
    mate = d + 1 - 2 * (d % 2)
    across = d + 2 - 4 * (d // 2)
    opposite = 3 - d
    far = 3 - s
    upper = s // 2
    end = jnp.logical_or(s == 0, s == SEQ - 1)
    inner = jnp.logical_not(end)

    pieces = ((0, quarter, half), (half, 0, quarter), (half + quarter, half + quarter, quarter))

    def conv_fetch(n):
        return pltpu.make_async_copy(
            conv_hbm.at[:, pl.ds(pl.multiple_of(n * TILE, TILE), TILE)],
            conv_w.at[n],
            fetched.at[6 + n],
        )

    def turn_fetch(i):
        to, at, count = pieces[i]
        return pltpu.make_async_copy(
            turn_hbm.at[pl.ds(pl.multiple_of(s * tokens + at, quarter), count)],
            turn.at[pl.ds(to, count)],
            fetched.at[5],
        )

    turn_whole = pltpu.make_async_copy(turn_hbm.at[pl.ds(0, tokens)], turn, fetched.at[5])

    x_fetch = pltpu.make_async_copy(x_hbm, x_rows, fetched.at[0])
    key_fetch = pltpu.make_async_copy(key_hbm, key_w, fetched.at[1])
    value_fetch = pltpu.make_async_copy(value_hbm, value_w, fetched.at[2])
    query_fetch = pltpu.make_async_copy(query_hbm, query_w, fetched.at[3])
    out_fetch = pltpu.make_async_copy(out_hbm, out_w, fetched.at[4])

    def cot_columns(owner):
        start = pl.multiple_of(owner * part_rows, part_rows)
        return cot_hbm.at[:, pl.ds(start, part_rows)]

    cot_local = tuple(
        pltpu.make_async_copy(cot_columns(block), cot_in.at[slot], cot_sems.at[slot])
        for slot, block in ((1, d), (4, across))
    )

    def cot_copy(slot):
        columns = {0: across, 2: mate, 3: opposite, 5: opposite}[slot]
        peer = mate if slot == 5 else columns
        return remote(
            cot_columns(columns), cot_in.at[slot], cot_sems.at[6], cot_sems.at[slot],
            {"dp": peer},
        )

    x_fetch.start()
    for n in range(tiles):
        conv_fetch(n).start()
    key_fetch.start()
    value_fetch.start()
    for i in range(3):
        turn_fetch(i).start()

    barrier = pltpu.get_barrier_semaphore()
    for peer in (mate, across, opposite):
        signal_to(barrier, {"dp": peer})

    @pl.when(s > 0)
    def _():
        signal_to(barrier, {"seq": s - 1})

    @pl.when(s < SEQ - 1)
    def _():
        signal_to(barrier, {"seq": s + 1})

    @pl.when(end)
    def _():
        signal_to(barrier, {"seq": far})

    bias[...] = bias_in[...].reshape(bias.shape)
    gain[...] = gain_in[...].reshape(gain.shape)

    def edge_ahead():
        return remote(
            x_hbm.at[pl.ds(rows - EDGE, EDGE)], edges.at[0], edge_sems.at[0], edge_sems.at[1],
            {"seq": s + 1},
        )

    def edge_back():
        return remote(
            x_hbm.at[pl.ds(0, EDGE)], edges.at[1], edge_sems.at[2], edge_sems.at[3],
            {"seq": s - 1},
        )

    x_fetch.wait()
    query_fetch.start()
    for j in range(blocks):
        spread[j, EDGE : EDGE + rows, :] = x_rows[:, j * LANES : (j + 1) * LANES].astype(
            jnp.float32
        )
    blank = jnp.zeros((EDGE, LANES), jnp.float32)
    for j in range(blocks):
        spread[j, :EDGE, :] = blank
        spread[j, EDGE + rows :, :] = blank

    def stack(tap, to, first, count):
        for parity in range(2):
            for j in range(blocks):
                start = EDGE + parity + DILATION_STEP * (tap - 1) + 2 * first
                lane = tap * channels + j * LANES
                row = 2 * half * (to // half) + parity * half + to % half
                stacked[row : row + count, lane : lane + LANES] = spread[
                    j, pl.ds(start, count, stride=2), :
                ].astype(jnp.bfloat16)

    for tap in range(taps):
        for piece in pieces:
            stack(tap, *piece)

    pl.semaphore_wait(barrier, 5)

    @pl.when(s < SEQ - 1)
    def _():
        edge_ahead().start()

    @pl.when(s > 0)
    def _():
        edge_back().start()

    for slot in (0, 2, 3, 5):
        cot_copy(slot).start()
    for copy in cot_local:
        copy.start()
    out_fetch.start()

    def put_edge(which, start, tap, to, first):
        (edge_ahead if which == 0 else edge_back)().wait_recv()
        for j in range(blocks):
            spread[j, start : start + EDGE, :] = edges[
                which, :, j * LANES : (j + 1) * LANES
            ].astype(jnp.float32)
        stack(tap, to, first, EDGE)

    def turned(vectors, first, count):
        return (
            vectors * turn[pl.ds(first, count), :KEY]
            + pltpu.roll(vectors, KEY // 2, 1) * turn[pl.ds(first, count), KEY:]
        ).astype(jnp.bfloat16)

    def kv_copy(owner, part, piece, sem, where):
        span = pl.ds(0, half) if piece == 0 else pl.ds(half, half + quarter)
        block = kv.at[owner, part, span]
        return remote(
            block, block, kv_send.at[sem], kv_recv.at[(owner * 2 + part) * 2 + piece],
            {"seq": where},
        )

    def kv_own(part):
        for piece in range(2):

            @pl.when(s > 0)
            def _():
                kv_copy(s, part, piece, 0, s - 1).start()

            @pl.when(s < SEQ - 1)
            def _():
                kv_copy(s, part, piece, 0, s + 1).start()

            @pl.when(end)
            def _():
                kv_copy(s, part, piece, 0, far).start()

    def kv_relay(part):
        for piece in range(2):
            kv_copy(s - 1, part, piece, 1, s + 1).wait_recv()
            kv_copy(s - 1, part, piece, 1, s + 1).start()
            kv_copy(s + 1, part, piece, 1, s - 1).wait_recv()
            kv_copy(s + 1, part, piece, 1, s - 1).start()

    def conv_pass(part, carry):
        first = part == 0
        base = pl.multiple_of(part * half, half)
        here = pl.ds(base, half)

        @pl.when(jnp.logical_and(part == 1, s > 0))
        def _():
            put_edge(0, 0, 0, half, 0)

        @pl.when(jnp.logical_and(part == 1, s < SEQ - 1))
        def _():
            put_edge(1, EDGE + rows, taps - 1, tokens - EDGE, tokens - EDGE)

        def conv_tile(n, carry):
            @pl.when(first)
            def _():
                conv_fetch(n).wait()

            columns = pl.ds(pl.multiple_of(n * TILE, TILE), TILE)
            pre = (
                jnp.dot(
                    stacked[pl.ds(pl.multiple_of(part * tokens, tokens), tokens), :],
                    conv_w[n],
                    preferred_element_type=jnp.float32,
                )
                + bias[:, columns]
            )
            root = math.sqrt(2.0 / math.pi)
            inside = pre * (root + (root * 0.044715) * (pre * pre))
            activated = pre * (0.5 + 0.5 * jnp.tanh(inside))
            pooled[here, columns] = jnp.maximum(activated[:half], activated[half:]).astype(
                jnp.bfloat16
            )
            return carry

        lax.fori_loop(0, tiles, conv_tile, 0)

        count = 32

        def norm_part(i, carry):
            few = pl.ds(pl.multiple_of(base + i * count, count), count)
            wide = pooled[few, :].astype(jnp.float32)
            squares = jnp.mean(wide * wide, axis=-1, keepdims=True)
            normed[few, :] = (wide * lax.rsqrt(squares + norm_eps) * gain[...]).astype(
                jnp.bfloat16
            )
            return carry

        lax.fori_loop(0, half // count, norm_part, 0)

        @pl.when(first)
        def _():
            key_fetch.wait()
            value_fetch.wait()
            turn_whole.wait()

        ready = normed[here, :]
        kv[s, part, :half, :] = turned(
            jnp.dot(ready, key_w[...], preferred_element_type=jnp.float32), base, half
        )
        own_values = lax.dot_general(
            ready, value_w[...], (((1,), (1,)), ((), ())), preferred_element_type=jnp.float32
        )
        kv[s, part, half : 2 * half, :] = own_values[:, :LANES].astype(jnp.bfloat16)
        kv[s, part, 2 * half :, :] = jnp.concatenate(
            [own_values[:quarter, LANES:], own_values[quarter:, LANES:]], axis=1
        ).astype(jnp.bfloat16)
        kv_own(part)
        return carry

    lax.fori_loop(0, 2, conv_pass, 0)

    @pl.when(inner)
    def _():
        kv_relay(0)

    query_fetch.wait()

    def query_pair(c, carry):
        pair = jnp.dot(
            normed[...],
            query_w[:, pl.ds(pl.multiple_of(c * 2 * KEY, 2 * KEY), 2 * KEY)],
            preferred_element_type=jnp.float32,
        )
        queries[2 * c] = turned(pair[:, :KEY], 0, tokens)
        queries[2 * c + 1] = turned(pair[:, KEY:], 0, tokens)
        return carry

    lax.fori_loop(0, heads // 2, query_pair, 0)

    def turn_over(slot):
        if slot in (1, 4):
            cot_local[slot // 4].wait()
        else:
            cot_copy(slot).wait_recv()
        middle = cot_in[slot, quarter : quarter + half, :]
        outer = jnp.concatenate(
            [cot_in[slot, :quarter, :], cot_in[slot, quarter + half :, :]], axis=0
        )
        at = slot * tokens
        cot_t[:, at : at + half] = jnp.transpose(middle)
        cot_t[:, at + half : at + tokens] = jnp.transpose(outer)

    def owner_of(k):
        low = s + upper * (3 - 2 * s)
        at = (k + low) % 2 if k < 2 else (k - 2 + 1 - low) % 2 + 2
        return at + upper * (3 - 2 * at)

    side = lax.broadcasted_iota(jnp.int32, (half, LANES), 1)

    def unpack(owner):
        for part in range(2):
            at = part * half
            values[at : at + half, :LANES] = kv[owner, part, half : 2 * half, :]
            rest = kv[owner, part, 2 * half :, :]
            rest = jnp.concatenate(
                [rest, pltpu.roll(rest.astype(jnp.float32), LANES // 2, 1).astype(jnp.bfloat16)],
                axis=0,
            ).astype(jnp.float32)
            rest = jnp.where(
                side < VAL - LANES, rest, jnp.where(side == VAL - LANES, 1.0, 0.0)
            )
            values[at : at + half, LANES:] = rest.astype(jnp.bfloat16)

    factor = KEY ** (-0.5) * math.log2(math.e)

    def twice(column):
        return jnp.concatenate([column, column], axis=1)

    def attend(h, keys, first):
        scores = lax.dot_general(
            queries[h], keys, (((1,), (1,)), ((), ())), preferred_element_type=jnp.float32
        )
        peak = jnp.max(scores, axis=-1, keepdims=True)
        if first:
            peak = jnp.broadcast_to(peak, (tokens, LANES))
        else:
            before = peaks[h]
            peak = jnp.maximum(before, peak)
        weights = jnp.exp2((scores - twice(peak)) * factor).astype(jnp.bfloat16)
        total = jnp.dot(weights, values[...], preferred_element_type=jnp.float32)
        if not first:
            total = total + sums[h] * twice(jnp.exp2((before - peak) * factor))
        return peak, total

    def keys_of(owner):
        return kv[owner, :, :half, :].reshape(tokens, KEY)

    def attend_block(k):
        owner = owner_of(k)
        unpack(owner)

        def pair(c, carry):
            for h in (2 * c, 2 * c + 1):
                peak, total = attend(h, keys_of(owner), k == 0)
                peaks[h] = peak
                sums[h] = total
            return carry

        lax.fori_loop(0, heads // 2, pair, 0)

    def wait_block(k):
        owner = owner_of(k)
        for part in range(2):
            for piece in range(2):
                kv_copy(owner, part, piece, 0, far).wait_recv()

    def att_copy(kind, b):
        slot = (1, 1, 0)[kind]
        to = (2, 0, 3)[kind]
        arrived = strips + b if kind == 1 else b
        return remote(
            att.at[b, slot], att.at[b, to], att_sems.at[2 * strips + kind], att_sems.at[arrived],
            {"dp": across if kind == 1 else mate},
        )

    def mate_strips(b):
        both = att.at[b, pl.ds(2, 2)]
        return remote(both, both, att_sems.at[2 * strips], att_sems.at[b], {"dp": mate})

    attend_block(0)

    @pl.when(inner)
    def _():
        kv_relay(1)

    for slot in range(6):
        turn_over(slot)

    @pl.when(end)
    def _():
        wait_block(1)

    attend_block(1)

    @pl.when(end)
    def _():
        wait_block(2)

    attend_block(2)
    wait_block(3)
    last_owner = owner_of(3)
    unpack(last_owner)
    chunk = 2 * VAL
    each = chunk // LANES

    def last_pair(c):
        done = []
        for h in (2 * c, 2 * c + 1):
            _, total = attend(h, keys_of(last_owner), False)
            done.append(total[:, :VAL] / total[:, VAL : VAL + 1])
        both = jnp.concatenate(done, axis=1).astype(jnp.bfloat16)
        for i in range(each):
            b = c * each + i
            att[b, 1] = both[:, i * LANES : (i + 1) * LANES]
            att_copy(0, b).start()

            @pl.when(b > 0)
            def _(b=b):
                att_copy(1, b).start()

        att_rows[:, pl.ds(pl.multiple_of(c * chunk, LANES), chunk)] = both

    def mixed_tile(n):
        columns = pl.ds(pl.multiple_of(n * TILE, TILE), TILE)
        total = pooled[:, columns].astype(jnp.float32) + jnp.dot(
            att_rows[...], out_w[:, columns], preferred_element_type=jnp.float32
        )
        total = total.astype(jnp.bfloat16)
        for at, to, count in pieces:
            mixed[to : to + count, columns] = total[at : at + count]

    out_fetch.wait()

    count = strips + 1
    size = part_rows // SPLIT
    units = count * SPLIT
    last = SEQ - 1

    def place(unit):
        return unit // SPLIT, unit % SPLIT

    def ahead_copy(unit):
        at = place(unit)
        return remote(
            ahead_out.at[at], ahead_in.at[at], line_sems.at[2 * TURNS], line_sems.at[unit % TURNS],
            {"seq": s + 1},
        )

    def back_copy(unit):
        at = place(unit)
        return remote(
            back_out.at[at], back_in.at[at], line_sems.at[2 * TURNS + 1],
            line_sems.at[TURNS + unit % TURNS], {"seq": s - 1},
        )

    def within(unit):
        return jnp.logical_and(unit >= 0, unit < units)

    def cross_copy():
        return remote(
            cross.at[0], cross.at[1], line_sems.at[2 * TURNS + 2], line_sems.at[2 * TURNS + 3],
            {"dp": across},
        )

    def step_at(step, carry):
        t = step - 1

        @pl.when(t == 0)
        def _():
            att_copy(0, 0).wait_recv()
            near = att[0, 1:3].reshape(2 * tokens, LANES)
            for i, at in enumerate((1, 4)):
                own[i] = jnp.dot(
                    cot_t[:, at * tokens : (at + 2) * tokens],
                    near,
                    preferred_element_type=jnp.float32,
                ).reshape(own.shape[1:])

        @pl.when(jnp.logical_and(jnp.logical_and(t >= 2 * SPLIT, t < units), t % SPLIT == 0))
        def _():
            q = t // SPLIT
            mate_strips(q - 1).wait_recv()
            own[q] = jnp.dot(
                cot_t[:, : DP * tokens],
                att[q - 1].reshape(DP * tokens, LANES),
                preferred_element_type=jnp.float32,
            ).reshape(own.shape[1:])

        fore = t - GAP * s

        @pl.when(jnp.logical_and(within(fore), s == 0))
        def _():
            ahead_out[place(fore)] = own[place(fore)].astype(jnp.bfloat16)
            ahead_copy(fore).start()

        @pl.when(jnp.logical_and(within(fore), s > 0))
        def _():
            ahead_copy(fore).wait_recv()

            @pl.when(s < last)
            def _():
                ahead_out[place(fore)] = (
                    own[place(fore)] + ahead_in[place(fore)].astype(jnp.float32)
                ).astype(jnp.bfloat16)
                ahead_copy(fore).start()

        rear = t - GAP * (last - s)

        @pl.when(jnp.logical_and(within(rear), s == last))
        def _():
            back_out[place(rear)] = own[place(rear)].astype(jnp.bfloat16)
            back_copy(rear).start()

        @pl.when(jnp.logical_and(within(rear), s < last))
        def _():
            back_copy(rear).wait_recv()

            @pl.when(s > 0)
            def _():
                back_out[place(rear)] = (
                    own[place(rear)] + back_in[place(rear)].astype(jnp.float32)
                ).astype(jnp.bfloat16)
                back_copy(rear).start()

        ready = t - GAP * last

        def store(value):
            q, i = place(ready)
            row = pl.multiple_of(i * size, size)

            @pl.when(q == 1)
            def _():
                cross[0, pl.ds(row, size), :] = value.astype(cross.dtype)

            @pl.when(q == 0)
            def _():
                grad_out[pl.ds(row, size), :LANES] = value

            @pl.when(q > 1)
            def _():
                column = pl.multiple_of((q - 1) * LANES, LANES)
                grad_out[pl.ds(row, size), pl.ds(column, LANES)] = value

        @pl.when(jnp.logical_and(within(ready), s == 0))
        def _():
            store(own[place(ready)] + back_in[place(ready)].astype(jnp.float32))

        @pl.when(jnp.logical_and(within(ready), s == last))
        def _():
            store(own[place(ready)] + ahead_in[place(ready)].astype(jnp.float32))

        @pl.when(jnp.logical_and(within(ready), inner))
        def _():
            store(
                own[place(ready)]
                + ahead_in[place(ready)].astype(jnp.float32)
                + back_in[place(ready)].astype(jnp.float32)
            )

        @pl.when(ready == 2 * SPLIT - 1)
        def _():
            cross_copy().start()

        @pl.when(jnp.logical_and(step < heads, step % 2 == 0))
        def _():
            last_pair(step // 2)

        @pl.when(
            jnp.logical_and(
                jnp.logical_and(t >= SPLIT, t < strips * SPLIT), t % SPLIT == 0
            )
        )
        def _():
            b = t // SPLIT
            att_copy(1, b).wait_recv()
            att_copy(2, b).start()

        tile = t - 4 * SPLIT

        @pl.when(
            jnp.logical_and(jnp.logical_and(tile >= 0, tile < 2 * tiles), tile % 2 == 0)
        )
        def _():
            mixed_tile(tile // 2)

        return carry

    lax.fori_loop(0, units + GAP * last + 1, step_at, 0)
    cross_copy().wait_recv()
    grad_out[:, :LANES] = grad_out[:, :LANES] + cross[1].astype(jnp.float32)
    cross_copy().wait_send()

    @pl.when(s < last)
    def _():
        remote(
            ahead_out, ahead_in, line_sems.at[2 * TURNS], line_sems.at[0], {"seq": s + 1}
        ).wait_send()

    @pl.when(s > 0)
    def _():
        remote(
            back_out, back_in, line_sems.at[2 * TURNS + 1], line_sems.at[0], {"seq": s - 1}
        ).wait_send()

    for kind in range(3):
        sent = att.at[:, 0] if kind == 0 else att.at[pl.ds(1, strips - 1), 0]
        remote(
            sent, sent, att_sems.at[2 * strips + kind], att_sems.at[0], {"dp": mate}
        ).wait_send()
    pair_of = kv.at[pl.ds(0, 2)]
    remote(pair_of, pair_of, kv_send.at[0], kv_recv.at[0], {"seq": far}).wait_send()

    @pl.when(inner)
    def _():
        remote(pair_of, pair_of, kv_send.at[1], kv_recv.at[0], {"seq": far}).wait_send()

    others = cot_in.at[pl.ds(0, 4)]
    remote(others, others, cot_sems.at[6], cot_sems.at[0], {"dp": mate}).wait_send()

    @pl.when(s < SEQ - 1)
    def _():
        edge_ahead().wait_send()

    @pl.when(s > 0)
    def _():
        edge_back().wait_send()


def turn_table(count):
    frequency = np.exp(
        np.float32(-math.log(rope_base) * 2.0) * np.arange(KEY // 2, dtype=np.float32) / KEY
    ).astype(np.float32)
    angles = np.arange(count, dtype=np.float32)[:, None] * frequency[None, :]
    cosine, sines = np.cos(angles), np.sin(angles)
    return np.concatenate([cosine, cosine, -sines, sines], axis=1).astype(np.float32)


def finish_kernel(mixed_in, grad_in, mixed, grad, sems):
    copies = (
        pltpu.make_async_copy(grad_in, grad, sems.at[0]),
        pltpu.make_async_copy(mixed_in, mixed, sems.at[1]),
    )
    for copy in copies:
        copy.start()
    for copy in copies:
        copy.wait()


def finish(mixed, gradient):
    away = pl.BlockSpec(memory_space=pl.ANY)
    return pl.pallas_call(
        finish_kernel,
        out_shape=(
            jax.ShapeDtypeStruct(mixed.shape, mixed.dtype),
            jax.ShapeDtypeStruct(gradient.shape, gradient.dtype),
        ),
        in_specs=[pl.BlockSpec(memory_space=pltpu.VMEM)] * 2,
        out_specs=(away, away),
        scratch_shapes=[pltpu.SemaphoreType.DMA((2,))],
        name="finish",
    )(
        pltpu.with_memory_space_constraint(mixed, pltpu.VMEM),
        pltpu.with_memory_space_constraint(gradient, pltpu.VMEM),
    )


def section(x_in, kernel_weight, conv_bias, norm_gain, w_query, w_key, w_value, w_out, cotangent):
    inputs, upstream = x_in[0], cotangent[0]
    rows, channels = inputs.shape
    width, columns = kernel_weight.shape[2], w_out.shape[0]
    tokens, tiles, strips = rows // 2, width // TILE, columns // LANES
    heads, part_rows = w_query.shape[1] // KEY, width // DP
    depth = KERNEL_TAPS * channels
    bf, f32 = jnp.bfloat16, jnp.float32
    line = pltpu.VMEM((strips + 1, SPLIT, part_rows // SPLIT, LANES), bf)
    held = pl.BlockSpec(memory_space=pltpu.VMEM)
    away = pl.BlockSpec(memory_space=pl.ANY)
    mixed, gradient = pl.pallas_call(
        section_kernel,
        out_shape=(
            pltpu.VMEM((tokens, width), bf),
            pltpu.VMEM((part_rows, columns), f32),
        ),
        in_specs=[away, away, held, held, away, away, away, away, away, away],
        out_specs=(held, held),
        scratch_shapes=[
            pltpu.VMEM((rows, channels), bf),
            pltpu.VMEM((tiles, depth, TILE), bf),
            pltpu.VMEM(w_query.shape, bf),
            pltpu.VMEM(w_key.shape, bf),
            pltpu.VMEM(w_value.shape[::-1], bf),
            pltpu.VMEM(w_out.shape, bf),
            pltpu.VMEM((tokens, 2 * KEY), f32),
            pltpu.SemaphoreType.DMA((6 + tiles,)),
            pltpu.VMEM((2, EDGE, channels), bf),
            pltpu.SemaphoreType.DMA((4,)),
            pltpu.VMEM((channels // LANES, rows + 2 * EDGE, LANES), f32),
            pltpu.VMEM((rows, depth), bf),
            pltpu.VMEM((tokens, width), bf),
            pltpu.VMEM((tokens, width), bf),
            pltpu.VMEM((heads, tokens, KEY), bf),
            pltpu.VMEM((SEQ, 2, 5 * tokens // 4, KEY), bf),
            pltpu.SemaphoreType.DMA((2,)),
            pltpu.SemaphoreType.DMA((4 * SEQ,)),
            pltpu.VMEM((tokens, HOLD), bf),
            pltpu.VMEM((heads, tokens, LANES), f32),
            pltpu.VMEM((heads, tokens, HOLD), f32),
            pltpu.VMEM((1, width), f32),
            pltpu.VMEM((1, width), f32),
            pltpu.VMEM((6, tokens, part_rows), bf),
            pltpu.VMEM((part_rows, 6 * tokens), bf),
            pltpu.SemaphoreType.DMA((7,)),
            pltpu.VMEM((tokens, columns), bf),
            pltpu.VMEM((strips, DP, tokens, LANES), bf),
            pltpu.SemaphoreType.DMA((2 * strips + 3,)),
            pltpu.VMEM((strips + 1, SPLIT, part_rows // SPLIT, LANES), f32),
            line, line, line, line,
            pltpu.SemaphoreType.DMA((2 * TURNS + 4,)),
            pltpu.VMEM((2, part_rows, LANES), bf),
        ],
        compiler_params=pltpu.CompilerParams(
            collective_id=1, has_side_effects=True, vmem_limit_bytes=54 * 2**20
        ),
        name="section",
    )(
        inputs,
        kernel_weight.reshape(depth, width),
        conv_bias,
        norm_gain,
        w_query,
        w_key,
        jnp.transpose(w_value),
        w_out,
        upstream,
        turn_table(tokens * SEQ),
    )
    mixed, gradient = finish(mixed, gradient)
    return mixed[None], gradient


def local(x_in, kernel_weight, conv_bias, norm_gain, w_query, w_key, w_value, w_out, cotangent):
    inputs = x_in[0]
    edge_padding = DILATION_STEP * (KERNEL_TAPS - 1) // 2
    padded_rows = padded(inputs, (("seq", 0),), edge_padding)
    padded_row_count = inputs.shape[0]
    before_activation = jnp.broadcast_to(
        conv_bias[None, :], (padded_row_count, kernel_weight.shape[2])
    )
    for kernel_tap_index in range(KERNEL_TAPS):
        before_activation = before_activation + jnp.dot(
            padded_rows[
                kernel_tap_index * DILATION_STEP : kernel_tap_index * DILATION_STEP
                + padded_row_count
            ],
            kernel_weight[kernel_tap_index],
            preferred_element_type=jnp.float32,
        )
    activated = jax.nn.gelu(before_activation)
    pooled = jnp.max(activated.reshape(padded_row_count // 2, 2, -1), axis=1).astype(jnp.bfloat16)
    token_count = pooled.shape[0]
    features = lax.all_gather(pooled, "head", axis=1, tiled=True)
    widened = features.astype(jnp.float32)
    squares = jnp.mean(widened * widened, axis=-1, keepdims=True)
    normed = (widened * lax.rsqrt(squares + norm_eps) * norm_gain).astype(jnp.bfloat16)
    seq_offset = lax.axis_index("seq") * token_count
    positions = seq_offset + jnp.arange(token_count, dtype=jnp.int32)
    local_heads = w_query.shape[1] // KEY
    queries = rotate(
        jnp.dot(normed, w_query, preferred_element_type=jnp.float32).reshape(
            token_count, local_heads, KEY
        ),
        positions,
    ).astype(jnp.bfloat16)
    own_rows = token_count // lax.axis_size("head")
    row_offset = lax.axis_index("head") * own_rows
    own_normed = lax.dynamic_slice_in_dim(normed, row_offset, own_rows, 0)
    own_positions = seq_offset + row_offset + jnp.arange(own_rows, dtype=jnp.int32)
    key_rows = rotate(
        jnp.dot(own_normed, w_key, preferred_element_type=jnp.float32), own_positions
    ).astype(jnp.bfloat16)
    value_rows = jnp.dot(own_normed, w_value, preferred_element_type=jnp.float32).astype(
        jnp.bfloat16
    )
    start_state = (
        jnp.full((local_heads, token_count), -1e30, jnp.float32),
        jnp.zeros((local_heads, token_count), jnp.float32),
        jnp.zeros((token_count, local_heads, VAL), jnp.float32),
    )
    both = lax.all_gather(
        jnp.concatenate([key_rows, value_rows], axis=1), ("seq", "head"), axis=0, tiled=True
    )
    final_state = attend_pieces(
        queries,
        both[:, :KEY],
        both[:, KEY:],
        start_state,
    )
    running_max, running_sum, weighted = final_state
    attended = (
        (weighted / jnp.transpose(running_sum)[:, :, None])
        .astype(jnp.bfloat16)
        .reshape(token_count, local_heads * VAL)
    )
    projected = lax.psum_scatter(
        lax.dot_general(
            w_out, attended, (((0,), (1,)), ((), ())), preferred_element_type=jnp.float32
        ).astype(jnp.bfloat16),
        "head",
        scatter_dimension=0,
        tiled=True,
    ).astype(jnp.float32)
    mixed = (pooled.astype(jnp.float32) + jnp.transpose(projected)).astype(jnp.bfloat16)[None]
    upstream = cotangent[0]
    gradient = reduced_gradient(upstream, attended)
    return (mixed, gradient)


def solution(mesh):
    sizes = tuple(mesh.shape[axis] for axis in ("head", "seq", "dp"))
    return jax.shard_map(
        section if sizes == (1, SEQ, DP) else local,
        mesh=mesh,
        in_specs=(
            P(("groups", "dp"), "seq", None),
            P(None, None, "head"),
            P("head"),
            P(),
            P(None, "head"),
            P(),
            P(),
            P("head", None),
            P(("groups", "dp"), "seq", None),
        ),
        out_specs=(P(("groups", "dp"), "seq", "head"), P(("groups", "dp"), "head")),
        check_vma=False,
    )
```

```python
import functools
import math

import jax
import jax.numpy as jnp
from jax import lax
from jax.experimental import pallas as pl
from jax.experimental.pallas import tpu as pltpu
import numpy as np
from jax.sharding import PartitionSpec as P

KEY = 128
VAL = 192
KERNEL_TAPS = 3
DILATION_STEP = 2


rope_base = 10000.0
norm_eps = 1e-06


def padded(cells, sides, width):
    for axis, dim in sides:
        count = lax.axis_size(axis)
        ends = count - 1
        head = lax.slice_in_dim(cells, 0, width, axis=dim)
        tail = lax.slice_in_dim(cells, cells.shape[dim] - width, cells.shape[dim], axis=dim)
        cells = jnp.concatenate(
            [
                lax.ppermute(tail, axis, [(i, (i + 1) % count) for i in range(ends)]),
                cells,
                lax.ppermute(head, axis, [((i + 1) % count, i) for i in range(ends)]),
            ],
            axis=dim,
        )
    return cells


def rotate(vectors, positions):
    halfway = vectors.shape[-1] // 2
    frequency = jnp.exp(
        -math.log(rope_base) * 2.0 * jnp.arange(halfway, dtype=jnp.float32) / vectors.shape[-1]
    )
    angles = positions.astype(jnp.float32)[:, None] * frequency[None, :]
    layout = (positions.shape[0],) + (1,) * (vectors.ndim - 2) + (halfway,)
    cosine = jnp.cos(angles).reshape(layout)
    sines = jnp.sin(angles).reshape(layout)
    leading = vectors[..., :halfway]
    trailing = vectors[..., halfway:]
    return jnp.concatenate(
        [leading * cosine - trailing * sines, leading * sines + trailing * cosine], axis=-1
    )


def attend_pieces(queries, key_rows, value_rows, state_in):
    total_keys = key_rows.shape[0]
    block_size = math.gcd(total_keys, 512)

    def one_block(block_index, state):
        running_max, running_sum, weighted = state
        key_block = lax.dynamic_slice_in_dim(key_rows, block_index * block_size, block_size, 0)
        value_block = lax.dynamic_slice_in_dim(value_rows, block_index * block_size, block_size, 0)
        scores = jnp.einsum(
            "thd,ud->htu", queries, key_block, preferred_element_type=jnp.float32
        ) * KEY ** (-0.5)
        new_max = jnp.maximum(running_max, jnp.max(scores, axis=-1))
        rescale = jnp.exp(running_max - new_max)
        weights = jnp.exp(scores - new_max[:, :, None])
        running_sum = running_sum * rescale + jnp.sum(weights, axis=-1)
        weighted = weighted * jnp.transpose(rescale)[:, :, None] + jnp.einsum(
            "htu,uv->thv",
            weights.astype(jnp.bfloat16),
            value_block,
            preferred_element_type=jnp.float32,
        )
        return (new_max, running_sum, weighted)

    return lax.fori_loop(0, total_keys // block_size, one_block, state_in)


def signal_to(sem, where):
    pl.semaphore_signal(sem, inc=1, device_id=where, device_id_type=pl.DeviceIdType.MESH)


def remote(src, dst, send_sem, recv_sem, where):
    return pltpu.make_async_remote_copy(
        src_ref=src,
        dst_ref=dst,
        send_sem=send_sem,
        recv_sem=recv_sem,
        device_id=where,
        device_id_type=pl.DeviceIdType.MESH,
    )


class Plan:
    def __init__(self, tokens, width, columns, dp, seq):
        self.tokens, self.width, self.columns = tokens, width, columns
        self.dp, self.seq = dp, seq
        self.levels = dp.bit_length() - 1
        self.block = width // dp
        self.rows = 64 if self.block % 64 == 0 else self.block
        self.pieces = self.block // self.rows
        self.chunk = 2 * VAL
        self.chunks = columns // self.chunk
        self.units = self.chunks * self.pieces
        self.gap = 4

    def scratch(self):
        tile = (self.rows, self.chunk)
        self.slots = self.gap * self.levels + 1
        shapes = [
            pltpu.VMEM((self.pieces, self.dp * self.rows, self.tokens), jnp.bfloat16),
            pltpu.VMEM((self.chunks, self.tokens, self.chunk), jnp.bfloat16),
            pltpu.VMEM((self.units,) + tile, jnp.float32),
            pltpu.VMEM((self.slots, self.dp * self.rows, self.chunk), jnp.float32),
        ]
        sends = self.levels + 2
        for level in range(self.levels):
            held = self.dp >> (level + 1)
            shapes += [pltpu.VMEM((self.units, held) + tile, jnp.bfloat16)] * 2
        shapes += [pltpu.VMEM((self.units,) + tile, jnp.bfloat16)] * 4
        shapes += [pltpu.SemaphoreType.DMA((self.units,))] * (2 * sends)
        return shapes


def turn_over(plan, cot_ref, cot_t):
    for piece in range(plan.pieces):
        for p in range(plan.dp):
            start = p * plan.block + piece * plan.rows
            cot_t[piece, p * plan.rows : (p + 1) * plan.rows, :] = jnp.transpose(
                cot_ref[:, start : start + plan.rows]
            )


def gradient_loop(plan, refs, out_ref, produce=None, least=0):
    cot_t, att, own, products = refs[:4]
    refs = refs[1:]
    levels, units = plan.levels, plan.units
    pairs = refs[3 : 3 + 2 * levels]
    ahead_out, ahead_in, back_out, back_in = refs[3 + 2 * levels : 7 + 2 * levels]
    sems = refs[7 + 2 * levels :]
    d = lax.axis_index("dp")
    s = lax.axis_index("seq")
    gap = plan.gap
    last = plan.seq - 1

    def summed(unit, p, level):
        start = pl.multiple_of(p * plan.rows, plan.rows)
        value = products[unit % plan.slots, pl.ds(start, plan.rows), :]
        for done in range(level):
            value = value + pairs[2 * done + 1][unit, p // (2 << done)].astype(jnp.float32)
        return value

    def level_copy(unit, level):
        step = 1 << level
        peer = d + (1 - 2 * ((d // step) % 2)) * step
        return remote(
            pairs[2 * level].at[unit],
            pairs[2 * level + 1].at[unit],
            sems[2 * level].at[unit],
            sems[2 * level + 1].at[unit],
            {"dp": peer},
        )

    def ahead_copy(unit):
        at = 2 * levels
        return remote(
            ahead_out.at[unit], ahead_in.at[unit], sems[at].at[unit], sems[at + 1].at[unit],
            {"seq": s + 1},
        )

    def back_copy(unit):
        at = 2 * levels + 2
        return remote(
            back_out.at[unit], back_in.at[unit], sems[at].at[unit], sems[at + 1].at[unit],
            {"seq": s - 1},
        )

    def within(unit):
        return jnp.logical_and(unit >= 0, unit < units)

    def step_at(t, carry):
        if produce is not None:
            produce(t)
        for level in range(levels):
            unit = t - gap * level

            @pl.when(within(unit))
            def _(unit=unit, level=level):
                if level == 0:
                    products[unit % plan.slots] = jnp.dot(
                        cot_t[unit % plan.pieces],
                        att[unit // plan.pieces],
                        preferred_element_type=jnp.float32,
                    )
                else:
                    level_copy(unit, level - 1).wait_recv()
                step = 1 << level
                base = d % step + (1 - (d // step) % 2) * step
                for i in range(plan.dp >> (level + 1)):
                    pairs[2 * level][unit, i] = summed(unit, base + i * 2 * step, level).astype(
                        jnp.bfloat16
                    )
                level_copy(unit, level).start()

        unit = t - gap * levels

        @pl.when(within(unit))
        def _():
            if levels > 0:
                level_copy(unit, levels - 1).wait_recv()
            else:
                products[unit % plan.slots] = jnp.dot(
                    cot_t[unit % plan.pieces],
                    att[unit // plan.pieces],
                    preferred_element_type=jnp.float32,
                )
            own[unit] = summed(unit, d, levels)

        if last > 0:
            fore = t - gap * (levels + s)

            @pl.when(jnp.logical_and(within(fore), s == 0))
            def _():
                ahead_out[fore] = own[fore].astype(jnp.bfloat16)
                ahead_copy(fore).start()

            @pl.when(jnp.logical_and(within(fore), s > 0))
            def _():
                ahead_copy(fore).wait_recv()

                @pl.when(s < last)
                def _():
                    ahead_out[fore] = (own[fore] + ahead_in[fore].astype(jnp.float32)).astype(
                        jnp.bfloat16
                    )
                    ahead_copy(fore).start()

            rear = t - gap * (levels + last - s)

            @pl.when(jnp.logical_and(within(rear), s == last))
            def _():
                back_out[rear] = own[rear].astype(jnp.bfloat16)
                back_copy(rear).start()

            @pl.when(jnp.logical_and(within(rear), s < last))
            def _():
                back_copy(rear).wait_recv()

                @pl.when(s > 0)
                def _():
                    back_out[rear] = (own[rear] + back_in[rear].astype(jnp.float32)).astype(
                        jnp.bfloat16
                    )
                    back_copy(rear).start()

        ready = t - gap * (levels + last)

        def store(value):
            row = pl.multiple_of((ready % plan.pieces) * plan.rows, plan.rows)
            column = pl.multiple_of((ready // plan.pieces) * plan.chunk, plan.chunk)
            out_ref[pl.ds(row, plan.rows), pl.ds(column, plan.chunk)] = value.astype(out_ref.dtype)

        if last == 0:

            @pl.when(within(ready))
            def _():
                store(own[ready])

        else:

            @pl.when(jnp.logical_and(within(ready), s == 0))
            def _():
                store(own[ready] + back_in[ready].astype(jnp.float32))

            @pl.when(jnp.logical_and(within(ready), s == last))
            def _():
                store(own[ready] + ahead_in[ready].astype(jnp.float32))

            if last > 1:

                @pl.when(
                    jnp.logical_and(within(ready), jnp.logical_and(s > 0, s < last))
                )
                def _():
                    store(
                        own[ready]
                        + ahead_in[ready].astype(jnp.float32)
                        + back_in[ready].astype(jnp.float32)
                    )

        return carry

    lax.fori_loop(0, max(least, units + gap * (levels + last)), step_at, 0)

    def drain(unit, carry):
        for level in range(levels):
            level_copy(unit, level).wait_send()
        if last > 0:

            @pl.when(s < last)
            def _():
                ahead_copy(unit).wait_send()

            @pl.when(s > 0)
            def _():
                back_copy(unit).wait_send()

        return carry

    lax.fori_loop(0, units, drain, 0)


def greet(plan):
    barrier = pltpu.get_barrier_semaphore()
    d = lax.axis_index("dp")
    s = lax.axis_index("seq")
    for level in range(plan.levels):
        step = 1 << level
        signal_to(barrier, {"dp": d + (1 - 2 * ((d // step) % 2)) * step})
    if plan.seq > 1:

        @pl.when(s > 0)
        def _():
            signal_to(barrier, {"seq": s - 1})

        @pl.when(s < plan.seq - 1)
        def _():
            signal_to(barrier, {"seq": s + 1})

    if plan.seq == 1:
        pl.semaphore_wait(barrier, plan.levels)
        return
    edge = jnp.logical_or(s == 0, s == plan.seq - 1)

    @pl.when(edge)
    def _():
        pl.semaphore_wait(barrier, plan.levels + 1)

    @pl.when(jnp.logical_not(edge))
    def _():
        pl.semaphore_wait(barrier, plan.levels + 2)


def gradient_kernel(plan, cot_ref, att_ref, out_ref, *refs):
    greet(plan)
    turn_over(plan, cot_ref, refs[0])
    for c in range(plan.chunks):
        refs[1][c] = att_ref[:, c * plan.chunk : (c + 1) * plan.chunk]
    gradient_loop(plan, refs, out_ref)


def reduced_gradient(upstream, attended):
    plan = Plan(
        upstream.shape[0], upstream.shape[1], attended.shape[1],
        lax.axis_size("dp"), lax.axis_size("seq"),
    )
    whole = pl.BlockSpec(memory_space=pltpu.VMEM)
    return pl.pallas_call(
        functools.partial(gradient_kernel, plan),
        out_shape=jax.ShapeDtypeStruct((plan.block, plan.columns), jnp.float32),
        in_specs=[whole, whole],
        out_specs=whole,
        scratch_shapes=plan.scratch(),
        compiler_params=pltpu.CompilerParams(
            collective_id=0, has_side_effects=True, vmem_limit_bytes=56 * 2**20
        ),
        name="reduced_gradient",
    )(upstream, attended)


EDGE = 16
TILE = 512
LANES = 128
DP = 4
SEQ = 4
HOLD = 256
SPLIT = 3
GAP = 5
TURNS = 20


def section_kernel(*refs):
    (x_hbm, conv_hbm, bias_in, gain_in, query_hbm, key_hbm, value_hbm, out_hbm, cot_hbm, turn_hbm) = refs[:10]
    mixed, grad_out = refs[10:12]
    (
        x_rows, conv_w, query_w, key_w, value_w, out_w, turn, fetched,
        edges, edge_sems, spread, stacked, pooled, normed, queries,
        kv, kv_send, kv_recv, values, peaks, sums, bias, gain,
        cot_in, cot_t, cot_sems, att_rows, att, att_sems, own,
        ahead_out, ahead_in, back_out, back_in, line_sems, cross,
    ) = refs[12:]
    rows, channels = x_rows.shape
    tokens, width = pooled.shape
    tiles, blocks = width // TILE, channels // LANES
    half, quarter = tokens // 2, tokens // 4
    heads = queries.shape[0]
    part_rows = width // DP
    strips = att.shape[0]
    taps = KERNEL_TAPS
    d = lax.axis_index("dp")
    s = lax.axis_index("seq")
    mate = d + 1 - 2 * (d % 2)
    across = d + 2 - 4 * (d // 2)
    opposite = 3 - d
    far = 3 - s
    upper = s // 2
    end = jnp.logical_or(s == 0, s == SEQ - 1)
    inner = jnp.logical_not(end)

    pieces = ((0, quarter, half), (half, 0, quarter), (half + quarter, half + quarter, quarter))

    def conv_fetch(n):
        return pltpu.make_async_copy(
            conv_hbm.at[:, pl.ds(pl.multiple_of(n * TILE, TILE), TILE)],
            conv_w.at[n],
            fetched.at[6 + n],
        )

    def turn_fetch(i):
        to, at, count = pieces[i]
        return pltpu.make_async_copy(
            turn_hbm.at[pl.ds(pl.multiple_of(s * tokens + at, quarter), count)],
            turn.at[pl.ds(to, count)],
            fetched.at[5],
        )

    turn_whole = pltpu.make_async_copy(turn_hbm.at[pl.ds(0, tokens)], turn, fetched.at[5])

    x_fetch = pltpu.make_async_copy(x_hbm, x_rows, fetched.at[0])
    key_fetch = pltpu.make_async_copy(key_hbm, key_w, fetched.at[1])
    value_fetch = pltpu.make_async_copy(value_hbm, value_w, fetched.at[2])
    query_fetch = pltpu.make_async_copy(query_hbm, query_w, fetched.at[3])
    out_fetch = pltpu.make_async_copy(out_hbm, out_w, fetched.at[4])

    def cot_columns(owner):
        start = pl.multiple_of(owner * part_rows, part_rows)
        return cot_hbm.at[:, pl.ds(start, part_rows)]

    cot_local = tuple(
        pltpu.make_async_copy(cot_columns(block), cot_in.at[slot], cot_sems.at[slot])
        for slot, block in ((1, d), (4, across))
    )

    def cot_copy(slot):
        columns = {0: across, 2: mate, 3: opposite, 5: opposite}[slot]
        peer = mate if slot == 5 else columns
        return remote(
            cot_columns(columns), cot_in.at[slot], cot_sems.at[6], cot_sems.at[slot],
            {"dp": peer},
        )

    x_fetch.start()
    for n in range(tiles):
        conv_fetch(n).start()
    key_fetch.start()
    value_fetch.start()
    for i in range(3):
        turn_fetch(i).start()

    barrier = pltpu.get_barrier_semaphore()
    for peer in (mate, across, opposite):
        signal_to(barrier, {"dp": peer})

    @pl.when(s > 0)
    def _():
        signal_to(barrier, {"seq": s - 1})

    @pl.when(s < SEQ - 1)
    def _():
        signal_to(barrier, {"seq": s + 1})

    @pl.when(end)
    def _():
        signal_to(barrier, {"seq": far})

    bias[...] = bias_in[...].reshape(bias.shape)
    gain[...] = gain_in[...].reshape(gain.shape)

    def edge_ahead():
        return remote(
            x_hbm.at[pl.ds(rows - EDGE, EDGE)], edges.at[0], edge_sems.at[0], edge_sems.at[1],
            {"seq": s + 1},
        )

    def edge_back():
        return remote(
            x_hbm.at[pl.ds(0, EDGE)], edges.at[1], edge_sems.at[2], edge_sems.at[3],
            {"seq": s - 1},
        )

    x_fetch.wait()
    query_fetch.start()
    for j in range(blocks):
        spread[j, EDGE : EDGE + rows, :] = x_rows[:, j * LANES : (j + 1) * LANES].astype(
            jnp.float32
        )
    blank = jnp.zeros((EDGE, LANES), jnp.float32)
    for j in range(blocks):
        spread[j, :EDGE, :] = blank
        spread[j, EDGE + rows :, :] = blank

    def stack(tap, to, first, count):
        for parity in range(2):
            for j in range(blocks):
                start = EDGE + parity + DILATION_STEP * (tap - 1) + 2 * first
                lane = tap * channels + j * LANES
                row = 2 * half * (to // half) + parity * half + to % half
                stacked[row : row + count, lane : lane + LANES] = spread[
                    j, pl.ds(start, count, stride=2), :
                ].astype(jnp.bfloat16)

    for tap in range(taps):
        for piece in pieces:
            stack(tap, *piece)

    pl.semaphore_wait(barrier, 5)

    @pl.when(s < SEQ - 1)
    def _():
        edge_ahead().start()

    @pl.when(s > 0)
    def _():
        edge_back().start()

    for slot in (0, 2, 3, 5):
        cot_copy(slot).start()
    for copy in cot_local:
        copy.start()
    out_fetch.start()

    def put_edge(which, start, tap, to, first):
        (edge_ahead if which == 0 else edge_back)().wait_recv()
        for j in range(blocks):
            spread[j, start : start + EDGE, :] = edges[
                which, :, j * LANES : (j + 1) * LANES
            ].astype(jnp.float32)
        stack(tap, to, first, EDGE)

    def turned(vectors, first, count):
        return (
            vectors * turn[pl.ds(first, count), :KEY]
            + pltpu.roll(vectors, KEY // 2, 1) * turn[pl.ds(first, count), KEY:]
        ).astype(jnp.bfloat16)

    def kv_copy(owner, part, piece, sem, where):
        span = pl.ds(0, half) if piece == 0 else pl.ds(half, half + quarter)
        block = kv.at[owner, part, span]
        return remote(
            block, block, kv_send.at[sem], kv_recv.at[(owner * 2 + part) * 2 + piece],
            {"seq": where},
        )

    def kv_own(part):
        for piece in range(2):

            @pl.when(end)
            def _():
                kv_copy(s, part, piece, 0, far).start()

            @pl.when(s > 0)
            def _():
                kv_copy(s, part, piece, 0, s - 1).start()

            @pl.when(s < SEQ - 1)
            def _():
                kv_copy(s, part, piece, 0, s + 1).start()

    def kv_relay(part):
        for piece in range(2):
            kv_copy(s - 1, part, piece, 1, s + 1).wait_recv()
            kv_copy(s - 1, part, piece, 1, s + 1).start()
            kv_copy(s + 1, part, piece, 1, s - 1).wait_recv()
            kv_copy(s + 1, part, piece, 1, s - 1).start()

    def conv_pass(part, carry):
        first = part == 0
        base = pl.multiple_of(part * half, half)
        here = pl.ds(base, half)

        @pl.when(jnp.logical_and(part == 1, s > 0))
        def _():
            put_edge(0, 0, 0, half, 0)

        @pl.when(jnp.logical_and(part == 1, s < SEQ - 1))
        def _():
            put_edge(1, EDGE + rows, taps - 1, tokens - EDGE, tokens - EDGE)

        def conv_tile(n, carry):
            @pl.when(first)
            def _():
                conv_fetch(n).wait()

            columns = pl.ds(pl.multiple_of(n * TILE, TILE), TILE)
            pre = (
                jnp.dot(
                    stacked[pl.ds(pl.multiple_of(part * tokens, tokens), tokens), :],
                    conv_w[n],
                    preferred_element_type=jnp.float32,
                )
                + bias[:, columns]
            )
            root = math.sqrt(2.0 / math.pi)
            inside = pre * (root + (root * 0.044715) * (pre * pre))
            activated = pre * (0.5 + 0.5 * jnp.tanh(inside))
            pooled[here, columns] = jnp.maximum(activated[:half], activated[half:]).astype(
                jnp.bfloat16
            )
            return carry

        lax.fori_loop(0, tiles, conv_tile, 0)

        count = 32

        def norm_part(i, carry):
            few = pl.ds(pl.multiple_of(base + i * count, count), count)
            wide = pooled[few, :].astype(jnp.float32)
            squares = jnp.mean(wide * wide, axis=-1, keepdims=True)
            normed[few, :] = (wide * lax.rsqrt(squares + norm_eps) * gain[...]).astype(
                jnp.bfloat16
            )
            return carry

        lax.fori_loop(0, half // count, norm_part, 0)

        @pl.when(first)
        def _():
            key_fetch.wait()
            value_fetch.wait()
            turn_whole.wait()

        ready = normed[here, :]
        kv[s, part, :half, :] = turned(
            jnp.dot(ready, key_w[...], preferred_element_type=jnp.float32), base, half
        )
        own_values = lax.dot_general(
            ready, value_w[...], (((1,), (1,)), ((), ())), preferred_element_type=jnp.float32
        )
        kv[s, part, half : 2 * half, :] = own_values[:, :LANES].astype(jnp.bfloat16)
        kv[s, part, 2 * half :, :] = jnp.concatenate(
            [own_values[:quarter, LANES:], own_values[quarter:, LANES:]], axis=1
        ).astype(jnp.bfloat16)
        kv_own(part)
        return carry

    lax.fori_loop(0, 2, conv_pass, 0)

    @pl.when(inner)
    def _():
        kv_relay(0)

    query_fetch.wait()

    def query_pair(c, carry):
        pair = jnp.dot(
            normed[...],
            query_w[:, pl.ds(pl.multiple_of(c * 2 * KEY, 2 * KEY), 2 * KEY)],
            preferred_element_type=jnp.float32,
        )
        queries[2 * c] = turned(pair[:, :KEY], 0, tokens)
        queries[2 * c + 1] = turned(pair[:, KEY:], 0, tokens)
        return carry

    lax.fori_loop(0, heads // 2, query_pair, 0)

    def turn_over(slot):
        if slot in (1, 4):
            cot_local[slot // 4].wait()
        else:
            cot_copy(slot).wait_recv()
        middle = cot_in[slot, quarter : quarter + half, :]
        outer = jnp.concatenate(
            [cot_in[slot, :quarter, :], cot_in[slot, quarter + half :, :]], axis=0
        )
        at = slot * tokens
        cot_t[:, at : at + half] = jnp.transpose(middle)
        cot_t[:, at + half : at + tokens] = jnp.transpose(outer)

    def owner_of(k):
        low = s + upper * (3 - 2 * s)
        at = (k + low) % 2 if k < 2 else (k - 2 + 1 - low) % 2 + 2
        return at + upper * (3 - 2 * at)

    side = lax.broadcasted_iota(jnp.int32, (half, LANES), 1)

    def unpack(owner):
        for part in range(2):
            at = part * half
            values[at : at + half, :LANES] = kv[owner, part, half : 2 * half, :]
            rest = kv[owner, part, 2 * half :, :]
            rest = jnp.concatenate(
                [rest, pltpu.roll(rest.astype(jnp.float32), LANES // 2, 1).astype(jnp.bfloat16)],
                axis=0,
            ).astype(jnp.float32)
            rest = jnp.where(
                side < VAL - LANES, rest, jnp.where(side == VAL - LANES, 1.0, 0.0)
            )
            values[at : at + half, LANES:] = rest.astype(jnp.bfloat16)

    factor = KEY ** (-0.5) * math.log2(math.e)

    def twice(column):
        return jnp.concatenate([column, column], axis=1)

    def attend(h, keys, first):
        scores = lax.dot_general(
            queries[h], keys, (((1,), (1,)), ((), ())), preferred_element_type=jnp.float32
        )
        peak = jnp.max(scores, axis=-1, keepdims=True)
        if first:
            peak = jnp.broadcast_to(peak, (tokens, LANES))
        else:
            before = peaks[h]
            peak = jnp.maximum(before, peak)
        weights = jnp.exp2((scores - twice(peak)) * factor).astype(jnp.bfloat16)
        total = jnp.dot(weights, values[...], preferred_element_type=jnp.float32)
        if not first:
            total = total + sums[h] * twice(jnp.exp2((before - peak) * factor))
        return peak, total

    def keys_of(owner):
        return kv[owner, :, :half, :].reshape(tokens, KEY)

    def attend_block(k):
        owner = owner_of(k)
        unpack(owner)

        def pair(c, carry):
            for h in (2 * c, 2 * c + 1):
                peak, total = attend(h, keys_of(owner), k == 0)
                peaks[h] = peak
                sums[h] = total
            return carry

        lax.fori_loop(0, heads // 2, pair, 0)

    def wait_block(k):
        owner = owner_of(k)
        for part in range(2):
            for piece in range(2):
                kv_copy(owner, part, piece, 0, far).wait_recv()

    def att_copy(kind, b):
        slot = (1, 1, 0)[kind]
        to = (2, 0, 3)[kind]
        arrived = strips + b if kind == 1 else b
        return remote(
            att.at[b, slot], att.at[b, to], att_sems.at[2 * strips + kind], att_sems.at[arrived],
            {"dp": across if kind == 1 else mate},
        )

    def mate_strips(b):
        both = att.at[b, pl.ds(2, 2)]
        return remote(both, both, att_sems.at[2 * strips], att_sems.at[b], {"dp": mate})

    attend_block(0)

    @pl.when(inner)
    def _():
        kv_relay(1)

    for slot in range(6):
        turn_over(slot)

    @pl.when(end)
    def _():
        wait_block(1)

    attend_block(1)

    @pl.when(end)
    def _():
        wait_block(2)

    attend_block(2)
    wait_block(3)
    last_owner = owner_of(3)
    unpack(last_owner)
    chunk = 2 * VAL
    each = chunk // LANES

    def last_pair(c):
        done = []
        for h in (2 * c, 2 * c + 1):
            _, total = attend(h, keys_of(last_owner), False)
            done.append(total[:, :VAL] / total[:, VAL : VAL + 1])
        both = jnp.concatenate(done, axis=1).astype(jnp.bfloat16)
        for i in range(each):
            b = c * each + i
            att[b, 1] = both[:, i * LANES : (i + 1) * LANES]
            att_copy(0, b).start()

            @pl.when(b > 0)
            def _(b=b):
                att_copy(1, b).start()

        att_rows[:, pl.ds(pl.multiple_of(c * chunk, LANES), chunk)] = both

    def mixed_tile(n):
        columns = pl.ds(pl.multiple_of(n * TILE, TILE), TILE)
        total = pooled[:, columns].astype(jnp.float32) + jnp.dot(
            att_rows[...], out_w[:, columns], preferred_element_type=jnp.float32
        )
        total = total.astype(jnp.bfloat16)
        for at, to, count in pieces:
            mixed[to : to + count, columns] = total[at : at + count]

    out_fetch.wait()

    count = strips + 1
    size = part_rows // SPLIT
    units = count * SPLIT
    last = SEQ - 1

    def place(unit):
        return unit // SPLIT, unit % SPLIT

    def ahead_copy(unit):
        at = place(unit)
        return remote(
            ahead_out.at[at], ahead_in.at[at], line_sems.at[2 * TURNS], line_sems.at[unit % TURNS],
            {"seq": s + 1},
        )

    def back_copy(unit):
        at = place(unit)
        return remote(
            back_out.at[at], back_in.at[at], line_sems.at[2 * TURNS + 1],
            line_sems.at[TURNS + unit % TURNS], {"seq": s - 1},
        )

    def within(unit):
        return jnp.logical_and(unit >= 0, unit < units)

    def cross_copy():
        return remote(
            cross.at[0], cross.at[1], line_sems.at[2 * TURNS + 2], line_sems.at[2 * TURNS + 3],
            {"dp": across},
        )

    def step_at(step, carry):
        t = step - 1

        @pl.when(t == 0)
        def _():
            att_copy(0, 0).wait_recv()
            near = att[0, 1:3].reshape(2 * tokens, LANES)
            for i, at in enumerate((1, 4)):
                own[i] = jnp.dot(
                    cot_t[:, at * tokens : (at + 2) * tokens],
                    near,
                    preferred_element_type=jnp.float32,
                ).reshape(own.shape[1:])

        @pl.when(jnp.logical_and(jnp.logical_and(t >= 2 * SPLIT, t < units), t % SPLIT == 0))
        def _():
            q = t // SPLIT
            mate_strips(q - 1).wait_recv()
            own[q] = jnp.dot(
                cot_t[:, : DP * tokens],
                att[q - 1].reshape(DP * tokens, LANES),
                preferred_element_type=jnp.float32,
            ).reshape(own.shape[1:])

        fore = t - GAP * s

        @pl.when(jnp.logical_and(within(fore), s == 0))
        def _():
            ahead_out[place(fore)] = own[place(fore)].astype(jnp.bfloat16)
            ahead_copy(fore).start()

        @pl.when(jnp.logical_and(within(fore), s > 0))
        def _():
            ahead_copy(fore).wait_recv()

            @pl.when(s < last)
            def _():
                ahead_out[place(fore)] = (
                    own[place(fore)] + ahead_in[place(fore)].astype(jnp.float32)
                ).astype(jnp.bfloat16)
                ahead_copy(fore).start()

        rear = t - GAP * (last - s)

        @pl.when(jnp.logical_and(within(rear), s == last))
        def _():
            back_out[place(rear)] = own[place(rear)].astype(jnp.bfloat16)
            back_copy(rear).start()

        @pl.when(jnp.logical_and(within(rear), s < last))
        def _():
            back_copy(rear).wait_recv()

            @pl.when(s > 0)
            def _():
                back_out[place(rear)] = (
                    own[place(rear)] + back_in[place(rear)].astype(jnp.float32)
                ).astype(jnp.bfloat16)
                back_copy(rear).start()

        ready = t - GAP * last

        def store(value):
            q, i = place(ready)
            row = pl.multiple_of(i * size, size)

            @pl.when(q == 1)
            def _():
                cross[0, pl.ds(row, size), :] = value.astype(cross.dtype)

            @pl.when(q == 0)
            def _():
                grad_out[pl.ds(row, size), :LANES] = value

            @pl.when(q > 1)
            def _():
                column = pl.multiple_of((q - 1) * LANES, LANES)
                grad_out[pl.ds(row, size), pl.ds(column, LANES)] = value

        @pl.when(jnp.logical_and(within(ready), s == 0))
        def _():
            store(own[place(ready)] + back_in[place(ready)].astype(jnp.float32))

        @pl.when(jnp.logical_and(within(ready), s == last))
        def _():
            store(own[place(ready)] + ahead_in[place(ready)].astype(jnp.float32))

        @pl.when(jnp.logical_and(within(ready), inner))
        def _():
            store(
                own[place(ready)]
                + ahead_in[place(ready)].astype(jnp.float32)
                + back_in[place(ready)].astype(jnp.float32)
            )

        @pl.when(ready == 2 * SPLIT - 1)
        def _():
            cross_copy().start()

        @pl.when(jnp.logical_and(step < heads, step % 2 == 0))
        def _():
            last_pair(step // 2)

        @pl.when(
            jnp.logical_and(
                jnp.logical_and(t >= SPLIT, t < strips * SPLIT), t % SPLIT == 0
            )
        )
        def _():
            b = t // SPLIT
            att_copy(1, b).wait_recv()
            att_copy(2, b).start()

        tile = t - 4 * SPLIT

        @pl.when(
            jnp.logical_and(jnp.logical_and(tile >= 0, tile < 2 * tiles), tile % 2 == 0)
        )
        def _():
            mixed_tile(tile // 2)

        return carry

    lax.fori_loop(0, units + GAP * last + 1, step_at, 0)
    cross_copy().wait_recv()
    grad_out[:, :LANES] = grad_out[:, :LANES] + cross[1].astype(jnp.float32)
    cross_copy().wait_send()

    @pl.when(s < last)
    def _():
        remote(
            ahead_out, ahead_in, line_sems.at[2 * TURNS], line_sems.at[0], {"seq": s + 1}
        ).wait_send()

    @pl.when(s > 0)
    def _():
        remote(
            back_out, back_in, line_sems.at[2 * TURNS + 1], line_sems.at[0], {"seq": s - 1}
        ).wait_send()

    for kind in range(3):
        sent = att.at[:, 0] if kind == 0 else att.at[pl.ds(1, strips - 1), 0]
        remote(
            sent, sent, att_sems.at[2 * strips + kind], att_sems.at[0], {"dp": mate}
        ).wait_send()
    pair_of = kv.at[pl.ds(0, 2)]
    remote(pair_of, pair_of, kv_send.at[0], kv_recv.at[0], {"seq": far}).wait_send()

    @pl.when(inner)
    def _():
        remote(pair_of, pair_of, kv_send.at[1], kv_recv.at[0], {"seq": far}).wait_send()

    others = cot_in.at[pl.ds(0, 4)]
    remote(others, others, cot_sems.at[6], cot_sems.at[0], {"dp": mate}).wait_send()

    @pl.when(s < SEQ - 1)
    def _():
        edge_ahead().wait_send()

    @pl.when(s > 0)
    def _():
        edge_back().wait_send()


def turn_table(count):
    frequency = np.exp(
        np.float32(-math.log(rope_base) * 2.0) * np.arange(KEY // 2, dtype=np.float32) / KEY
    ).astype(np.float32)
    angles = np.arange(count, dtype=np.float32)[:, None] * frequency[None, :]
    cosine, sines = np.cos(angles), np.sin(angles)
    return np.concatenate([cosine, cosine, -sines, sines], axis=1).astype(np.float32)


def finish_kernel(mixed_in, grad_in, mixed, grad, sems):
    copies = (
        pltpu.make_async_copy(grad_in, grad, sems.at[0]),
        pltpu.make_async_copy(mixed_in, mixed, sems.at[1]),
    )
    for copy in copies:
        copy.start()
    for copy in copies:
        copy.wait()


def finish(mixed, gradient):
    away = pl.BlockSpec(memory_space=pl.ANY)
    return pl.pallas_call(
        finish_kernel,
        out_shape=(
            jax.ShapeDtypeStruct(mixed.shape, mixed.dtype),
            jax.ShapeDtypeStruct(gradient.shape, gradient.dtype),
        ),
        in_specs=[pl.BlockSpec(memory_space=pltpu.VMEM)] * 2,
        out_specs=(away, away),
        scratch_shapes=[pltpu.SemaphoreType.DMA((2,))],
        name="finish",
    )(
        pltpu.with_memory_space_constraint(mixed, pltpu.VMEM),
        pltpu.with_memory_space_constraint(gradient, pltpu.VMEM),
    )


def section(x_in, kernel_weight, conv_bias, norm_gain, w_query, w_key, w_value, w_out, cotangent):
    inputs, upstream = x_in[0], cotangent[0]
    rows, channels = inputs.shape
    width, columns = kernel_weight.shape[2], w_out.shape[0]
    tokens, tiles, strips = rows // 2, width // TILE, columns // LANES
    heads, part_rows = w_query.shape[1] // KEY, width // DP
    depth = KERNEL_TAPS * channels
    bf, f32 = jnp.bfloat16, jnp.float32
    line = pltpu.VMEM((strips + 1, SPLIT, part_rows // SPLIT, LANES), bf)
    held = pl.BlockSpec(memory_space=pltpu.VMEM)
    away = pl.BlockSpec(memory_space=pl.ANY)
    mixed, gradient = pl.pallas_call(
        section_kernel,
        out_shape=(
            pltpu.VMEM((tokens, width), bf),
            pltpu.VMEM((part_rows, columns), f32),
        ),
        in_specs=[away, away, held, held, away, away, away, away, away, away],
        out_specs=(held, held),
        scratch_shapes=[
            pltpu.VMEM((rows, channels), bf),
            pltpu.VMEM((tiles, depth, TILE), bf),
            pltpu.VMEM(w_query.shape, bf),
            pltpu.VMEM(w_key.shape, bf),
            pltpu.VMEM(w_value.shape[::-1], bf),
            pltpu.VMEM(w_out.shape, bf),
            pltpu.VMEM((tokens, 2 * KEY), f32),
            pltpu.SemaphoreType.DMA((6 + tiles,)),
            pltpu.VMEM((2, EDGE, channels), bf),
            pltpu.SemaphoreType.DMA((4,)),
            pltpu.VMEM((channels // LANES, rows + 2 * EDGE, LANES), f32),
            pltpu.VMEM((rows, depth), bf),
            pltpu.VMEM((tokens, width), bf),
            pltpu.VMEM((tokens, width), bf),
            pltpu.VMEM((heads, tokens, KEY), bf),
            pltpu.VMEM((SEQ, 2, 5 * tokens // 4, KEY), bf),
            pltpu.SemaphoreType.DMA((2,)),
            pltpu.SemaphoreType.DMA((4 * SEQ,)),
            pltpu.VMEM((tokens, HOLD), bf),
            pltpu.VMEM((heads, tokens, LANES), f32),
            pltpu.VMEM((heads, tokens, HOLD), f32),
            pltpu.VMEM((1, width), f32),
            pltpu.VMEM((1, width), f32),
            pltpu.VMEM((6, tokens, part_rows), bf),
            pltpu.VMEM((part_rows, 6 * tokens), bf),
            pltpu.SemaphoreType.DMA((7,)),
            pltpu.VMEM((tokens, columns), bf),
            pltpu.VMEM((strips, DP, tokens, LANES), bf),
            pltpu.SemaphoreType.DMA((2 * strips + 3,)),
            pltpu.VMEM((strips + 1, SPLIT, part_rows // SPLIT, LANES), f32),
            line, line, line, line,
            pltpu.SemaphoreType.DMA((2 * TURNS + 4,)),
            pltpu.VMEM((2, part_rows, LANES), bf),
        ],
        compiler_params=pltpu.CompilerParams(
            collective_id=1, has_side_effects=True, vmem_limit_bytes=54 * 2**20
        ),
        name="section",
    )(
        inputs,
        kernel_weight.reshape(depth, width),
        conv_bias,
        norm_gain,
        w_query,
        w_key,
        jnp.transpose(w_value),
        w_out,
        upstream,
        turn_table(tokens * SEQ),
    )
    mixed, gradient = finish(mixed, gradient)
    return mixed[None], gradient


def local(x_in, kernel_weight, conv_bias, norm_gain, w_query, w_key, w_value, w_out, cotangent):
    inputs = x_in[0]
    edge_padding = DILATION_STEP * (KERNEL_TAPS - 1) // 2
    padded_rows = padded(inputs, (("seq", 0),), edge_padding)
    padded_row_count = inputs.shape[0]
    before_activation = jnp.broadcast_to(
        conv_bias[None, :], (padded_row_count, kernel_weight.shape[2])
    )
    for kernel_tap_index in range(KERNEL_TAPS):
        before_activation = before_activation + jnp.dot(
            padded_rows[
                kernel_tap_index * DILATION_STEP : kernel_tap_index * DILATION_STEP
                + padded_row_count
            ],
            kernel_weight[kernel_tap_index],
            preferred_element_type=jnp.float32,
        )
    activated = jax.nn.gelu(before_activation)
    pooled = jnp.max(activated.reshape(padded_row_count // 2, 2, -1), axis=1).astype(jnp.bfloat16)
    token_count = pooled.shape[0]
    features = lax.all_gather(pooled, "head", axis=1, tiled=True)
    widened = features.astype(jnp.float32)
    squares = jnp.mean(widened * widened, axis=-1, keepdims=True)
    normed = (widened * lax.rsqrt(squares + norm_eps) * norm_gain).astype(jnp.bfloat16)
    seq_offset = lax.axis_index("seq") * token_count
    positions = seq_offset + jnp.arange(token_count, dtype=jnp.int32)
    local_heads = w_query.shape[1] // KEY
    queries = rotate(
        jnp.dot(normed, w_query, preferred_element_type=jnp.float32).reshape(
            token_count, local_heads, KEY
        ),
        positions,
    ).astype(jnp.bfloat16)
    own_rows = token_count // lax.axis_size("head")
    row_offset = lax.axis_index("head") * own_rows
    own_normed = lax.dynamic_slice_in_dim(normed, row_offset, own_rows, 0)
    own_positions = seq_offset + row_offset + jnp.arange(own_rows, dtype=jnp.int32)
    key_rows = rotate(
        jnp.dot(own_normed, w_key, preferred_element_type=jnp.float32), own_positions
    ).astype(jnp.bfloat16)
    value_rows = jnp.dot(own_normed, w_value, preferred_element_type=jnp.float32).astype(
        jnp.bfloat16
    )
    start_state = (
        jnp.full((local_heads, token_count), -1e30, jnp.float32),
        jnp.zeros((local_heads, token_count), jnp.float32),
        jnp.zeros((token_count, local_heads, VAL), jnp.float32),
    )
    both = lax.all_gather(
        jnp.concatenate([key_rows, value_rows], axis=1), ("seq", "head"), axis=0, tiled=True
    )
    final_state = attend_pieces(
        queries,
        both[:, :KEY],
        both[:, KEY:],
        start_state,
    )
    running_max, running_sum, weighted = final_state
    attended = (
        (weighted / jnp.transpose(running_sum)[:, :, None])
        .astype(jnp.bfloat16)
        .reshape(token_count, local_heads * VAL)
    )
    projected = lax.psum_scatter(
        lax.dot_general(
            w_out, attended, (((0,), (1,)), ((), ())), preferred_element_type=jnp.float32
        ).astype(jnp.bfloat16),
        "head",
        scatter_dimension=0,
        tiled=True,
    ).astype(jnp.float32)
    mixed = (pooled.astype(jnp.float32) + jnp.transpose(projected)).astype(jnp.bfloat16)[None]
    upstream = cotangent[0]
    gradient = reduced_gradient(upstream, attended)
    return (mixed, gradient)


def solution(mesh):
    sizes = tuple(mesh.shape[axis] for axis in ("head", "seq", "dp"))
    return jax.shard_map(
        section if sizes == (1, SEQ, DP) else local,
        mesh=mesh,
        in_specs=(
            P(("groups", "dp"), "seq", None),
            P(None, None, "head"),
            P("head"),
            P(),
            P(None, "head"),
            P(),
            P(),
            P("head", None),
            P(("groups", "dp"), "seq", None),
        ),
        out_specs=(P(("groups", "dp"), "seq", "head"), P(("groups", "dp"), "head")),
        check_vma=False,
    )
```
